32 devices in a mesh: dp: 8 (over z, x), tensor: 4 (over y, core).
Axes of the slice: x: 2, y: 2, z: 4, core: 2. Of those that a mesh axis runs over, the one named last changes fastest.
Arguments:
- tokens: bfloat16 [16384, 768], P(('dp', 'tensor')), may hold values from -6 to 6
- cotangent: bfloat16 [16384, 768], P(('dp', 'tensor')), may hold values from -6 to 6
- lengths: int32 [16], P('dp'), may hold values from 128 to 1024, as said below
- tie_sets: int32 [16], P('dp'), may hold values from 0 to 1
- qkv_weight: bfloat16 [768, 3, 768], P(None, None, 'tensor'), may hold values from -0.21875 to 0.21875
- qkv_bias: bfloat16 [2, 768], P(None, 'tensor'), may hold values from -1.5 to 1.5
- out_weight: bfloat16 [768, 768], P('tensor'), may hold values from -1.75 to 1.75
- out_bias: bfloat16 [768], replicated, may hold values from -1.5 to 1.5
- fc_weight: bfloat16 [768, 3072], P(None, 'tensor'), may hold values from -0.21875 to 0.21875
- fc_bias: bfloat16 [3072], P('tensor'), may hold values from -1.5 to 1.5
- proj_weight: bfloat16 [3072, 768], P('tensor'), may hold values from -0.15625 to 0.15625
- proj_bias: bfloat16 [768], replicated, may hold values from -1.5 to 1.5
- norm_gain: float32 [2, 2, 768], replicated, may hold values from 0.25 to 1.75
- norm_bias: float32 [2, 2, 768], replicated, may hold values from -1.5 to 1.5
Outputs:
- block_out: bfloat16 [16384, 768], P(('dp', 'tensor'))
- grad_input: bfloat16 [16384, 768], P(('dp', 'tensor'))
- grad_qkv_weight: float32 [768, 3, 768], P(None, None, 'tensor')
- grad_qkv_bias: float32 [2, 768], P(None, 'tensor')
- grad_out_weight: float32 [768, 768], P('tensor')
- grad_out_bias: float32 [768], replicated
- grad_fc_weight: float32 [768, 3072], P(None, 'tensor')
- grad_fc_bias: float32 [3072], P('tensor')
- grad_proj_weight: float32 [3072, 768], P('tensor')
- grad_proj_bias: float32 [768], replicated
- grad_norm_gain: float32 [2, 2, 768], replicated
- grad_norm_bias: float32 [2, 2, 768], replicated
The draws below stay inside these ranges and needn't reach their ends.
Inputs may be any that keep to these rules, and one draw needn't show every extreme that they name: `lengths`: some sequence in every draw has exactly 1024 true tokens; the others have between 128 and 1024.
All inputs are finite; a program needn't handle non-finite values.
Results may differ from the reference program's by a relative error of at most 0.013.
The reference program's roundings to bfloat16 on the way count: a program that leaves them out, or rounds other values in their place, can miss the bound.
Values may be sent and summed in bfloat16 or wider, within the bound.
A program may use at most 192 MiB of HBM per device.

```python
import jax
import jax.numpy as jnp
from jax import lax

D = 768
HEADS = 12
HD = 64
FF = 3072
LEN = 1024
NSETS = 2
SEQS = 16
TOKENS = 16384


def draw_lengths(key, part):
    first_key = jax.random.fold_in(key, 11)
    second_key = jax.random.fold_in(key, 12)
    values = jax.random.randint(first_key, (SEQS,), LEN // 8, LEN + 1)
    where = jax.random.randint(second_key, (), 0, SEQS)
    return values.at[where].set(LEN).astype(jnp.int32)


def plant(array, stream_key, smallest, largest):
    dims = array.shape
    spot = [jax.random.randint(jax.random.fold_in(stream_key, axis), (), 0, dims[axis]) for axis in range(len(dims))]
    array = array.at[tuple(spot)].set(smallest)
    longest = dims.index(max(dims))
    spot[longest] = (spot[longest] + 1) % dims[longest]
    return array.at[tuple(spot)].set(largest)


def levels(key, shape, cuts, least, high):
    level = 1.0
    for position, shards_of in cuts:
        draws = jax.random.uniform(jax.random.fold_in(jax.random.fold_in(key, 6), position), (shards_of,), jnp.float32, least / len(cuts), high / len(cuts))
        level = level * jnp.repeat(jnp.exp(draws), shape[position] // shards_of).reshape((-1,) + (1,) * (len(shape) - 1 - position))
    return level


def gaussian(rng, extent, width, most, pieces=(), held_as=jnp.bfloat16):
    factor_of = levels(rng, extent, pieces, -0.22, 0.18) if pieces else 1.0
    values = jax.random.normal(rng, extent, jnp.float32) * width * factor_of
    return jnp.minimum(jnp.maximum(values, -most), most).astype(held_as)


def setup_inputs(seed: int = 0) -> dict:
    arg_keys = jax.random.split(jax.random.key(seed), 15)
    tokens = gaussian(arg_keys[0], (TOKENS, D), 1.0, 6.0, ((0, 32),))
    cotangent = gaussian(arg_keys[1], (TOKENS, D), 1.0, 6.0, ((0, 32),))
    lengths = draw_lengths(jax.random.fold_in(arg_keys[14], 71), 0)
    tie_sets = plant(jax.random.randint(arg_keys[3], (SEQS,), 0, NSETS), jax.random.fold_in(arg_keys[3], 1), 0, NSETS - 1).astype(jnp.int32)
    qkv_weight = gaussian(arg_keys[4], (D, 3, D), D ** -0.5, 0.21875, ((2, 4),))
    qkv_bias = gaussian(arg_keys[5], (2, D), 0.3, 1.5, ((1, 4),))
    out_weight = gaussian(arg_keys[6], (D, D), (D // 64) ** -0.5, 1.75, ((0, 4),))
    out_bias = gaussian(arg_keys[7], (D,), 0.3, 1.5)
    fc_weight = gaussian(arg_keys[8], (D, FF), D ** -0.5, 0.21875, ((1, 4),))
    fc_bias = gaussian(arg_keys[9], (FF,), 0.3, 1.5, ((0, 4),))
    proj_weight = gaussian(arg_keys[10], (FF, D), (FF // 2) ** -0.5, 0.15625, ((0, 4),))
    proj_bias = gaussian(arg_keys[11], (D,), 0.3, 1.5)
    norm_gain = jnp.clip(1.0 + 0.15 * jax.random.normal(arg_keys[12], (2, NSETS, D), jnp.float32), 0.25, 1.75)
    norm_bias = gaussian(arg_keys[13], (2, NSETS, D), 0.3, 1.5, (), jnp.float32)
    return {"tokens": tokens, "cotangent": cotangent, "lengths": lengths, "tie_sets": tie_sets, "qkv_weight": qkv_weight, "qkv_bias": qkv_bias, "out_weight": out_weight, "out_bias": out_bias, "fc_weight": fc_weight, "fc_bias": fc_bias, "proj_weight": proj_weight, "proj_bias": proj_bias, "norm_gain": norm_gain, "norm_bias": norm_bias}


@jax.custom_vjp
def low(v):
    return lax.optimization_barrier(v.astype(jnp.bfloat16)).astype(jnp.float32)

@jax.custom_vjp
def low_back(v):
    return v

def low_keep(v):
    return (low(v), None)

def low_pass(kept, grad):
    return (grad,)

def back_keep(v):
    return (v, None)

def back_low(kept, grad):
    return (low(grad),)
low.defvjp(low_keep, low_pass)
low_back.defvjp(back_keep, back_low)
HIGHEST = lax.Precision.HIGHEST

def gelu(v):
    return 0.5 * v * (1.0 + jnp.tanh(0.7978845608028654 * (v + 0.044715 * v * v * v)))

def norm_rows(v, gain, bias):
    mean = lax.optimization_barrier(jnp.mean(v, axis=-1, keepdims=True))
    centered = v - mean
    var = lax.optimization_barrier(jnp.mean(centered * centered, axis=-1, keepdims=True))
    return centered * lax.rsqrt(var + 1e-05) * gain + bias

def forward(x, params, length, chosen):
    qkv_w, qkv_b, out_w, out_b, fc_w, fc_b, proj_w, proj_b, gains, biases = params
    first = low(norm_rows(x, gains[0, chosen], biases[0, chosen]))
    qkv = jnp.einsum('td,dcf->tcf', first, qkv_w, precision=HIGHEST)
    query = low(low_back(qkv[:, 0] + qkv_b[0]))
    key = low(low_back(qkv[:, 1]))
    value = low(low_back(qkv[:, 2] + qkv_b[1]))
    query_h = query.reshape(LEN, HEADS, HD)
    key_h = key.reshape(LEN, HEADS, HD)
    value_h = value.reshape(LEN, HEADS, HD)
    scores = jnp.einsum('qhe,khe->hqk', query_h, key_h, precision=HIGHEST) * (1.0 / math_sqrt(HD))
    qpos = lax.broadcasted_iota(jnp.int32, (LEN, LEN), 0)
    kpos = lax.broadcasted_iota(jnp.int32, (LEN, LEN), 1)
    mask = (kpos <= qpos) & (kpos < length)
    scores = low_back(jnp.where(mask[None], scores, -1e+30))
    probs = low(jax.nn.softmax(scores, axis=-1))
    attended = jnp.einsum('hqk,khe->qhe', probs, value_h, precision=HIGHEST).reshape(LEN, D)
    attended = low(low_back(attended))
    middle = x + low_back(jnp.dot(attended, out_w, precision=HIGHEST)) + out_b
    second = low(norm_rows(middle, gains[1, chosen], biases[1, chosen]))
    pre = low_back(jnp.dot(second, fc_w, precision=HIGHEST) + fc_b)
    act = low(gelu(pre))
    return middle + low_back(jnp.dot(act, proj_w, precision=HIGHEST)) + proj_b

def math_sqrt(value):
    return float(value) ** 0.5

def reference(tokens, cotangent, lengths, tie_sets, qkv_weight, qkv_bias, out_weight, out_bias, fc_weight, fc_bias, proj_weight, proj_bias, norm_gain, norm_bias):
    params = tuple((p.astype(jnp.float32) for p in (qkv_weight, qkv_bias, out_weight, out_bias, fc_weight, fc_bias, proj_weight, proj_bias, norm_gain, norm_bias)))
    inputs = tokens.astype(jnp.float32).reshape(SEQS, LEN, D)
    grads_in = cotangent.astype(jnp.float32).reshape(SEQS, LEN, D)

    def step(total, item):
        x, ct, length, chosen = item
        out, pull = jax.vjp(lambda xx, pp: forward(xx, pp, length, chosen), x, params)
        dx, dparams = pull(ct)
        total = jax.tree.map(lambda a, b: a + b, total, dparams)
        return (total, (out.astype(jnp.bfloat16), dx.astype(jnp.bfloat16)))
    zeros = jax.tree.map(jnp.zeros_like, params)
    total, (outs, dxs) = lax.scan(step, zeros, (inputs, grads_in, lengths, tie_sets))
    return (outs.reshape(TOKENS, D), dxs.reshape(TOKENS, D), total[0], total[1], total[2], total[3], total[4], total[5], total[6], total[7], total[8], total[9])
```

```python
import jax
import jax.numpy as jnp
from jax import lax
from jax.experimental import pallas as pl
from jax.experimental.pallas import tpu as pltpu
from jax.sharding import PartitionSpec as P

HD = 64
EPS = 1e-05
F32 = jnp.float32
BF16 = jnp.bfloat16
GELU_K = 0.7978845608028654
GELU_C = 0.044715
VMEM = pl.BlockSpec(memory_space=pltpu.VMEM)
SMEM = pl.BlockSpec(memory_space=pltpu.SMEM)
NT = (((1,), (1,)), ((), ()))
TN = (((0,), (0,)), ((), ()))


def dg(a, b, dims):
    return lax.dot_general(a, b, dims, preferred_element_type=F32)


def mm(a, b):
    return jnp.dot(a, b, preferred_element_type=F32)


def call(kernel, outs, n_in, smem=0, scratch=(), limit=48, flops=0, nbytes=0):
    return pl.pallas_call(
        kernel,
        out_shape=[jax.ShapeDtypeStruct(s, d) for s, d in outs],
        in_specs=[SMEM] * smem + [VMEM] * (n_in - smem),
        out_specs=[VMEM] * len(outs),
        scratch_shapes=list(scratch),
        cost_estimate=pl.CostEstimate(flops=flops, bytes_accessed=nbytes, transcendentals=0),
        compiler_params=pltpu.CompilerParams(vmem_limit_bytes=limit << 20),
    )


def stats(v):
    mean = jnp.mean(v, axis=-1, keepdims=True)
    cent = v - mean
    var = jnp.mean(cent * cent, axis=-1, keepdims=True)
    r = lax.rsqrt(var + EPS)
    return cent * r, r


def norm_first(meta, x, gain, bias, out):
    k = meta[2]
    xhat, _ = stats(x[...].astype(F32))
    out[...] = (xhat * gain[pl.ds(k, 1), :] + bias[pl.ds(k, 1), :]).astype(BF16)


def norm_second(meta, x, br, br_in, ob, gain, bias, middle, out):
    k = meta[2]
    mid = x[...].astype(F32) + (br[...] + br_in[...].astype(F32)) + ob[...]
    middle[...] = mid
    xhat, _ = stats(mid)
    out[...] = (xhat * gain[pl.ds(k, 1), :] + bias[pl.ds(k, 1), :]).astype(BF16)


def norm_pull(v, d, gain):
    xhat, r = stats(v)
    e = d * gain
    m1 = jnp.mean(e, axis=-1, keepdims=True)
    m2 = jnp.mean(e * xhat, axis=-1, keepdims=True)
    return r * (e - m1 - xhat * m2), jnp.sum(d * xhat, axis=0, keepdims=True), jnp.sum(d, axis=0, keepdims=True)


def back_second(meta, middle, feed, feed_in, pb, ds, ds_in, ct, gain, block_out, dmid, dlow, small):
    k = meta[2]
    mid = middle[...]
    block_out[...] = (mid + (feed[...] + feed_in[...].astype(F32)) + pb[...]).astype(BF16)
    d, gg, gb = norm_pull(mid, ds[...] + ds_in[...].astype(F32), gain[pl.ds(k, 1), :])
    c = ct[...].astype(F32)
    d = d + c
    dmid[...] = d
    dlow[...] = d.astype(BF16)
    small[0:1, :] = jnp.sum(d, axis=0, keepdims=True)
    small[1:2, :] = jnp.sum(c, axis=0, keepdims=True)
    small[2:3, :] = gg
    small[3:4, :] = gb
    small[4:8, :] = jnp.zeros((4, small.shape[1]), F32)


def back_first(meta, x, df, df_in, dmid, gain, grad_in, small):
    k = meta[2]
    d, gg, gb = norm_pull(x[...].astype(F32), df[...] + df_in[...].astype(F32), gain[pl.ds(k, 1), :])
    grad_in[...] = (d + dmid[...]).astype(BF16)
    small[0:1, :] = gg
    small[1:2, :] = gb
    small[2:8, :] = jnp.zeros((6, small.shape[1]), F32)


def mask_scores(scores, start, length):
    span, count = scores.shape
    kpos = lax.broadcasted_iota(jnp.int32, (span, count), 0)
    limit = jnp.minimum(start + lax.broadcasted_iota(jnp.int32, (1, count), 1), length - 1)
    return jnp.where(kpos <= limit, scores, -1e30)


def attn_forward(first_call, block, meta, x_own, x_oth, w, b, ow, *rest):
    if first_call:
        qkv, lse, att, br_own, br_oth, k_s = rest
    else:
        pr_own, pr_oth, qkv, lse, att, br_own, br_oth, k_s = rest
    c, length = meta[0], meta[1]
    rows = x_own.shape[0]
    local = w.shape[0] // 3
    heads = local // HD
    span = 2 * rows
    parts = ((x_own, c), (x_oth, 1 - c))
    for x, p in parts:
        at = pl.ds(pl.multiple_of(p * rows, rows), rows)
        y = dg(w[...], x[...], NT) + b[...]
        for h in range(heads):
            lo = h * HD
            qkv[0, h, :, at] = (y[lo : lo + HD] * 0.125).astype(BF16)
            kt = y[local + lo : local + lo + HD]
            qkv[1, h, :, at] = kt.astype(BF16)
            k_s[h, at, :] = kt.T.astype(BF16)
            qkv[2, h, :, at] = y[2 * local + lo : 2 * local + lo + HD].astype(BF16)

    def head(h, carry):
        for i in range(span // block):
            stop = (i + 1) * block
            cols = slice(i * block, stop)
            scores = mm(k_s[h, :stop, :], qkv[0, h, :, cols])
            scores = mask_scores(scores, i * block, length)
            top = jnp.max(scores, axis=0, keepdims=True)
            e = jnp.exp(scores - top)
            total = jnp.sum(e, axis=0, keepdims=True)
            probs = (e * (1.0 / total)).astype(BF16)
            att[h, :, cols] = mm(qkv[2, h, :, :stop], probs).astype(BF16)
            lse[h, :, cols] = top + jnp.log(total)
        return carry

    lax.fori_loop(0, heads, head, 0)
    for (x, p), prev, out in zip(parts, (None, None) if first_call else (pr_own, pr_oth), (br_own, br_oth)):
        at = pl.ds(pl.multiple_of(p * rows, rows), rows)
        a = att[:, :, at].reshape(local, rows)
        r = dg(a, ow[...], TN)
        if prev is not None:
            r = r + prev[...]
        out[...] = r.astype(out.dtype)


def attn_backward(first_call, block, meta, qkv, lse, att, d_own, d_oth, x_own, x_oth, w, ow, *rest):
    if first_call:
        gq, go, gb, f_own, f_oth, do_n, do_t, q_n, k_n, v_n, dqkv, dk, dv = rest
    else:
        pf_own, pf_oth, gq, go, gb, f_own, f_oth, do_n, do_t, q_n, k_n, v_n, dqkv, dk, dv = rest
    c, length = meta[0], meta[1]
    rows = x_own.shape[0]
    local = w.shape[0] // 3
    heads = local // HD
    span = 2 * rows
    spots = [pl.ds(pl.multiple_of(p * rows, rows), rows) for p in (c, 1 - c)]
    gout = None
    for d, at in zip((d_own, d_oth), spots):
        y = dg(ow[...], d[...], NT)
        for h in range(heads):
            part = y[h * HD : h * HD + HD]
            do_t[h, :, at] = part.astype(BF16)
            do_n[h, at, :] = part.T.astype(BF16)
        a = att[:, :, at].reshape(local, rows)
        term = mm(a, d[...])
        gout = term if gout is None else gout + term
    go[...] = gout.astype(go.dtype)

    def head(h, carry):
        q_n[...] = qkv[0, h].astype(F32).T.astype(BF16)
        k_n[...] = qkv[1, h].astype(F32).T.astype(BF16)
        v_n[...] = qkv[2, h].astype(F32).T.astype(BF16)
        for i in range(span // block):
            stop = (i + 1) * block
            cols = slice(i * block, stop)
            scores = mm(k_n[:stop, :], qkv[0, h, :, cols])
            scores = mask_scores(scores, i * block, length)
            probs = jnp.exp(scores - lse[h, :, cols])
            dp = mm(v_n[:stop, :], do_t[h, :, cols])
            total = jnp.sum(probs * dp, axis=0, keepdims=True)
            ds = (probs * (dp - total)).astype(BF16)
            dqkv[0, h, :, cols] = (mm(qkv[1, h, :, :stop], ds) * 0.125).astype(BF16)
            pv = mm(probs.astype(BF16), do_n[h, cols, :])
            pk = mm(ds, q_n[cols, :])
            last = i * block
            if i:
                dv[:last, :] += pv[:last]
                dk[:last, :] += pk[:last]
            dv[last:stop, :] = pv[last:]
            dk[last:stop, :] = pk[last:]
        dqkv[1, h] = dk[...].T.astype(BF16)
        dqkv[2, h] = dv[...].T.astype(BF16)
        return carry

    lax.fori_loop(0, heads, head, 0)
    gqkv = None
    gbias = None
    for x, at, prev, out in zip((x_own, x_oth), spots, (None, None) if first_call else (pf_own, pf_oth), (f_own, f_oth)):
        d = dqkv[:, :, :, at].reshape(3 * local, rows)
        term = mm(d, x[...])
        gqkv = term if gqkv is None else gqkv + term
        s = jnp.sum(d.astype(F32), axis=1, keepdims=True)
        gbias = s if gbias is None else gbias + s
        r = dg(d, w[...], TN)
        if prev is not None:
            r = r + prev[...]
        out[...] = r.astype(out.dtype)
    gq[...] = gqkv.astype(gq.dtype)
    gb[...] = gbias


def mlp_kernel(first_call, s_own, s_oth, c_own, c_oth, fc, fb, pw, *rest):
    if first_call:
        gf, gp, gb, fe_own, fe_oth, ds_own, ds_oth, st = rest
        prev = (None, None, None, None)
    else:
        prev = rest[:4]
        gf, gp, gb, fe_own, fe_oth, ds_own, ds_oth, st = rest[4:12]
        accs = rest[12:]
    j = pl.program_id(0)
    rows = s_own.shape[0]

    @pl.when(j == 0)
    def _():
        st[:, :rows] = s_own[...].T
        st[:, rows:] = s_oth[...].T

    gfc = gproj = gbias = None
    for n, (s, ct, fe, ds) in enumerate(((s_own, c_own, fe_own, ds_own), (s_oth, c_oth, fe_oth, ds_oth))):
        pre = mm(s[...], fc[...]) + fb[...]
        sq = pre * pre
        t = jnp.tanh(GELU_K * (pre + GELU_C * sq * pre))
        half = 0.5 * (1.0 + t)
        act = (pre * half).astype(BF16)
        slope = half + (0.5 * GELU_K) * pre * (1.0 - t * t) * (1.0 + (3.0 * GELU_C) * sq)
        dpre = dg(ct[...], pw[...], NT) * slope
        low = dpre.astype(BF16)
        bs = jnp.sum(low.astype(F32), axis=0, keepdims=True)
        tf = mm(st[:, n * rows : (n + 1) * rows], low)
        tp = dg(act, ct[...], TN)
        gfc = tf if gfc is None else gfc + tf
        gproj = tp if gproj is None else gproj + tp
        gbias = bs if gbias is None else gbias + bs
        add_f = mm(act, pw[...])
        add_s = dg(low, fc[...], NT)
        if first_call:
            fa, sa, pf, ps = fe, ds, None, None
        else:
            fa, sa = accs[2 * n], accs[2 * n + 1]
            pf, ps = prev[n], prev[2 + n]

        @pl.when(j == 0)
        def _():
            fa[...] = add_f if pf is None else add_f + pf[...]
            sa[...] = add_s if ps is None else add_s + ps[...]

        @pl.when(j > 0)
        def _():
            fa[...] += add_f
            sa[...] += add_s

        if not first_call:
            @pl.when(j == pl.num_programs(0) - 1)
            def _():
                fe[...] = fa[...].astype(fe.dtype)
                ds[...] = sa[...].astype(ds.dtype)

    gf[...] = gfc.astype(gf.dtype)
    gp[...] = gproj.astype(gp.dtype)
    gb[...] = gbias


def mlp(first_call, s_own, s_oth, c_own, c_oth, fc, fb, pw, prev=()):
    rows, width = s_own.shape
    hidden = fc.shape[1]
    hb = 256
    fixed = pl.BlockSpec((rows, width), lambda j: (0, 0))
    oth = F32 if first_call else BF16
    sums = [(rows, width)] * 4
    scratch = [pltpu.VMEM((width, 2 * rows), BF16)]
    if not first_call:
        scratch += [pltpu.VMEM(s, F32) for s in sums]
    return pl.pallas_call(
        lambda *r: mlp_kernel(first_call, *r),
        grid=(hidden // hb,),
        in_specs=[fixed] * 4
        + [
            pl.BlockSpec((width, hb), lambda j: (0, j)),
            pl.BlockSpec((1, hb), lambda j: (0, j)),
            pl.BlockSpec((hb, width), lambda j: (j, 0)),
        ]
        + [fixed] * len(prev),
        out_specs=[
            pl.BlockSpec((width, hb), lambda j: (0, j)),
            pl.BlockSpec((hb, width), lambda j: (j, 0)),
            pl.BlockSpec((1, hb), lambda j: (0, j)),
        ]
        + [fixed] * 4,
        out_shape=[
            jax.ShapeDtypeStruct((width, hidden), BF16),
            jax.ShapeDtypeStruct((hidden, width), BF16),
            jax.ShapeDtypeStruct((1, hidden), F32),
            jax.ShapeDtypeStruct((rows, width), F32),
            jax.ShapeDtypeStruct((rows, width), oth),
            jax.ShapeDtypeStruct((rows, width), F32),
            jax.ShapeDtypeStruct((rows, width), oth),
        ],
        scratch_shapes=scratch,
        cost_estimate=pl.CostEstimate(flops=24 * rows * width * hidden, bytes_accessed=20 * rows * width, transcendentals=0),
        compiler_params=pltpu.CompilerParams(vmem_limit_bytes=56 << 20),
    )(s_own, s_oth, c_own, c_oth, fc, fb, pw, *prev)


def body(
    tokens,
    cotangent,
    lengths,
    tie_sets,
    qkv_weight,
    qkv_bias,
    out_weight,
    out_bias,
    fc_weight,
    fc_bias,
    proj_weight,
    proj_bias,
    norm_gain,
    norm_bias,
):
    rows, width = tokens.shape
    groups = lax.axis_size("tensor")
    local = qkv_weight.shape[2]
    heads = local // HD
    hidden = fc_weight.shape[1]
    span = rows * groups // lengths.shape[0]
    assert groups == 4 and span == 2 * rows
    set_count = norm_gain.shape[1]
    t = lax.axis_index("tensor")
    c, yy = t % 2, t // 2
    length = lax.dynamic_index_in_dim(lengths, yy, keepdims=False)
    my_set = lax.dynamic_index_in_dim(tie_sets, yy, keepdims=False)
    meta = jnp.stack([c, length, my_set]).astype(jnp.int32)

    def swap_core(v):
        return lax.ppermute(v, "tensor", [(i, i ^ 1) for i in range(4)])

    def swap_chip(v):
        return lax.ppermute(v, "tensor", [(i, i ^ 2) for i in range(4)])

    w_own = qkv_weight.transpose(1, 2, 0).reshape(3 * local, width)
    b_own = jnp.concatenate([qkv_bias[:1], jnp.zeros_like(qkv_bias[:1]), qkv_bias[1:]], axis=0)
    bias_pack = jnp.concatenate([b_own.reshape(1, 3 * local), fc_bias.reshape(1, hidden)], axis=1)
    w_oth = swap_chip(w_own)
    bias_oth = swap_chip(bias_pack)
    ow_oth = swap_chip(out_weight)
    fc_oth = swap_chip(fc_weight)
    pw_oth = swap_chip(proj_weight)
    c_oth = swap_core(cotangent)

    def col(pack):
        return pack[:, : 3 * local].astype(F32).reshape(3 * local, 1)

    def fcb(pack):
        return pack[:, 3 * local :].astype(F32)

    act_bytes = rows * width * 4
    first = call(norm_first, [((rows, width), BF16)], 4, smem=1, nbytes=act_bytes)(
        meta, tokens, norm_gain[0], norm_bias[0]
    )[0]
    first_oth = swap_core(first)

    block = min(256, span)
    att_flops = 2 * 2 * rows * width * 4 * local + heads * 4 * span * span * HD * 4
    saved = [((3, heads, HD, span), BF16), ((heads, 1, span), F32), ((heads, HD, span), BF16)]
    k_scr = [pltpu.VMEM((heads, span, HD), BF16)]

    def forward(first_call, w, b, ow, prev=()):
        outs = saved + [((rows, width), F32), ((rows, width), F32 if first_call else BF16)]
        return call(
            lambda *r: attn_forward(first_call, block, *r),
            outs,
            6 + len(prev),
            smem=1,
            scratch=k_scr,
            flops=att_flops,
            nbytes=8 * act_bytes,
        )(meta, first, first_oth, w, b, ow, *prev)

    qkv_a, lse_a, att_a, br_own, br_oth = forward(True, w_own, col(bias_pack), out_weight)
    qkv_b, lse_b, att_b, br_own, br_oth = forward(False, w_oth, col(bias_oth), ow_oth, (br_own, br_oth))
    br_in = swap_core(br_oth)
    middle, second = call(norm_second, [((rows, width), F32), ((rows, width), BF16)], 7, smem=1, nbytes=3 * act_bytes)(
        meta, tokens, br_own, br_in, out_bias.astype(F32).reshape(1, width), norm_gain[1], norm_bias[1]
    )
    second_oth = swap_core(second)
    gf_a, gp_a, gfb_a, fe_own, fe_oth, ds_own, ds_oth = mlp(
        True, second, second_oth, cotangent, c_oth, fc_weight, fcb(bias_pack), proj_weight
    )
    gf_b, gp_b, gfb_b, fe_own, fe_oth, ds_own, ds_oth = mlp(
        False, second, second_oth, cotangent, c_oth, fc_oth, fcb(bias_oth), pw_oth, (fe_own, fe_oth, ds_own, ds_oth)
    )
    ds_in = swap_core(ds_oth)
    fe_in = swap_core(fe_oth)
    block_out, dmid, dlow, small_two = call(
        back_second,
        [((rows, width), BF16), ((rows, width), F32), ((rows, width), BF16), ((8, width), F32)],
        9,
        smem=1,
        nbytes=6 * act_bytes,
    )(meta, middle, fe_own, fe_in, proj_bias.astype(F32).reshape(1, width), ds_own, ds_in, cotangent, norm_gain[1])
    dlow_oth = swap_core(dlow)

    def backward(first_call, qkv, lse, att, w, ow, prev=()):
        outs = [
            ((3 * local, width), BF16),
            ((local, width), BF16),
            ((3 * local, 1), F32),
            ((rows, width), F32),
            ((rows, width), F32 if first_call else BF16),
        ]
        n = pltpu.VMEM((heads, span, HD), BF16)
        tr = pltpu.VMEM((heads, HD, span), BF16)
        one = pltpu.VMEM((span, HD), BF16)
        acc = pltpu.VMEM((span, HD), F32)
        return call(
            lambda *r: attn_backward(first_call, block, *r),
            outs,
            10 + len(prev),
            smem=1,
            scratch=[n, tr, one, one, one, pltpu.VMEM((3, heads, HD, span), BF16), acc, acc],
            flops=3 * att_flops,
            nbytes=12 * act_bytes,
        )(meta, qkv, lse, att, dlow, dlow_oth, first, first_oth, w, ow, *prev)

    gq_b, go_b, gqb_b, df_own, df_oth = backward(True, qkv_b, lse_b, att_b, w_oth, ow_oth)
    gq_a, go_a, gqb_a, df_own, df_oth = backward(False, qkv_a, lse_a, att_a, w_own, out_weight, (df_own, df_oth))
    df_in = swap_core(df_oth)
    grad_input, small_one = call(back_first, [((rows, width), BF16), ((8, width), F32)], 6, smem=1, nbytes=4 * act_bytes)(
        meta, tokens, df_own, df_in, dmid, norm_gain[0]
    )

    def fold(own, other):
        return (own.astype(F32) + swap_chip(other).astype(F32)).astype(BF16)

    g_mlp = lax.psum((fold(gp_a, gp_b), fold(gf_a, gf_b)), "dp")
    g_att = lax.psum((fold(gq_a, gq_b), fold(go_a, go_b)), "dp")
    bias_b = swap_chip(jnp.concatenate([gqb_b.reshape(1, 3 * local), gfb_b], axis=1))
    bias_a = jnp.concatenate([gqb_a.reshape(1, 3 * local), gfb_a], axis=1)
    bias_sum = lax.psum(bias_a + bias_b, "dp")
    hot = (my_set == lax.broadcasted_iota(jnp.int32, (set_count, 1), 0)).astype(F32)
    pack = jnp.concatenate(
        [small_two[0:2]]
        + [v * hot for v in (small_one[0:1], small_two[2:3], small_one[1:2], small_two[3:4])],
        axis=0,
    )
    pack = lax.psum(pack, ("dp", "tensor"))
    gains = pack[2 : 2 + 2 * set_count].reshape(2, set_count, width)
    biases = pack[2 + 2 * set_count :].reshape(2, set_count, width)
    gqb = bias_sum[0, : 3 * local].reshape(3, local)
    return (
        block_out,
        grad_input,
        g_att[0].astype(F32).reshape(3, local, width).transpose(2, 0, 1),
        jnp.stack([gqb[0], gqb[2]]),
        g_att[1].astype(F32),
        pack[0],
        g_mlp[1].astype(F32),
        bias_sum[0, 3 * local :],
        g_mlp[0].astype(F32),
        pack[1],
        gains,
        biases,
    )


def solution(mesh):
    in_specs = (
        P(("dp", "tensor"), None),
        P(("dp", "tensor"), None),
        P("dp"),
        P("dp"),
        P(None, None, "tensor"),
        P(None, "tensor"),
        P("tensor", None),
        P(),
        P(None, "tensor"),
        P("tensor"),
        P("tensor", None),
        P(),
        P(),
        P(),
    )
    out_specs = (
        P(("dp", "tensor"), None),
        P(("dp", "tensor"), None),
        P(None, None, "tensor"),
        P(None, "tensor"),
        P("tensor", None),
        P(),
        P(None, "tensor"),
        P("tensor"),
        P("tensor", None),
        P(),
        P(),
        P(),
    )
    return jax.shard_map(body, mesh=mesh, in_specs=in_specs, out_specs=out_specs, check_vma=False)
```

```python
import jax
import jax.numpy as jnp
from jax import lax
from jax.experimental import pallas as pl
from jax.experimental.pallas import tpu as pltpu
from jax.sharding import PartitionSpec as P

HD = 64
EPS = 1e-05
F32 = jnp.float32
BF16 = jnp.bfloat16
GELU_K = 0.7978845608028654
GELU_C = 0.044715
VMEM = pl.BlockSpec(memory_space=pltpu.VMEM)
SMEM = pl.BlockSpec(memory_space=pltpu.SMEM)
NT = (((1,), (1,)), ((), ()))
TN = (((0,), (0,)), ((), ()))


def dg(a, b, dims):
    return lax.dot_general(a, b, dims, preferred_element_type=F32)


def mm(a, b):
    return jnp.dot(a, b, preferred_element_type=F32)


def call(kernel, outs, n_in, smem=0, scratch=(), limit=48, flops=0, nbytes=0):
    return pl.pallas_call(
        kernel,
        out_shape=[jax.ShapeDtypeStruct(s, d) for s, d in outs],
        in_specs=[SMEM] * smem + [VMEM] * (n_in - smem),
        out_specs=[VMEM] * len(outs),
        scratch_shapes=list(scratch),
        cost_estimate=pl.CostEstimate(flops=flops, bytes_accessed=nbytes, transcendentals=0),
        compiler_params=pltpu.CompilerParams(vmem_limit_bytes=limit << 20),
    )


def place():
    t = lax.axis_index("tensor")
    return t % 2, t // 2


def stats(v):
    mean = jnp.mean(v, axis=-1, keepdims=True)
    cent = v - mean
    var = jnp.mean(cent * cent, axis=-1, keepdims=True)
    r = lax.rsqrt(var + EPS)
    return cent * r, r


def norm_first(sets, x, gain, bias, out):
    k = sets[place()[1]]
    xhat, _ = stats(x[...].astype(F32))
    out[...] = (xhat * gain[pl.ds(k, 1), :] + bias[pl.ds(k, 1), :]).astype(BF16)


def norm_second(sets, x, br, br_in, ob, gain, bias, middle, out):
    k = sets[place()[1]]
    mid = x[...].astype(F32) + (br[...] + br_in[...].astype(F32)) + ob[...]
    middle[...] = mid
    xhat, _ = stats(mid)
    out[...] = (xhat * gain[pl.ds(k, 1), :] + bias[pl.ds(k, 1), :]).astype(BF16)


def norm_pull(v, d, gain):
    xhat, r = stats(v)
    e = d * gain
    m1 = jnp.mean(e, axis=-1, keepdims=True)
    m2 = jnp.mean(e * xhat, axis=-1, keepdims=True)
    return r * (e - m1 - xhat * m2), jnp.sum(d * xhat, axis=0, keepdims=True), jnp.sum(d, axis=0, keepdims=True)


def split_sets(small, at, k, count, gg, gb):
    for i in range(count):
        mine = (k == i).astype(F32)
        small[at + i : at + i + 1, :] = gg * mine
        small[at + count + i : at + count + i + 1, :] = gb * mine
    end = at + 2 * count
    small[end:, :] = jnp.zeros((small.shape[0] - end, small.shape[1]), F32)


def back_second(sets, middle, feed, feed_in, pb, ds, ds_in, ct, gain, block_out, dmid, dlow, small):
    k = sets[place()[1]]
    mid = middle[...]
    block_out[...] = (mid + (feed[...] + feed_in[...].astype(F32)) + pb[...]).astype(BF16)
    d, gg, gb = norm_pull(mid, ds[...] + ds_in[...].astype(F32), gain[pl.ds(k, 1), :])
    c = ct[...].astype(F32)
    d = d + c
    dmid[...] = d
    dlow[...] = d.astype(BF16)
    small[0:1, :] = jnp.sum(d, axis=0, keepdims=True)
    small[1:2, :] = jnp.sum(c, axis=0, keepdims=True)
    split_sets(small, 2, k, gain.shape[0], gg, gb)


def back_first(sets, x, df, df_in, dmid, gain, grad_in, small):
    k = sets[place()[1]]
    d, gg, gb = norm_pull(x[...].astype(F32), df[...] + df_in[...].astype(F32), gain[pl.ds(k, 1), :])
    grad_in[...] = (d + dmid[...]).astype(BF16)
    split_sets(small, 0, k, gain.shape[0], gg, gb)


def mask_scores(scores, start, length):
    span, count = scores.shape
    kpos = lax.broadcasted_iota(jnp.int32, (span, count), 0)
    limit = jnp.minimum(start + lax.broadcasted_iota(jnp.int32, (1, count), 1), length - 1)
    return jnp.where(kpos <= limit, scores, -1e30)


def attn_forward(first_call, block, lengths, x_own, x_oth, w, b, ow, *rest):
    if first_call:
        qkv, lse, att, br_own, br_oth, k_s = rest
    else:
        pr_own, pr_oth, qkv, lse, att, br_own, br_oth, k_s = rest
    c, seq = place()
    length = lengths[seq]
    rows = x_own.shape[0]
    local = w.shape[0] // 3
    heads = local // HD
    span = 2 * rows
    parts = ((x_own, c), (x_oth, 1 - c))
    for x, p in parts:
        at = pl.ds(pl.multiple_of(p * rows, rows), rows)
        y = dg(w[...], x[...], NT) + b[...]
        for h in range(heads):
            lo = h * HD
            qkv[0, h, :, at] = (y[lo : lo + HD] * 0.125).astype(BF16)
            kt = y[local + lo : local + lo + HD]
            qkv[1, h, :, at] = kt.astype(BF16)
            k_s[h, at, :] = kt.T.astype(BF16)
            qkv[2, h, :, at] = y[2 * local + lo : 2 * local + lo + HD].astype(BF16)

    def head(h, carry):
        for i in range(span // block):
            stop = (i + 1) * block
            cols = slice(i * block, stop)
            scores = mm(k_s[h, :stop, :], qkv[0, h, :, cols])
            scores = mask_scores(scores, i * block, length)
            top = jnp.max(scores, axis=0, keepdims=True)
            e = jnp.exp(scores - top)
            total = jnp.sum(e, axis=0, keepdims=True)
            probs = (e * (1.0 / total)).astype(BF16)
            att[h, :, cols] = mm(qkv[2, h, :, :stop], probs).astype(BF16)
            lse[h, :, cols] = top + jnp.log(total)
        return carry

    lax.fori_loop(0, heads, head, 0)
    for (x, p), prev, out in zip(parts, (None, None) if first_call else (pr_own, pr_oth), (br_own, br_oth)):
        at = pl.ds(pl.multiple_of(p * rows, rows), rows)
        a = att[:, :, at].reshape(local, rows)
        r = dg(a, ow[...], TN)
        if prev is not None:
            r = r + prev[...]
        out[...] = r.astype(out.dtype)


def attn_backward(first_call, block, lengths, qkv, lse, att, d_own, d_oth, x_own, x_oth, w, ow, *rest):
    if first_call:
        gq, gb, f_own, f_oth, do_n, do_t, q_n, k_n, v_n, dqkv, dk, dv = rest
    else:
        pf_own, pf_oth, gq, gb, f_own, f_oth, do_n, do_t, q_n, k_n, v_n, dqkv, dk, dv = rest
    c, seq = place()
    length = lengths[seq]
    rows = x_own.shape[0]
    local = w.shape[0] // 3
    heads = local // HD
    span = 2 * rows
    spots = [pl.ds(pl.multiple_of(p * rows, rows), rows) for p in (c, 1 - c)]
    gout = None
    for d, at in zip((d_own, d_oth), spots):
        y = dg(ow[...], d[...], NT)
        for h in range(heads):
            part = y[h * HD : h * HD + HD]
            do_t[h, :, at] = part.astype(BF16)
            do_n[h, at, :] = part.T.astype(BF16)
        a = att[:, :, at].reshape(local, rows)
        term = mm(a, d[...])
        gout = term if gout is None else gout + term
    gq[3 * local :, :] = gout.astype(gq.dtype)

    def head(h, carry):
        q_n[...] = qkv[0, h].astype(F32).T.astype(BF16)
        k_n[...] = qkv[1, h].astype(F32).T.astype(BF16)
        v_n[...] = qkv[2, h].astype(F32).T.astype(BF16)
        for i in range(span // block):
            stop = (i + 1) * block
            cols = slice(i * block, stop)
            scores = mm(k_n[:stop, :], qkv[0, h, :, cols])
            scores = mask_scores(scores, i * block, length)
            probs = jnp.exp(scores - lse[h, :, cols])
            dp = mm(v_n[:stop, :], do_t[h, :, cols])
            total = jnp.sum(probs * dp, axis=0, keepdims=True)
            ds = (probs * (dp - total)).astype(BF16)
            dqkv[0, h, :, cols] = (mm(qkv[1, h, :, :stop], ds) * 0.125).astype(BF16)
            pv = mm(probs.astype(BF16), do_n[h, cols, :])
            pk = mm(ds, q_n[cols, :])
            last = i * block
            if i:
                dv[:last, :] += pv[:last]
                dk[:last, :] += pk[:last]
            dv[last:stop, :] = pv[last:]
            dk[last:stop, :] = pk[last:]
        dqkv[1, h] = dk[...].T.astype(BF16)
        dqkv[2, h] = dv[...].T.astype(BF16)
        return carry

    lax.fori_loop(0, heads, head, 0)
    gqkv = None
    gbias = None
    for x, at, prev, out in zip((x_own, x_oth), spots, (None, None) if first_call else (pf_own, pf_oth), (f_own, f_oth)):
        d = dqkv[:, :, :, at].reshape(3 * local, rows)
        term = mm(d, x[...])
        gqkv = term if gqkv is None else gqkv + term
        s = dg(jnp.ones((8, rows), BF16), d, NT)
        gbias = s if gbias is None else gbias + s
        r = dg(d, w[...], TN)
        if prev is not None:
            r = r + prev[...]
        out[...] = r.astype(out.dtype)
    gq[: 3 * local, :] = gqkv.astype(gq.dtype)
    gb[...] = jnp.zeros_like(gb)
    gb[:, : 3 * local] = gbias


def mlp_kernel(first_call, s_own, s_oth, c_own, c_oth, fc, fb, pw, *rest):
    if first_call:
        gf, gp, gb, fe_own, fe_oth, ds_own, ds_oth, st = rest
        prev = (None, None, None, None)
    else:
        prev = rest[:4]
        gf, gp, gb, fe_own, fe_oth, ds_own, ds_oth, st = rest[4:12]
        accs = rest[12:]
    j = pl.program_id(0)
    rows = s_own.shape[0]

    @pl.when(j == 0)
    def _():
        st[:, :rows] = s_own[...].T
        st[:, rows:] = s_oth[...].T

    gfc = gproj = gbias = None
    for n, (s, ct, fe, ds) in enumerate(((s_own, c_own, fe_own, ds_own), (s_oth, c_oth, fe_oth, ds_oth))):
        pre = mm(s[...], fc[...]) + fb[...]
        sq = pre * pre
        t = jnp.tanh(GELU_K * (pre + GELU_C * sq * pre))
        half = 0.5 * (1.0 + t)
        act = (pre * half).astype(BF16)
        slope = half + (0.5 * GELU_K) * pre * (1.0 - t * t) * (1.0 + (3.0 * GELU_C) * sq)
        dpre = dg(ct[...], pw[...], NT) * slope
        low = dpre.astype(BF16)
        bs = jnp.sum(low.astype(F32), axis=0, keepdims=True)
        tf = mm(st[:, n * rows : (n + 1) * rows], low)
        tp = dg(act, ct[...], TN)
        gfc = tf if gfc is None else gfc + tf
        gproj = tp if gproj is None else gproj + tp
        gbias = bs if gbias is None else gbias + bs
        add_f = mm(act, pw[...])
        add_s = dg(low, fc[...], NT)
        if first_call:
            fa, sa, pf, ps = fe, ds, None, None
        else:
            fa, sa = accs[2 * n], accs[2 * n + 1]
            pf, ps = prev[n], prev[2 + n]

        @pl.when(j == 0)
        def _():
            fa[...] = add_f if pf is None else add_f + pf[...]
            sa[...] = add_s if ps is None else add_s + ps[...]

        @pl.when(j > 0)
        def _():
            fa[...] += add_f
            sa[...] += add_s

        if not first_call:
            @pl.when(j == pl.num_programs(0) - 1)
            def _():
                fe[...] = fa[...].astype(fe.dtype)
                ds[...] = sa[...].astype(ds.dtype)

    gf[...] = gfc.astype(gf.dtype)
    gp[...] = gproj.astype(gp.dtype)
    gb[...] = gbias


def mlp(first_call, s_own, s_oth, c_own, c_oth, fc, fb, pw, prev=()):
    rows, width = s_own.shape
    hidden = fc.shape[1]
    hb = 256
    fixed = pl.BlockSpec((rows, width), lambda j: (0, 0))
    oth = F32 if first_call else BF16
    sums = [(rows, width)] * 4
    scratch = [pltpu.VMEM((width, 2 * rows), BF16)]
    if not first_call:
        scratch += [pltpu.VMEM(s, F32) for s in sums]
    return pl.pallas_call(
        lambda *r: mlp_kernel(first_call, *r),
        grid=(hidden // hb,),
        in_specs=[fixed] * 4
        + [
            pl.BlockSpec((width, hb), lambda j: (0, j)),
            pl.BlockSpec((1, hb), lambda j: (0, j)),
            pl.BlockSpec((hb, width), lambda j: (j, 0)),
        ]
        + [fixed] * len(prev),
        out_specs=[
            pl.BlockSpec((width, hb), lambda j: (0, j)),
            pl.BlockSpec((hb, width), lambda j: (j, 0)),
            pl.BlockSpec((1, hb), lambda j: (0, j)),
        ]
        + [fixed] * 4,
        out_shape=[
            jax.ShapeDtypeStruct((width, hidden), BF16),
            jax.ShapeDtypeStruct((hidden, width), BF16),
            jax.ShapeDtypeStruct((1, hidden), F32),
            jax.ShapeDtypeStruct((rows, width), F32),
            jax.ShapeDtypeStruct((rows, width), oth),
            jax.ShapeDtypeStruct((rows, width), F32),
            jax.ShapeDtypeStruct((rows, width), oth),
        ],
        scratch_shapes=scratch,
        cost_estimate=pl.CostEstimate(flops=24 * rows * width * hidden, bytes_accessed=20 * rows * width, transcendentals=0),
        compiler_params=pltpu.CompilerParams(vmem_limit_bytes=56 << 20),
    )(s_own, s_oth, c_own, c_oth, fc, fb, pw, *prev)


def reduce_kernel(u_a, u_b, q_own, q_oth, small_two, small_one, qb_own, fb_own, qb_oth, fb_oth, o_a, o_b, o_q, o_pack, *scratch):
    acc, acc_o, r_y, r_x, r_xo, r_1, r_2, s_1, r_pack, send, recv = scratch
    t = lax.axis_index("tensor")
    d = lax.axis_index("dp")
    x, z1, z2 = d % 2, (d // 2) % 2, d // 4
    total, width = o_a.shape
    half, quarter, eighth = total // 2, total // 4, total // 8
    to = {
        "c": {"tensor": t + 1 - 2 * (t % 2)},
        "y": {"tensor": (t + 2) % 4},
        "x": {"dp": d + 1 - 2 * x},
        "1": {"dp": d + 2 - 4 * z1},
        "2": {"dp": (d + 4) % 8},
    }
    barrier = pltpu.get_barrier_semaphore()
    for where in to.values():
        pl.semaphore_signal(barrier, inc=1, device_id=where, device_id_type=pl.DeviceIdType.MESH)
    pl.semaphore_wait(barrier, len(to))

    def rows(start, n):
        return pl.ds(pl.multiple_of(start, 16), n)

    keep_x, give_x = rows(x * half, half), rows((1 - x) * half, half)
    keep_1 = rows(x * half + z1 * quarter, quarter)
    give_1 = rows(x * half + (1 - z1) * quarter, quarter)
    keep_2 = rows(x * half + z1 * quarter + z2 * eighth, eighth)
    live = {}

    def start(flow, n, where, src, dst):
        cp = pltpu.make_async_remote_copy(
            src_ref=src,
            dst_ref=dst,
            send_sem=send.at[flow, n],
            recv_sem=recv.at[flow, n],
            device_id=to[where],
            device_id_type=pl.DeviceIdType.MESH,
        )
        cp.start()
        live[flow, n] = cp

    def wait(flow, n):
        live[flow, n].wait()

    def add(dst, a, b):
        dst[...] = (a[...].astype(F32) + b[...].astype(F32)).astype(BF16)

    pair = [slice(0, width // 2), slice(width // 2, width)]
    flows = [("q", pair[0], "yx"), ("q", pair[1], "xy"), ("a", pair[0], ""), ("a", pair[1], ""), ("b", pair[0], ""), ("b", pair[1], "")]
    index = {"a": 0, "b": 1, "q": 2}
    out = {"a": o_a, "b": o_b, "q": o_q}
    half_in = {"a": u_a, "b": u_b}

    def step(f, k):
        unit, lanes, order = flows[f]
        u = index[unit]
        if k == 0:
            if order == "yx":
                start(f, 0, "y", q_oth.at[:, lanes], r_y.at[:, lanes])
            elif order == "xy":
                start(f, 7, "x", q_oth.at[give_x, lanes], r_xo.at[:, lanes])
                start(f, 0, "x", q_own.at[give_x, lanes], r_x.at[:, lanes])
        elif k == 1:
            if order == "yx":
                wait(f, 0)
                add(acc.at[:, lanes], q_own.at[:, lanes], r_y.at[:, lanes])
                start(f, 1, "x", acc.at[give_x, lanes], r_x.at[:, lanes])
            elif order == "xy":
                wait(f, 7)
                add(acc_o.at[:, lanes], q_oth.at[keep_x, lanes], r_xo.at[:, lanes])
                start(f, 1, "y", acc_o.at[:, lanes], r_y.at[rows(0, half), lanes])
                wait(f, 0)
                add(acc.at[keep_x, lanes], q_own.at[keep_x, lanes], r_x.at[:, lanes])
        elif k == 2:
            if order:
                wait(f, 1)
                here = acc.at[keep_x, lanes]
                add(here, here, r_x.at[:, lanes] if order == "yx" else r_y.at[rows(0, half), lanes])
                give = acc.at[give_1, lanes]
            else:
                give = half_in[unit].at[rows((1 - z1) * quarter, quarter), lanes]
            start(f, 2, "1", give, r_1.at[u, :, lanes])
        elif k == 3:
            wait(f, 2)
            here = acc.at[keep_1, lanes] if order else half_in[unit].at[rows(z1 * quarter, quarter), lanes]
            add(s_1.at[u, :, lanes], here, r_1.at[u, :, lanes])
            start(f, 3, "2", s_1.at[u, rows((1 - z2) * eighth, eighth), lanes], r_2.at[u, :, lanes])
        elif k == 4:
            wait(f, 3)
            here = out[unit].at[keep_2, lanes]
            add(here, s_1.at[u, rows(z2 * eighth, eighth), lanes], r_2.at[u, :, lanes])
            start(f, 4, "2", here, here)
        elif k == 5:
            wait(f, 4)
            here = out[unit].at[keep_1, lanes]
            start(f, 5, "1", here, here)
        elif k == 6:
            wait(f, 5)
            here = out[unit].at[keep_x, lanes]
            start(f, 6, "x", here, here)
        else:
            wait(f, 6)

    o_pack[:8, :] = small_two[...]
    o_pack[8:16, :] = small_one[...]
    for at, qb, fb in ((16, qb_own, fb_own), (24, qb_oth, fb_oth)):
        o_pack[at : at + 8, :] = qb[...]
        o_pack[at + 1 : at + 2, :] = fb[...]
    order = ("c", "y", "x", "1", "2")
    n_small = len(flows)

    def small(n):
        if n:
            wait(n_small, n - 1)
            got = r_pack[n - 1]
            top = o_pack[:16, :] + got[:16]
            mid = o_pack[16:24, :]
            if n == 2:
                mid = mid + got[24:]
            elif n > 2:
                mid = mid + got[16:24]
            o_pack[:16, :] = top
            o_pack[16:24, :] = mid
        if n < len(order):
            start(n_small, n, order[n], o_pack, r_pack.at[n])

    for f, k in EVENTS:
        if f < 0:
            small(k)
        else:
            step(f, k)


EVENTS = (
    [(0, 0), (1, 0), (-1, 0), (2, 2), (3, 2), (4, 2), (5, 2), (-1, 1)]
    + [(2, 3), (3, 3), (-1, 2), (4, 3), (5, 3), (0, 1), (1, 1), (-1, 3)]
    + [(2, 4), (3, 4), (-1, 4), (0, 2), (1, 2), (4, 4), (5, 4), (-1, 5)]
    + [(2, 5), (3, 5), (0, 3), (1, 3), (4, 5), (5, 5), (0, 4), (1, 4)]
    + [(2, 6), (3, 6), (0, 5), (1, 5), (4, 6), (5, 6), (0, 6), (1, 6)]
    + [(2, 7), (3, 7), (4, 7), (5, 7), (0, 7), (1, 7)]
)


def reduce_call(u_a, u_b, q_own, q_oth, *smalls):
    total, width = q_own.shape
    half, quarter, eighth = total // 2, total // 4, total // 8
    whole = jax.ShapeDtypeStruct((total, width), BF16)
    return pl.pallas_call(
        reduce_kernel,
        out_shape=[whole, whole, whole, jax.ShapeDtypeStruct((32, width), F32)],
        in_specs=[VMEM] * 10,
        out_specs=[VMEM] * 4,
        scratch_shapes=[
            pltpu.VMEM((total, width), BF16),
            pltpu.VMEM((half, width), BF16),
            pltpu.VMEM((total, width), BF16),
            pltpu.VMEM((half, width), BF16),
            pltpu.VMEM((half, width), BF16),
            pltpu.VMEM((3, quarter, width), BF16),
            pltpu.VMEM((3, eighth, width), BF16),
            pltpu.VMEM((3, quarter, width), BF16),
            pltpu.VMEM((5, 32, width), F32),
            pltpu.SemaphoreType.DMA((7, 8)),
            pltpu.SemaphoreType.DMA((7, 8)),
        ],
        compiler_params=pltpu.CompilerParams(vmem_limit_bytes=48 << 20, collective_id=1, has_side_effects=True),
    )(u_a, u_b, q_own, q_oth, *smalls)


def body(
    tokens,
    cotangent,
    lengths,
    tie_sets,
    qkv_weight,
    qkv_bias,
    out_weight,
    out_bias,
    fc_weight,
    fc_bias,
    proj_weight,
    proj_bias,
    norm_gain,
    norm_bias,
):
    rows, width = tokens.shape
    groups = lax.axis_size("tensor")
    local = qkv_weight.shape[2]
    heads = local // HD
    hidden = fc_weight.shape[1]
    span = rows * groups // lengths.shape[0]
    assert groups == 4 and span == 2 * rows
    set_count = norm_gain.shape[1]
    dps = lax.axis_size("dp")

    def swap_core(v):
        return lax.ppermute(v, "tensor", [(i, i ^ 1) for i in range(4)])

    def swap_chip(v):
        return lax.ppermute(v, "tensor", [(i, i ^ 2) for i in range(4)])

    def swap_dp(v):
        return lax.ppermute(v, "dp", [(i, i ^ 1) for i in range(dps)])

    def after(v, *first):
        return lax.optimization_barrier((v, *first))[0]

    w_own = qkv_weight.transpose(1, 2, 0).reshape(3 * local, width)
    b_own = jnp.concatenate([qkv_bias[:1], jnp.zeros_like(qkv_bias[:1]), qkv_bias[1:]], axis=0)
    bias_pack = jnp.concatenate([b_own.reshape(1, 3 * local), fc_bias.reshape(1, hidden)], axis=1)
    w_oth = swap_chip(w_own)
    bias_oth = swap_chip(bias_pack)
    ow_oth = swap_chip(out_weight)
    fc_oth = swap_chip(fc_weight)
    pw_oth = swap_chip(proj_weight)
    c_oth = swap_core(cotangent)

    def col(pack):
        return pack[:, : 3 * local].astype(F32).reshape(3 * local, 1)

    def fcb(pack):
        return pack[:, 3 * local :].astype(F32)

    act_bytes = rows * width * 4
    first = call(norm_first, [((rows, width), BF16)], 4, smem=1, nbytes=act_bytes)(
        tie_sets, tokens, norm_gain[0], norm_bias[0]
    )[0]
    first_oth = swap_core(first)

    block = min(256, span)
    att_flops = 2 * 2 * rows * width * 4 * local + heads * 4 * span * span * HD * 4
    saved = [((3, heads, HD, span), BF16), ((heads, 1, span), F32), ((heads, HD, span), BF16)]
    k_scr = [pltpu.VMEM((heads, span, HD), BF16)]

    def forward(first_call, w, b, ow, prev=()):
        outs = saved + [((rows, width), F32), ((rows, width), F32 if first_call else BF16)]
        return call(
            lambda *r: attn_forward(first_call, block, *r),
            outs,
            6 + len(prev),
            smem=1,
            scratch=k_scr,
            flops=att_flops,
            nbytes=8 * act_bytes,
        )(lengths, first, first_oth, w, b, ow, *prev)

    qkv_a, lse_a, att_a, br_own, br_oth = forward(True, w_own, col(bias_pack), out_weight)
    w_oth, bias_oth, ow_oth = (after(v, br_own) for v in (w_oth, bias_oth, ow_oth))
    qkv_b, lse_b, att_b, br_own, br_oth = forward(False, w_oth, col(bias_oth), ow_oth, (br_own, br_oth))
    br_in = swap_core(br_oth)
    middle, second = call(norm_second, [((rows, width), F32), ((rows, width), BF16)], 7, smem=1, nbytes=3 * act_bytes)(
        tie_sets, tokens, br_own, br_in, out_bias.astype(F32).reshape(1, width), norm_gain[1], norm_bias[1]
    )
    second_oth = swap_core(second)
    gf_a, gp_a, gfb_a, fe_own, fe_oth, ds_own, ds_oth = mlp(
        True, second, second_oth, cotangent, c_oth, fc_weight, fcb(bias_pack), proj_weight
    )
    fc_oth, pw_oth = (after(v, fe_own) for v in (fc_oth, pw_oth))
    gf_b, gp_b, gfb_b, fe_own, fe_oth, ds_own, ds_oth = mlp(
        False, second, second_oth, cotangent, c_oth, fc_oth, fcb(bias_oth), pw_oth, (fe_own, fe_oth, ds_own, ds_oth)
    )
    ds_in = swap_core(ds_oth)
    fe_in = swap_core(fe_oth)
    block_out, dmid, dlow, small_two = call(
        back_second,
        [((rows, width), BF16), ((rows, width), F32), ((rows, width), BF16), ((8, width), F32)],
        9,
        smem=1,
        nbytes=6 * act_bytes,
    )(tie_sets, middle, fe_own, fe_in, proj_bias.astype(F32).reshape(1, width), ds_own, ds_in, cotangent, norm_gain[1])
    dlow_oth = swap_core(dlow)

    def backward(first_call, qkv, lse, att, w, ow, prev=()):
        outs = [
            ((4 * local, width), BF16),
            ((8, width), F32),
            ((rows, width), F32),
            ((rows, width), F32 if first_call else BF16),
        ]
        n = pltpu.VMEM((heads, span, HD), BF16)
        tr = pltpu.VMEM((heads, HD, span), BF16)
        one = pltpu.VMEM((span, HD), BF16)
        acc = pltpu.VMEM((span, HD), F32)
        return call(
            lambda *r: attn_backward(first_call, block, *r),
            outs,
            10 + len(prev),
            smem=1,
            scratch=[n, tr, one, one, one, pltpu.VMEM((3, heads, HD, span), BF16), acc, acc],
            flops=3 * att_flops,
            nbytes=12 * act_bytes,
        )(lengths, qkv, lse, att, dlow, dlow_oth, first, first_oth, w, ow, *prev)

    bit = lax.axis_index("dp") % 2
    half = hidden // 2

    def part(v, which):
        return lax.dynamic_slice_in_dim(v, which * half, half, axis=0)

    custom = dps == 8
    if custom:
        gp_in = swap_chip(gp_b)
        gf_in = swap_dp(jnp.concatenate([part(gf_a, 1 - bit), part(gf_b, 1 - bit)], axis=0))
    gq_b, gqb_b, df_own, df_oth = backward(True, qkv_b, lse_b, att_b, w_oth, ow_oth)
    if custom:
        gp_in, gf_in = after(gp_in, df_own), after(gf_in, df_own)
        gp_sum = gp_a.astype(F32) + gp_in.astype(F32)
        gp_out = swap_dp(part(gp_sum, 1 - bit).astype(BF16))
        gf_out = swap_chip((part(gf_b, bit).astype(F32) + gf_in[half:].astype(F32)).astype(BF16))
        gp_keep = part(gp_sum, bit)
        gf_keep = part(gf_a, bit).astype(F32) + gf_in[:half].astype(F32)
    gq_a, gqb_a, df_own, df_oth = backward(False, qkv_a, lse_a, att_a, w_own, out_weight, (df_own, df_oth))
    df_in = swap_core(df_oth)
    grad_input, small_one = call(back_first, [((rows, width), BF16), ((8, width), F32)], 6, smem=1, nbytes=4 * act_bytes)(
        tie_sets, tokens, df_own, df_in, dmid, norm_gain[0]
    )
    if custom:
        gp_out, gf_out = after(gp_out, small_one), after(gf_out, small_one)
        u_p = (gp_keep + gp_out.astype(F32)).astype(BF16)
        u_f = (gf_keep + gf_out.astype(F32)).astype(BF16)
        g_p, g_f, g_q, pack = reduce_call(u_p, u_f, gq_a, gq_b, small_two, small_one, gqb_a, gfb_a, gqb_b, gfb_b)
    else:
        def total(own, other):
            return lax.psum((own.astype(F32) + swap_chip(other).astype(F32)).astype(BF16), "dp")

        g_p, g_f, g_q = total(gp_a, gp_b), total(gf_a, gf_b), total(gq_a, gq_b)
        bias_a = jnp.concatenate([gqb_a[:1], gfb_a], axis=0)
        bias_b = jnp.concatenate([gqb_b[:1], gfb_b], axis=0)
        pack = jnp.concatenate(
            [
                lax.psum(jnp.concatenate([small_two, small_one], axis=0), ("dp", "tensor")),
                lax.psum(bias_a + swap_chip(bias_b), "dp"),
            ],
            axis=0,
        )
    gains = jnp.stack([pack[8 : 8 + set_count], pack[2 : 2 + set_count]])
    biases = jnp.stack([pack[8 + set_count : 8 + 2 * set_count], pack[2 + set_count : 2 + 2 * set_count]])
    gqb = pack[16, : 3 * local].reshape(3, local)
    return (
        block_out,
        grad_input,
        g_q[: 3 * local].astype(F32).reshape(3, local, width).transpose(2, 0, 1),
        jnp.stack([gqb[0], gqb[2]]),
        g_q[3 * local :].astype(F32),
        pack[0],
        g_f.astype(F32),
        pack[17],
        g_p.astype(F32),
        pack[1],
        gains,
        biases,
    )


def solution(mesh):
    in_specs = (
        P(("dp", "tensor"), None),
        P(("dp", "tensor"), None),
        P("dp"),
        P("dp"),
        P(None, None, "tensor"),
        P(None, "tensor"),
        P("tensor", None),
        P(),
        P(None, "tensor"),
        P("tensor"),
        P("tensor", None),
        P(),
        P(),
        P(),
    )
    out_specs = (
        P(("dp", "tensor"), None),
        P(("dp", "tensor"), None),
        P(None, None, "tensor"),
        P(None, "tensor"),
        P("tensor", None),
        P(),
        P(None, "tensor"),
        P("tensor"),
        P("tensor", None),
        P(),
        P(),
        P(),
    )
    return jax.shard_map(body, mesh=mesh, in_specs=in_specs, out_specs=out_specs, check_vma=False)
```

```python
import jax
import jax.numpy as jnp
from jax import lax
from jax.experimental import pallas as pl
from jax.experimental.pallas import tpu as pltpu
from jax.sharding import PartitionSpec as P

HD = 64
EPS = 1e-05
F32 = jnp.float32
BF16 = jnp.bfloat16
GELU_K = 0.7978845608028654
GELU_C = 0.044715
VMEM = pl.BlockSpec(memory_space=pltpu.VMEM)
SMEM = pl.BlockSpec(memory_space=pltpu.SMEM)
NT = (((1,), (1,)), ((), ()))
TN = (((0,), (0,)), ((), ()))


def dg(a, b, dims):
    return lax.dot_general(a, b, dims, preferred_element_type=F32)


def mm(a, b):
    return jnp.dot(a, b, preferred_element_type=F32)


def call(kernel, outs, n_in, smem=0, scratch=(), limit=48, flops=0, nbytes=0):
    return pl.pallas_call(
        kernel,
        out_shape=[jax.ShapeDtypeStruct(s, d) for s, d in outs],
        in_specs=[SMEM] * smem + [VMEM] * (n_in - smem),
        out_specs=[VMEM] * len(outs),
        scratch_shapes=list(scratch),
        cost_estimate=pl.CostEstimate(flops=flops, bytes_accessed=nbytes, transcendentals=0),
        compiler_params=pltpu.CompilerParams(vmem_limit_bytes=limit << 20),
    )


def place():
    t = lax.axis_index("tensor")
    return t % 2, t // 2


def stats(v):
    mean = jnp.mean(v, axis=-1, keepdims=True)
    cent = v - mean
    var = jnp.mean(cent * cent, axis=-1, keepdims=True)
    r = lax.rsqrt(var + EPS)
    return cent * r, r


def norm_first(sets, x, gain, bias, out):
    k = sets[place()[1]]
    xhat, _ = stats(x[...].astype(F32))
    out[...] = (xhat * gain[pl.ds(k, 1), :] + bias[pl.ds(k, 1), :]).astype(BF16)


def norm_second(sets, x, br, br_in, ob, gain, bias, middle, out):
    k = sets[place()[1]]
    mid = x[...].astype(F32) + (br[...] + br_in[...].astype(F32)) + ob[...]
    middle[...] = mid
    xhat, _ = stats(mid)
    out[...] = (xhat * gain[pl.ds(k, 1), :] + bias[pl.ds(k, 1), :]).astype(BF16)


def norm_pull(v, d, gain):
    xhat, r = stats(v)
    e = d * gain
    m1 = jnp.mean(e, axis=-1, keepdims=True)
    m2 = jnp.mean(e * xhat, axis=-1, keepdims=True)
    return r * (e - m1 - xhat * m2), jnp.sum(d * xhat, axis=0, keepdims=True), jnp.sum(d, axis=0, keepdims=True)


def split_sets(small, at, k, count, gg, gb):
    for i in range(count):
        mine = (k == i).astype(F32)
        small[at + i : at + i + 1, :] = gg * mine
        small[at + count + i : at + count + i + 1, :] = gb * mine
    end = at + 2 * count
    small[end:, :] = jnp.zeros((small.shape[0] - end, small.shape[1]), F32)


def back_second(sets, middle, feed, feed_in, pb, ds, ds_in, ct, gain, block_out, dmid, dlow, small):
    k = sets[place()[1]]
    mid = middle[...]
    block_out[...] = (mid + (feed[...] + feed_in[...].astype(F32)) + pb[...]).astype(BF16)
    d, gg, gb = norm_pull(mid, ds[...] + ds_in[...].astype(F32), gain[pl.ds(k, 1), :])
    c = ct[...].astype(F32)
    d = d + c
    dmid[...] = d
    dlow[...] = d.astype(BF16)
    small[0:1, :] = jnp.sum(d, axis=0, keepdims=True)
    small[1:2, :] = jnp.sum(c, axis=0, keepdims=True)
    split_sets(small, 2, k, gain.shape[0], gg, gb)


def back_first(sets, x, df, df_in, dmid, gain, grad_in, small):
    k = sets[place()[1]]
    d, gg, gb = norm_pull(x[...].astype(F32), df[...] + df_in[...].astype(F32), gain[pl.ds(k, 1), :])
    grad_in[...] = (d + dmid[...]).astype(BF16)
    split_sets(small, 0, k, gain.shape[0], gg, gb)


def mask_scores(scores, start, length):
    span, count = scores.shape
    kpos = lax.broadcasted_iota(jnp.int32, (span, count), 0)
    limit = jnp.minimum(start + lax.broadcasted_iota(jnp.int32, (1, count), 1), length - 1)
    return jnp.where(kpos <= limit, scores, -1e30)


def attn_forward(first_call, block, lengths, x_own, x_oth, w, b, ow, *rest):
    if first_call:
        qkv, lse, att, br_own, br_oth, k_s = rest
    else:
        pr_own, pr_oth, qkv, lse, att, br_own, br_oth, k_s = rest
    c, seq = place()
    length = lengths[seq]
    rows = x_own.shape[0]
    local = w.shape[0] // 3
    heads = local // HD
    span = 2 * rows
    parts = ((x_own, c), (x_oth, 1 - c))
    for x, p in parts:
        at = pl.ds(pl.multiple_of(p * rows, rows), rows)
        y = dg(w[...], x[...], NT) + b[...]
        for h in range(heads):
            lo = h * HD
            qkv[0, h, :, at] = (y[lo : lo + HD] * 0.125).astype(BF16)
            kt = y[local + lo : local + lo + HD]
            qkv[1, h, :, at] = kt.astype(BF16)
            k_s[h, at, :] = kt.T.astype(BF16)
            qkv[2, h, :, at] = y[2 * local + lo : 2 * local + lo + HD].astype(BF16)

    def head(h, carry):
        for i in range(span // block):
            stop = (i + 1) * block
            cols = slice(i * block, stop)
            scores = mm(k_s[h, :stop, :], qkv[0, h, :, cols])
            scores = mask_scores(scores, i * block, length)
            top = jnp.max(scores, axis=0, keepdims=True)
            e = jnp.exp(scores - top)
            total = jnp.sum(e, axis=0, keepdims=True)
            probs = (e * (1.0 / total)).astype(BF16)
            att[h, :, cols] = mm(qkv[2, h, :, :stop], probs).astype(BF16)
            lse[h, :, cols] = top + jnp.log(total)
        return carry

    lax.fori_loop(0, heads, head, 0)
    for (x, p), prev, out in zip(parts, (None, None) if first_call else (pr_own, pr_oth), (br_own, br_oth)):
        at = pl.ds(pl.multiple_of(p * rows, rows), rows)
        a = att[:, :, at].reshape(local, rows)
        r = dg(a, ow[...], TN)
        if prev is not None:
            r = r + prev[...]
        out[...] = r.astype(out.dtype)


def attn_backward(first_call, block, lengths, qkv, lse, att, d_own, d_oth, x_own, x_oth, w, ow, *rest):
    if first_call:
        gq, gb, f_own, f_oth, do_n, do_t, q_n, k_n, v_n, dqkv, dk, dv = rest
    else:
        pf_own, pf_oth, gq, gb, f_own, f_oth, do_n, do_t, q_n, k_n, v_n, dqkv, dk, dv = rest
    c, seq = place()
    length = lengths[seq]
    rows = x_own.shape[0]
    local = w.shape[0] // 3
    heads = local // HD
    span = 2 * rows
    spots = [pl.ds(pl.multiple_of(p * rows, rows), rows) for p in (c, 1 - c)]
    gout = None
    for d, at in zip((d_own, d_oth), spots):
        y = dg(ow[...], d[...], NT)
        for h in range(heads):
            part = y[h * HD : h * HD + HD]
            do_t[h, :, at] = part.astype(BF16)
            do_n[h, at, :] = part.T.astype(BF16)
        a = att[:, :, at].reshape(local, rows)
        term = mm(a, d[...])
        gout = term if gout is None else gout + term
    gq[3 * local :, :] = gout.astype(gq.dtype)

    def head(h, carry):
        q_n[...] = qkv[0, h].astype(F32).T.astype(BF16)
        k_n[...] = qkv[1, h].astype(F32).T.astype(BF16)
        v_n[...] = qkv[2, h].astype(F32).T.astype(BF16)
        for i in range(span // block):
            stop = (i + 1) * block
            cols = slice(i * block, stop)
            scores = mm(k_n[:stop, :], qkv[0, h, :, cols])
            scores = mask_scores(scores, i * block, length)
            probs = jnp.exp(scores - lse[h, :, cols])
            dp = mm(v_n[:stop, :], do_t[h, :, cols])
            total = jnp.sum(probs * dp, axis=0, keepdims=True)
            ds = (probs * (dp - total)).astype(BF16)
            dqkv[0, h, :, cols] = (mm(qkv[1, h, :, :stop], ds) * 0.125).astype(BF16)
            pv = mm(probs.astype(BF16), do_n[h, cols, :])
            pk = mm(ds, q_n[cols, :])
            last = i * block
            if i:
                dv[:last, :] += pv[:last]
                dk[:last, :] += pk[:last]
            dv[last:stop, :] = pv[last:]
            dk[last:stop, :] = pk[last:]
        dqkv[1, h] = dk[...].T.astype(BF16)
        dqkv[2, h] = dv[...].T.astype(BF16)
        return carry

    lax.fori_loop(0, heads, head, 0)
    gqkv = None
    gbias = None
    for x, at, prev, out in zip((x_own, x_oth), spots, (None, None) if first_call else (pf_own, pf_oth), (f_own, f_oth)):
        d = dqkv[:, :, :, at].reshape(3 * local, rows)
        term = mm(d, x[...])
        gqkv = term if gqkv is None else gqkv + term
        s = dg(jnp.ones((8, rows), BF16), d, NT)
        gbias = s if gbias is None else gbias + s
        r = dg(d, w[...], TN)
        if prev is not None:
            r = r + prev[...]
        out[...] = r.astype(out.dtype)
    gq[: 3 * local, :] = gqkv.astype(gq.dtype)
    gb[...] = jnp.zeros_like(gb)
    gb[:, : 3 * local] = gbias


def mlp_kernel(first_call, s_own, s_oth, c_own, c_oth, fc, fb, pw, *rest):
    if first_call:
        gf, gp, gb, fe_own, fe_oth, ds_own, ds_oth, st = rest
        prev = (None, None, None, None)
    else:
        prev = rest[:4]
        gf, gp, gb, fe_own, fe_oth, ds_own, ds_oth, st = rest[4:12]
        accs = rest[12:]
    j = pl.program_id(0)
    rows = s_own.shape[0]

    @pl.when(j == 0)
    def _():
        st[:, :rows] = s_own[...].T
        st[:, rows:] = s_oth[...].T

    gfc = gproj = gbias = None
    for n, (s, ct, fe, ds) in enumerate(((s_own, c_own, fe_own, ds_own), (s_oth, c_oth, fe_oth, ds_oth))):
        pre = mm(s[...], fc[...]) + fb[...]
        sq = pre * pre
        t = jnp.tanh(GELU_K * (pre + GELU_C * sq * pre))
        half = 0.5 * (1.0 + t)
        act = (pre * half).astype(BF16)
        slope = half + (0.5 * GELU_K) * pre * (1.0 - t * t) * (1.0 + (3.0 * GELU_C) * sq)
        dpre = dg(ct[...], pw[...], NT) * slope
        low = dpre.astype(BF16)
        bs = jnp.sum(low.astype(F32), axis=0, keepdims=True)
        tf = mm(st[:, n * rows : (n + 1) * rows], low)
        tp = dg(act, ct[...], TN)
        gfc = tf if gfc is None else gfc + tf
        gproj = tp if gproj is None else gproj + tp
        gbias = bs if gbias is None else gbias + bs
        add_f = mm(act, pw[...])
        add_s = dg(low, fc[...], NT)
        if first_call:
            fa, sa, pf, ps = fe, ds, None, None
        else:
            fa, sa = accs[2 * n], accs[2 * n + 1]
            pf, ps = prev[n], prev[2 + n]

        @pl.when(j == 0)
        def _():
            fa[...] = add_f if pf is None else add_f + pf[...]
            sa[...] = add_s if ps is None else add_s + ps[...]

        @pl.when(j > 0)
        def _():
            fa[...] += add_f
            sa[...] += add_s

        if not first_call:
            @pl.when(j == pl.num_programs(0) - 1)
            def _():
                fe[...] = fa[...].astype(fe.dtype)
                ds[...] = sa[...].astype(ds.dtype)

    gf[...] = gfc.astype(gf.dtype)
    gp[...] = gproj.astype(gp.dtype)
    gb[...] = gbias


def mlp(first_call, s_own, s_oth, c_own, c_oth, fc, fb, pw, prev=()):
    rows, width = s_own.shape
    hidden = fc.shape[1]
    hb = 256
    fixed = pl.BlockSpec((rows, width), lambda j: (0, 0))
    oth = F32 if first_call else BF16
    sums = [(rows, width)] * 4
    scratch = [pltpu.VMEM((width, 2 * rows), BF16)]
    if not first_call:
        scratch += [pltpu.VMEM(s, F32) for s in sums]
    return pl.pallas_call(
        lambda *r: mlp_kernel(first_call, *r),
        grid=(hidden // hb,),
        in_specs=[fixed] * 4
        + [
            pl.BlockSpec((width, hb), lambda j: (0, j)),
            pl.BlockSpec((1, hb), lambda j: (0, j)),
            pl.BlockSpec((hb, width), lambda j: (j, 0)),
        ]
        + [fixed] * len(prev),
        out_specs=[
            pl.BlockSpec((width, hb), lambda j: (0, j)),
            pl.BlockSpec((hb, width), lambda j: (j, 0)),
            pl.BlockSpec((1, hb), lambda j: (0, j)),
        ]
        + [fixed] * 4,
        out_shape=[
            jax.ShapeDtypeStruct((width, hidden), BF16),
            jax.ShapeDtypeStruct((hidden, width), BF16),
            jax.ShapeDtypeStruct((1, hidden), F32),
            jax.ShapeDtypeStruct((rows, width), F32),
            jax.ShapeDtypeStruct((rows, width), oth),
            jax.ShapeDtypeStruct((rows, width), F32),
            jax.ShapeDtypeStruct((rows, width), oth),
        ],
        scratch_shapes=scratch,
        cost_estimate=pl.CostEstimate(flops=24 * rows * width * hidden, bytes_accessed=20 * rows * width, transcendentals=0),
        compiler_params=pltpu.CompilerParams(vmem_limit_bytes=56 << 20),
    )(s_own, s_oth, c_own, c_oth, fc, fb, pw, *prev)


def partners():
    t, d = lax.axis_index("tensor"), lax.axis_index("dp")
    bits = {"x": d % 2, "1": (d // 2) % 2, "2": d // 4}
    to = {
        "c": {"tensor": t + 1 - 2 * (t % 2)},
        "y": {"tensor": (t + 2) % 4},
        "x": {"dp": d + 1 - 2 * bits["x"]},
        "1": {"dp": d + 2 - 4 * bits["1"]},
        "2": {"dp": (d + 4) % 8},
        "3": {"dp": (d + 4) % 8 + 2 - 4 * bits["1"]},
    }
    return to, bits


def remote(src, dst, send, recv, where):
    return pltpu.make_async_remote_copy(
        src_ref=src, dst_ref=dst, send_sem=send, recv_sem=recv, device_id=where, device_id_type=pl.DeviceIdType.MESH
    )


def aligned(start, n):
    return pl.ds(pl.multiple_of(start, 16), n)


class Flow:
    def __init__(self, own, oth, res, buf, out, order, to, bits, sems):
        self.acts, self.out = [], pltpu.make_async_copy(res, out, sems(None))
        base, n, at, both = 0, own.shape[0], 0, True
        back, waits, adds, slot = [], [], [], 0
        for k, o in enumerate(order):
            copies, sums = [], []
            last = k == len(order) - 1
            if o == "y":
                here = aligned(base, n)
                got = buf.at[aligned(at, n)]
                at += n
                copies.append(remote(oth.at[here], got, *sems(slot), to[o]))
                sums.append(((res if last else own).at[here], own.at[here], [got]))
                slot += 1
                both = False
            else:
                size = n // 4 if o == "Z" else n // 2
                back.append((o, base, size))
                mine = bits["1"] + 2 * bits["2"] if o == "Z" else bits[o]
                keep = aligned(base + mine * size, size)
                for ref in (own, oth) if both else (own,):
                    gots = []
                    for peer in "123" if o == "Z" else o:
                        other = zs(bits, peer) if o == "Z" else 1 - mine
                        got = buf.at[aligned(at, size)]
                        at += size
                        copies.append(remote(ref.at[aligned(base + other * size, size)], got, *sems(slot), to[peer]))
                        gots.append(got)
                        slot += 1
                    sums.append(((res if last else ref).at[keep], ref.at[keep], gots))
                base, n = base + mine * size, size
            if k == 0 and both:
                self.acts += [([], [], copies[:1]), ([], [], copies[1:])]
            else:
                self.acts.append((waits, adds, copies))
            waits, adds = copies, sums
        for o, start, size in reversed(back):
            here = res.at[aligned(base, n)]
            copies = []
            for peer in "123" if o == "Z" else o:
                copies.append(remote(here, here, *sems(slot), to[peer]))
                slot += 1
            self.acts.append((waits, adds, copies))
            waits, adds = copies, []
            base, n = start, size * (4 if o == "Z" else 2)
        self.acts.append((waits, adds, [self.out]))

    def step(self, k):
        waits, adds, starts = self.acts[k]
        for copy in waits:
            copy.wait()
        for dst, mine, gots in adds:
            total = mine[...].astype(F32)
            for got in gots:
                total = total + got[...].astype(F32)
            dst[...] = total.astype(BF16)
        for copy in starts:
            copy.start()


def zs(bits, peer):
    one = 1 - bits["1"] if peer in "13" else bits["1"]
    two = 1 - bits["2"] if peer in "23" else bits["2"]
    return one + 2 * two


def pick(gains, chosen):
    row = gains[0:1, :]
    for i in range(1, gains.shape[0]):
        row = jnp.where(chosen == i, gains[i : i + 1, :], row)
    return row


def block_kernel(*refs):
    (lengths, sets, tok_h, ct_h, w_h, ow_h, fc_h, pw_h, bias_h, gains, biases, ob, pb) = refs[:13]
    block_out, grad_in, o_p, o_f, o_q, pack = refs[13:19]
    (tok, ct, ct_oth, first, first_oth, w, ow, fc, pw, bias, qkv, lse, att, nat, trn) = refs[19:34]
    (give, fe_send, br_in, middle, second, second_oth, st, acc, ds_in, fe_in) = refs[34:44]
    (dlow_oth, q_n, k_n, v_n, dqkv, dk, dv, df_in) = refs[44:52]
    (grad, res, buf, fbg, r_pack, load, sends, recvs, wsend, wrecv, done) = refs[52:]
    dlow = second
    block = 256
    to, bits = partners()
    c, seq = place()
    length, chosen = lengths[seq], sets[seq]
    rows, width = tok.shape
    local = ow.shape[1]
    heads = local // HD
    span = 2 * rows
    hidden = fc.shape[2]
    blocks = hidden // block
    spots = [pl.ds(pl.multiple_of(p * rows, rows), rows) for p in (c, 1 - c)]

    loads = {}
    for name, src, dst in (
        ("tok", tok_h, tok),
        ("w", w_h, w.at[0]),
        ("bias", bias_h, bias.at[0]),
        ("ow", ow_h, ow.at[0]),
        ("ct", ct_h, ct),
        ("fc", fc_h, fc.at[0]),
        ("pw", pw_h, pw.at[0]),
    ):
        loads[name] = pltpu.make_async_copy(src, dst, load.at[len(loads)])
        loads[name].start()

    barrier = pltpu.get_barrier_semaphore()
    for where in to.values():
        pl.semaphore_signal(barrier, inc=1, device_id=where, device_id_type=pl.DeviceIdType.MESH)
    pl.semaphore_wait(barrier, len(to))

    bias_copy = remote(bias_h, bias.at[1], wsend.at[0], wrecv.at[0], to["y"])
    pieces = []
    for src, dst, start, n in (
        (w_h, w, 0, local),
        (w_h, w, local, local),
        (w_h, w, 2 * local, local),
        (ow_h, ow, 0, local),
        (fc_h, fc, 0, width // 2),
        (fc_h, fc, width // 2, width // 2),
        (pw_h, pw, 0, hidden // 2),
        (pw_h, pw, hidden // 2, hidden // 2),
    ):
        k = 1 + 2 * len(pieces)
        half = aligned(start + bits["x"] * (n // 2), n // 2)
        there = dst.at[1, half]
        over = remote(src.at[half], there, wsend.at[k], wrecv.at[k], to["y"])
        on = remote(there, there, wsend.at[k + 1], wrecv.at[k + 1], to["x"])
        pieces.append((over, on))
    bias_copy.start()
    for over, _ in pieces:
        over.start()

    def forward(*which):
        for i in which:
            pieces[i][0].wait()
            pieces[i][1].start()

    def arrived(*which):
        for i in which:
            pieces[i][1].wait()

    outs = (o_p, o_f, o_q)
    flows = []
    n_flow = 9
    for f in range(n_flow):
        unit, j = f // 3, f % 3
        part = (slice(None), slice(j * block, (j + 1) * block)) if unit == 1 else (slice(j * block, (j + 1) * block),)
        room = (slice(None), part[1]) if unit == 1 else (slice(j * 2 * block, (j + 1) * 2 * block),)

        def sems(k, f=f):
            return done.at[f] if k is None else (sends.at[f, k], recvs.at[f, k])

        flows.append(
            Flow(
                grad.at[(0, unit, *part)],
                grad.at[(1, unit, *part)],
                res.at[(unit, *part)],
                buf.at[(unit, *room)],
                outs[unit].at[part],
                ORDERS[f],
                to,
                bits,
                sems,
            )
        )

    def swap(n, src, dst):
        return remote(src, dst, sends.at[n_flow, n], recvs.at[n_flow, n], to["c"])

    small_order = "cyx12"
    small_copies = [
        remote(pack, r_pack.at[n], sends.at[n_flow + 1, n], recvs.at[n_flow + 1, n], to[o]) for n, o in enumerate(small_order)
    ]

    def small(n):
        if n:
            small_copies[n - 1].wait()
            got = r_pack[n - 1]
            mid = pack[16:24, :]
            if n == 2:
                mid = mid + got[24:]
            elif n > 2:
                mid = mid + got[16:24]
            pack[:16, :] = pack[:16, :] + got[:16]
            pack[16:24, :] = mid
        if n < len(small_order):
            small_copies[n].start()

    def run(events):
        for f, k in events:
            if f < 0:
                small(k)
            else:
                flows[f].step(k)

    def at_step(i, table, what):
        for n, some in enumerate(table):
            if some:

                @pl.when(i == n)
                def _():
                    what(some)

    tile = 128

    def by_rows(step, carry=0):
        return lax.fori_loop(0, rows // tile, lambda i, held: step(pl.multiple_of(i * tile, tile), held), carry)

    def norm(n, v):
        return (stats(v)[0] * pick(gains[n], chosen) + pick(biases[n], chosen)).astype(BF16)

    zero = jnp.zeros((1, width), F32)

    loads["tok"].wait()

    def norm_tokens(r, carry):
        r = pl.ds(r, tile)
        first[r] = norm(0, tok[r].astype(F32))
        return carry

    by_rows(norm_tokens)
    first_swap = swap(0, first, first_oth)
    first_swap.start()
    loads["ct"].wait()
    ct_swap = swap(1, ct, ct_oth)
    ct_swap.start()
    loads["w"].wait()
    loads["bias"].wait()

    pick_row = (lax.broadcasted_iota(jnp.int32, (16, rows), 0) == 0).astype(BF16)

    def attend(s, carry):
        @pl.when(s == 1)
        def _():
            forward(2, 3)
            bias_copy.wait()
            arrived(0, 1, 2)

        col = dg(bias[s, :, hidden:], pick_row, TN)
        for n, (x, at) in enumerate(zip((first, first_oth), spots)):
            if n:

                @pl.when(s == 0)
                def _():
                    first_swap.wait()

            y = dg(w[s], x[...], NT) + col
            for h in range(heads):
                lo = h * HD
                qkv[s, 0, h, :, at] = (y[lo : lo + HD] * 0.125).astype(BF16)
                kt = y[local + lo : local + lo + HD]
                qkv[s, 1, h, :, at] = kt.astype(BF16)
                nat[h, at, :] = kt.T.astype(BF16)
                qkv[s, 2, h, :, at] = y[2 * local + lo : 2 * local + lo + HD].astype(BF16)

        def head(h, carry):
            for i in range(span // block):
                stop = (i + 1) * block
                cols = slice(i * block, stop)
                scores = mask_scores(mm(nat[h, :stop, :], qkv[s, 0, h, :, cols]), i * block, length)
                top = jnp.max(scores, axis=0, keepdims=True)
                e = jnp.exp(scores - top)
                total = jnp.sum(e, axis=0, keepdims=True)
                probs = (e * (1.0 / total)).astype(BF16)
                att[s, h, :, cols] = mm(qkv[s, 2, h, :, :stop], probs).astype(BF16)
                lse[s, h, :, cols] = top + jnp.log(total)
            at_step(s * heads + h, FORWARD_HEADS, lambda some: forward(*some))
            return carry

        lax.fori_loop(0, heads, head, 0)
        return carry

    lax.fori_loop(0, 2, attend, 0)
    loads["ow"].wait()
    arrived(3)

    def project(p, r):
        at = pl.ds(pl.multiple_of(p * rows + r, tile), tile)
        return dg(att[0, :, :, at].reshape(local, tile), ow[0], TN) + dg(att[1, :, :, at].reshape(local, tile), ow[1], TN)

    def project_other(r, carry):
        give[pl.ds(r, tile)] = project(1 - c, r).astype(BF16)
        return carry

    by_rows(project_other)
    br_swap = swap(2, give, br_in)
    br_swap.start()

    def project_own(r, carry):
        middle[pl.ds(r, tile)] = tok[pl.ds(r, tile)].astype(F32) + ob[...] + project(c, r)
        return carry

    by_rows(project_own)
    br_swap.wait()

    def norm_middle(r, carry):
        r = pl.ds(r, tile)
        mid = middle[r] + br_in[r].astype(F32)
        middle[r] = mid
        second[r] = norm(1, mid)
        return carry

    by_rows(norm_middle)
    second_swap = swap(3, second, second_oth)
    second_swap.start()
    st[:, :rows] = second[...].T
    loads["fc"].wait()
    loads["pw"].wait()

    def units(jj, carry):
        s, j = jj // blocks, jj % blocks
        here = pl.ds(pl.multiple_of(j * block, block), block)

        @pl.when(jj == blocks)
        def _():
            arrived(4, 5, 6, 7)

        gfc = gproj = gbias = None
        for n, (x, g) in enumerate(((second, ct), (second_oth, ct_oth))):
            if n:

                @pl.when(jj == 0)
                def _():
                    ct_swap.wait()
                    second_swap.wait()
                    st[:, rows:] = second_oth[...].T

            pre = mm(x[...], fc[s, :, here]) + bias[s, 0:1, here].astype(F32)
            sq = pre * pre
            t = jnp.tanh(GELU_K * (pre + GELU_C * sq * pre))
            half = 0.5 * (1.0 + t)
            act = (pre * half).astype(BF16)
            slope = half + (0.5 * GELU_K) * pre * (1.0 - t * t) * (1.0 + (3.0 * GELU_C) * sq)
            low = (dg(g[...], pw[s, here, :], NT) * slope).astype(BF16)
            bs = jnp.sum(low.astype(F32), axis=0, keepdims=True)
            tf = mm(st[:, n * rows : (n + 1) * rows], low)
            tp = dg(act, g[...], TN)
            gfc = tf if gfc is None else gfc + tf
            gproj = tp if gproj is None else gproj + tp
            gbias = bs if gbias is None else gbias + bs
            add_f = mm(act, pw[s, here, :])
            add_s = dg(low, fc[s, :, here], NT)

            @pl.when(jj == 0)
            def _():
                acc[n] = add_f
                acc[2 + n] = add_s

            @pl.when(jj > 0)
            def _():
                acc[n] += add_f
                acc[2 + n] += add_s

        grad[s, 1, :, here] = gfc.astype(BF16)
        grad[s, 0, here, :] = gproj.astype(BF16)
        fbg[s, 0:1, here] = gbias
        at_step(jj, FORWARD_UNITS, lambda some: forward(*some))
        at_step(jj, UNITS, run)
        return carry

    lax.fori_loop(0, 2 * blocks, units, 0)
    give[...] = acc[3].astype(BF16)
    ds_swap = swap(4, give, ds_in)
    ds_swap.start()
    fe_send[...] = acc[1].astype(BF16)
    fe_swap = swap(5, fe_send, fe_in)
    fe_swap.start()
    run(AFTER_UNITS)
    ds_swap.wait()
    fe_swap.wait()

    def back_middle(r, held):
        r = pl.ds(r, tile)
        mid, cot = middle[r], ct[r].astype(F32)
        block_out[r] = (mid + (acc[0, r] + fe_in[r].astype(F32)) + pb[...]).astype(BF16)
        d, gg, gb = norm_pull(mid, acc[2, r] + ds_in[r].astype(F32), pick(gains[1], chosen))
        d = d + cot
        middle[r] = d
        dlow[r] = d.astype(BF16)
        new = (jnp.sum(d, axis=0, keepdims=True), jnp.sum(cot, axis=0, keepdims=True), gg, gb)
        return tuple(a + b for a, b in zip(held, new))

    sums = by_rows(back_middle, (zero,) * 4)
    low_swap = swap(6, dlow, dlow_oth)
    low_swap.start()
    pack[0:1, :] = sums[0]
    pack[1:2, :] = sums[1]
    split_sets(pack.at[0:8], 2, chosen, gains.shape[1], sums[2], sums[3])
    run(AFTER_SECOND)

    def pull(i, carry):
        s = 1 - i
        for n, (g, at) in enumerate(zip((dlow, dlow_oth), spots)):
            if n:

                @pl.when(i == 0)
                def _():
                    low_swap.wait()

            y = dg(ow[s], g[...], NT)
            for h in range(heads):
                piece = y[h * HD : h * HD + HD]
                trn[h, :, at] = piece.astype(BF16)
                nat[h, at, :] = piece.T.astype(BF16)

        def head(h, carry):
            q_n[...] = qkv[s, 0, h].astype(F32).T.astype(BF16)
            k_n[...] = qkv[s, 1, h].astype(F32).T.astype(BF16)
            v_n[...] = qkv[s, 2, h].astype(F32).T.astype(BF16)
            for b in range(span // block):
                stop = (b + 1) * block
                last = b * block
                cols = slice(last, stop)
                scores = mask_scores(mm(k_n[:stop, :], qkv[s, 0, h, :, cols]), last, length)
                probs = jnp.exp(scores - lse[s, h, :, cols])
                dp = mm(v_n[:stop, :], trn[h, :, cols])
                total = jnp.sum(probs * dp, axis=0, keepdims=True)
                ds = (probs * (dp - total)).astype(BF16)
                dqkv[s, 0, h, :, cols] = (mm(qkv[s, 1, h, :, :stop], ds) * 0.125).astype(BF16)
                pv = mm(probs.astype(BF16), nat[h, cols, :])
                pk = mm(ds, q_n[cols, :])
                if b:
                    dv[:last, :] += pv[:last]
                    dk[:last, :] += pk[:last]
                dv[last:stop, :] = pv[last:]
                dk[last:stop, :] = pk[last:]
            dqkv[s, 1, h] = dk[...].T.astype(BF16)
            dqkv[s, 2, h] = dv[...].T.astype(BF16)
            gq = go = None
            for x, g, at in zip((first, first_oth), (dlow, dlow_oth), spots):
                tq = mm(dqkv[s, :, h, :, at].reshape(3 * HD, rows), x[...])
                to_ = mm(att[s, h, :, at], g[...])
                gq = tq if gq is None else gq + tq
                go = to_ if go is None else go + to_
            top = pl.multiple_of(h * 4 * HD, 4 * HD)
            grad[s, 2, pl.ds(top, 3 * HD), :] = gq.astype(BF16)
            grad[s, 2, pl.ds(top + 3 * HD, HD), :] = go.astype(BF16)
            at_step(i * heads + h, HEADS, run)
            return carry

        lax.fori_loop(0, heads, head, 0)
        return carry

    lax.fori_loop(0, 2, pull, 0)

    def pull_first(p, r):
        at = pl.ds(pl.multiple_of(p * rows + r, tile), tile)
        return dg(dqkv[0, :, :, :, at].reshape(3 * local, tile), w[0], TN) + dg(
            dqkv[1, :, :, :, at].reshape(3 * local, tile), w[1], TN
        )

    def pull_other(r, carry):
        give[pl.ds(r, tile)] = pull_first(1 - c, r).astype(BF16)
        return carry

    by_rows(pull_other)
    df_swap = swap(7, give, df_in)
    df_swap.start()
    run(AFTER_HEADS)

    def pull_own(r, carry):
        acc[0, pl.ds(r, tile)] = pull_first(c, r)
        return carry

    by_rows(pull_own)
    df_swap.wait()

    def back_tokens(r, held):
        r = pl.ds(r, tile)
        d, gg, gb = norm_pull(tok[r].astype(F32), acc[0, r] + df_in[r].astype(F32), pick(gains[0], chosen))
        grad_in[r] = (d + middle[r]).astype(BF16)
        return (held[0] + gg, held[1] + gb)

    sums = by_rows(back_tokens, (zero,) * 2)
    split_sets(pack.at[8:16], 0, chosen, gains.shape[1], sums[0], sums[1])
    for s in range(2):
        at = 16 + 8 * s
        pack[at : at + 8, :] = jnp.zeros((8, width), F32)
        pack[at : at + 1, : 3 * local] = dg(jnp.ones((8, span), BF16), dqkv[s].reshape(3 * local, span), NT)[0:1]
        pack[at + 1 : at + 2, :] = fbg[s, 0:1]
    run(TAIL)
    for flow in flows:
        flow.out.wait()


ORDERS = ("1xy2", "x1y2", "1xy2", "yxZ", "x1y2", "yxZ", "yxZ", "yxZ", "yxZ")
FORWARD_HEADS = ([0], [1], [], [4], [], [5])
FORWARD_UNITS = ([6], [7])
UNITS = (
    [(0, 0)],
    [(1, 0), (4, 0)],
    [(2, 0)],
    [(0, 1), (3, 0)],
    [(1, 1), (4, 1)],
    [(0, 2), (5, 0), (2, 1)],
)
AFTER_UNITS = [
    (1, 2), (3, 1),
]
AFTER_SECOND = [
    (4, 2), (0, 3), (2, 2),
]
HEADS = (
    [(0, 4), (1, 3), (3, 2), (4, 3), (5, 1), (6, 0), (2, 3)],
    [(1, 4), (0, 5), (7, 0)],
    [(4, 4), (3, 3), (8, 0), (5, 2)],
    [(1, 5), (0, 6), (4, 5), (6, 1), (2, 4)],
    [(0, 7), (5, 3), (3, 4)],
    [(1, 6), (6, 2), (4, 6), (7, 1)],
)
AFTER_HEADS = []
TAIL = [
    (-1, 0), (2, 5), (3, 5), (-1, 1), (0, 8), (8, 1), (7, 2), (5, 4), (-1, 2), (1, 7), (8, 2), (6, 3), (4, 7),
    (2, 6), (-1, 3), (5, 5), (7, 3), (1, 8), (8, 3), (4, 8), (2, 7), (-1, 4), (6, 4), (7, 4), (6, 5), (8, 4), (7, 5),
    (2, 8), (-1, 5), (8, 5),
]


def block_call(lengths, sets, tok, ct, w, ow, fc, pw, bias, gains, biases, ob, pb):
    rows, width = tok.shape
    local, hidden = ow.shape[0], fc.shape[1]
    heads, span = local // HD, 2 * rows
    total = 4 * local
    assert total == width == hidden
    any_spec = pl.BlockSpec(memory_space=pl.ANY)

    def v(*shape, dtype=BF16):
        return pltpu.VMEM(shape, dtype)

    act, wide = v(rows, width), v(rows, width, dtype=F32)
    one, one_acc = v(span, HD), v(span, HD, dtype=F32)
    dma = pltpu.SemaphoreType.DMA
    scratch = [act, act, act, act, act]
    scratch += [v(2, 3 * local, width), v(2, local, width), v(2, width, hidden), v(2, hidden, width), v(2, *bias.shape)]
    scratch += [v(2, 3, heads, HD, span), v(2, heads, 1, span, dtype=F32), v(2, heads, HD, span), v(heads, span, HD), v(heads, HD, span)]
    scratch += [act, act, act, wide, act, act, v(width, span), v(4, rows, width, dtype=F32), act, act]
    scratch += [act, one, one, one, v(2, 3, heads, HD, span), one_acc, one_acc, act]
    scratch += [v(2, 3, total, width), v(3, total, width), v(3, 2 * total, width), v(2, 8, hidden, dtype=F32), v(5, 32, width, dtype=F32)]
    scratch += [dma((7,)), dma((11, 16)), dma((11, 16)), dma((17,)), dma((17,)), dma((9,))]
    whole = jax.ShapeDtypeStruct((total, width), BF16)
    return pl.pallas_call(
        block_kernel,
        out_shape=[jax.ShapeDtypeStruct((rows, width), BF16)] * 2 + [whole] * 3 + [jax.ShapeDtypeStruct((32, width), F32)],
        in_specs=[SMEM] * 2 + [any_spec] * 7 + [VMEM] * 4,
        out_specs=[VMEM] * 2 + [any_spec] * 3 + [VMEM],
        scratch_shapes=scratch,
        compiler_params=pltpu.CompilerParams(vmem_limit_bytes=63 << 20, collective_id=1, has_side_effects=True),
    )(lengths, sets, tok, ct, w, ow, fc, pw, bias, gains, biases, ob, pb)


def generic(tokens, cotangent, lengths, tie_sets, qkv_weight, qkv_bias, out_weight, out_bias, fc_weight, fc_bias, proj_weight, proj_bias, norm_gain, norm_bias):
    rows, width = tokens.shape
    local = qkv_weight.shape[2]
    heads = local // HD
    hidden = fc_weight.shape[1]
    span = 2 * rows

    def swap_core(v):
        return lax.ppermute(v, "tensor", [(i, i ^ 1) for i in range(4)])

    def swap_chip(v):
        return lax.ppermute(v, "tensor", [(i, i ^ 2) for i in range(4)])

    def after(v, *first):
        return lax.optimization_barrier((v, *first))[0]

    w_own = qkv_weight.transpose(1, 2, 0).reshape(3 * local, width)
    b_own = jnp.concatenate([qkv_bias[:1], jnp.zeros_like(qkv_bias[:1]), qkv_bias[1:]], axis=0)
    bias_pack = jnp.concatenate([b_own.reshape(1, 3 * local), fc_bias.reshape(1, hidden)], axis=1)
    w_oth = swap_chip(w_own)
    bias_oth = swap_chip(bias_pack)
    ow_oth = swap_chip(out_weight)
    fc_oth = swap_chip(fc_weight)
    pw_oth = swap_chip(proj_weight)
    c_oth = swap_core(cotangent)

    def col(pack):
        return pack[:, : 3 * local].astype(F32).reshape(3 * local, 1)

    def fcb(pack):
        return pack[:, 3 * local :].astype(F32)

    act_bytes = rows * width * 4
    first = call(norm_first, [((rows, width), BF16)], 4, smem=1, nbytes=act_bytes)(
        tie_sets, tokens, norm_gain[0], norm_bias[0]
    )[0]
    first_oth = swap_core(first)

    block = min(256, span)
    att_flops = 2 * 2 * rows * width * 4 * local + heads * 4 * span * span * HD * 4
    saved = [((3, heads, HD, span), BF16), ((heads, 1, span), F32), ((heads, HD, span), BF16)]
    k_scr = [pltpu.VMEM((heads, span, HD), BF16)]

    def forward(first_call, w, b, ow, prev=()):
        outs = saved + [((rows, width), F32), ((rows, width), F32 if first_call else BF16)]
        return call(
            lambda *r: attn_forward(first_call, block, *r),
            outs,
            6 + len(prev),
            smem=1,
            scratch=k_scr,
            flops=att_flops,
            nbytes=8 * act_bytes,
        )(lengths, first, first_oth, w, b, ow, *prev)

    qkv_a, lse_a, att_a, br_own, br_oth = forward(True, w_own, col(bias_pack), out_weight)
    w_oth, bias_oth, ow_oth = (after(v, br_own) for v in (w_oth, bias_oth, ow_oth))
    qkv_b, lse_b, att_b, br_own, br_oth = forward(False, w_oth, col(bias_oth), ow_oth, (br_own, br_oth))
    br_in = swap_core(br_oth)
    middle, second = call(norm_second, [((rows, width), F32), ((rows, width), BF16)], 7, smem=1, nbytes=3 * act_bytes)(
        tie_sets, tokens, br_own, br_in, out_bias.astype(F32).reshape(1, width), norm_gain[1], norm_bias[1]
    )
    second_oth = swap_core(second)
    gf_a, gp_a, gfb_a, fe_own, fe_oth, ds_own, ds_oth = mlp(
        True, second, second_oth, cotangent, c_oth, fc_weight, fcb(bias_pack), proj_weight
    )
    fc_oth, pw_oth = (after(v, fe_own) for v in (fc_oth, pw_oth))
    gf_b, gp_b, gfb_b, fe_own, fe_oth, ds_own, ds_oth = mlp(
        False, second, second_oth, cotangent, c_oth, fc_oth, fcb(bias_oth), pw_oth, (fe_own, fe_oth, ds_own, ds_oth)
    )
    ds_in = swap_core(ds_oth)
    fe_in = swap_core(fe_oth)
    block_out, dmid, dlow, small_two = call(
        back_second,
        [((rows, width), BF16), ((rows, width), F32), ((rows, width), BF16), ((8, width), F32)],
        9,
        smem=1,
        nbytes=6 * act_bytes,
    )(tie_sets, middle, fe_own, fe_in, proj_bias.astype(F32).reshape(1, width), ds_own, ds_in, cotangent, norm_gain[1])
    dlow_oth = swap_core(dlow)

    def backward(first_call, qkv, lse, att, w, ow, prev=()):
        outs = [
            ((4 * local, width), BF16),
            ((8, width), F32),
            ((rows, width), F32),
            ((rows, width), F32 if first_call else BF16),
        ]
        n = pltpu.VMEM((heads, span, HD), BF16)
        tr = pltpu.VMEM((heads, HD, span), BF16)
        one = pltpu.VMEM((span, HD), BF16)
        acc = pltpu.VMEM((span, HD), F32)
        return call(
            lambda *r: attn_backward(first_call, block, *r),
            outs,
            10 + len(prev),
            smem=1,
            scratch=[n, tr, one, one, one, pltpu.VMEM((3, heads, HD, span), BF16), acc, acc],
            flops=3 * att_flops,
            nbytes=12 * act_bytes,
        )(lengths, qkv, lse, att, dlow, dlow_oth, first, first_oth, w, ow, *prev)

    gq_b, gqb_b, df_own, df_oth = backward(True, qkv_b, lse_b, att_b, w_oth, ow_oth)
    gq_a, gqb_a, df_own, df_oth = backward(False, qkv_a, lse_a, att_a, w_own, out_weight, (df_own, df_oth))
    df_in = swap_core(df_oth)
    grad_input, small_one = call(back_first, [((rows, width), BF16), ((8, width), F32)], 6, smem=1, nbytes=4 * act_bytes)(
        tie_sets, tokens, df_own, df_in, dmid, norm_gain[0]
    )
    def total(own, other):
        return lax.psum((own.astype(F32) + swap_chip(other).astype(F32)).astype(BF16), "dp")

    g_p, g_f, g_q = total(gp_a, gp_b), total(gf_a, gf_b), total(gq_a, gq_b)
    bias_a = jnp.concatenate([gqb_a[:1], gfb_a], axis=0)
    bias_b = jnp.concatenate([gqb_b[:1], gfb_b], axis=0)
    pack = jnp.concatenate(
        [
            lax.psum(jnp.concatenate([small_two, small_one], axis=0), ("dp", "tensor")),
            lax.psum(bias_a + swap_chip(bias_b), "dp"),
        ],
        axis=0,
    )
    return block_out, grad_input, g_p, g_f, g_q, pack


def body(
    tokens,
    cotangent,
    lengths,
    tie_sets,
    qkv_weight,
    qkv_bias,
    out_weight,
    out_bias,
    fc_weight,
    fc_bias,
    proj_weight,
    proj_bias,
    norm_gain,
    norm_bias,
):
    rows, width = tokens.shape
    groups = lax.axis_size("tensor")
    local = qkv_weight.shape[2]
    heads = local // HD
    hidden = fc_weight.shape[1]
    span = rows * groups // lengths.shape[0]
    assert groups == 4 and span == 2 * rows
    set_count = norm_gain.shape[1]
    dps = lax.axis_size("dp")

    if dps == 8:
        w = qkv_weight.transpose(1, 2, 0).reshape(3 * local, width)
        flat = jnp.concatenate([fc_bias, qkv_bias[0], jnp.zeros_like(qkv_bias[0]), qkv_bias[1]])
        bias = jnp.broadcast_to(flat[None], (16, hidden + 3 * local))
        block_out, grad_input, g_p, g_f, g_q, pack = block_call(
            lengths,
            tie_sets,
            tokens,
            cotangent,
            w,
            out_weight,
            fc_weight,
            proj_weight,
            bias,
            norm_gain,
            norm_bias,
            out_bias.astype(F32).reshape(1, width),
            proj_bias.astype(F32).reshape(1, width),
        )
        g_q = g_q.reshape(heads, 4, HD, width).transpose(1, 0, 2, 3).reshape(4 * local, width)
    else:
        block_out, grad_input, g_p, g_f, g_q, pack = generic(
            tokens,
            cotangent,
            lengths,
            tie_sets,
            qkv_weight,
            qkv_bias,
            out_weight,
            out_bias,
            fc_weight,
            fc_bias,
            proj_weight,
            proj_bias,
            norm_gain,
            norm_bias,
        )
    gains = jnp.stack([pack[8 : 8 + set_count], pack[2 : 2 + set_count]])
    biases = jnp.stack([pack[8 + set_count : 8 + 2 * set_count], pack[2 + set_count : 2 + 2 * set_count]])
    gqb = pack[16, : 3 * local].reshape(3, local)
    return (
        block_out,
        grad_input,
        g_q[: 3 * local].astype(F32).reshape(3, local, width).transpose(2, 0, 1),
        jnp.stack([gqb[0], gqb[2]]),
        g_q[3 * local :].astype(F32),
        pack[0],
        g_f.astype(F32),
        pack[17],
        g_p.astype(F32),
        pack[1],
        gains,
        biases,
    )


def solution(mesh):
    in_specs = (
        P(("dp", "tensor"), None),
        P(("dp", "tensor"), None),
        P("dp"),
        P("dp"),
        P(None, None, "tensor"),
        P(None, "tensor"),
        P("tensor", None),
        P(),
        P(None, "tensor"),
        P("tensor"),
        P("tensor", None),
        P(),
        P(),
        P(),
    )
    out_specs = (
        P(("dp", "tensor"), None),
        P(("dp", "tensor"), None),
        P(None, None, "tensor"),
        P(None, "tensor"),
        P("tensor", None),
        P(),
        P(None, "tensor"),
        P("tensor"),
        P("tensor", None),
        P(),
        P(),
        P(),
    )
    return jax.shard_map(body, mesh=mesh, in_specs=in_specs, out_specs=out_specs, check_vma=False)
```

```python
import jax
import jax.numpy as jnp
from jax import lax
from jax.experimental import pallas as pl
from jax.experimental.pallas import tpu as pltpu
from jax.sharding import PartitionSpec as P

HD = 64
EPS = 1e-05
F32 = jnp.float32
BF16 = jnp.bfloat16
GELU_K = 0.7978845608028654
GELU_C = 0.044715
VMEM = pl.BlockSpec(memory_space=pltpu.VMEM)
SMEM = pl.BlockSpec(memory_space=pltpu.SMEM)
NT = (((1,), (1,)), ((), ()))
TN = (((0,), (0,)), ((), ()))


def dg(a, b, dims):
    return lax.dot_general(a, b, dims, preferred_element_type=F32)


def mm(a, b):
    return jnp.dot(a, b, preferred_element_type=F32)


def call(kernel, outs, n_in, smem=0, scratch=(), limit=48, flops=0, nbytes=0):
    return pl.pallas_call(
        kernel,
        out_shape=[jax.ShapeDtypeStruct(s, d) for s, d in outs],
        in_specs=[SMEM] * smem + [VMEM] * (n_in - smem),
        out_specs=[VMEM] * len(outs),
        scratch_shapes=list(scratch),
        cost_estimate=pl.CostEstimate(flops=flops, bytes_accessed=nbytes, transcendentals=0),
        compiler_params=pltpu.CompilerParams(vmem_limit_bytes=limit << 20),
    )


def place():
    t = lax.axis_index("tensor")
    return t % 2, t // 2


def stats(v):
    mean = jnp.mean(v, axis=-1, keepdims=True)
    cent = v - mean
    var = jnp.mean(cent * cent, axis=-1, keepdims=True)
    r = lax.rsqrt(var + EPS)
    return cent * r, r


def norm_first(sets, x, gain, bias, out):
    k = sets[place()[1]]
    xhat, _ = stats(x[...].astype(F32))
    out[...] = (xhat * gain[pl.ds(k, 1), :] + bias[pl.ds(k, 1), :]).astype(BF16)


def norm_second(sets, x, br, br_in, ob, gain, bias, middle, out):
    k = sets[place()[1]]
    mid = x[...].astype(F32) + (br[...] + br_in[...].astype(F32)) + ob[...]
    middle[...] = mid
    xhat, _ = stats(mid)
    out[...] = (xhat * gain[pl.ds(k, 1), :] + bias[pl.ds(k, 1), :]).astype(BF16)


def norm_pull(v, d, gain):
    xhat, r = stats(v)
    e = d * gain
    m1 = jnp.mean(e, axis=-1, keepdims=True)
    m2 = jnp.mean(e * xhat, axis=-1, keepdims=True)
    return r * (e - m1 - xhat * m2), jnp.sum(d * xhat, axis=0, keepdims=True), jnp.sum(d, axis=0, keepdims=True)


def split_sets(small, at, k, count, gg, gb):
    for i in range(count):
        mine = (k == i).astype(F32)
        small[at + i : at + i + 1, :] = gg * mine
        small[at + count + i : at + count + i + 1, :] = gb * mine
    end = at + 2 * count
    small[end:, :] = jnp.zeros((small.shape[0] - end, small.shape[1]), F32)


def back_second(sets, middle, feed, feed_in, pb, ds, ds_in, ct, gain, block_out, dmid, dlow, small):
    k = sets[place()[1]]
    mid = middle[...]
    block_out[...] = (mid + (feed[...] + feed_in[...].astype(F32)) + pb[...]).astype(BF16)
    d, gg, gb = norm_pull(mid, ds[...] + ds_in[...].astype(F32), gain[pl.ds(k, 1), :])
    c = ct[...].astype(F32)
    d = d + c
    dmid[...] = d
    dlow[...] = d.astype(BF16)
    small[0:1, :] = jnp.sum(d, axis=0, keepdims=True)
    small[1:2, :] = jnp.sum(c, axis=0, keepdims=True)
    split_sets(small, 2, k, gain.shape[0], gg, gb)


def back_first(sets, x, df, df_in, dmid, gain, grad_in, small):
    k = sets[place()[1]]
    d, gg, gb = norm_pull(x[...].astype(F32), df[...] + df_in[...].astype(F32), gain[pl.ds(k, 1), :])
    grad_in[...] = (d + dmid[...]).astype(BF16)
    split_sets(small, 0, k, gain.shape[0], gg, gb)


def mask_scores(scores, start, length):
    span, count = scores.shape
    kpos = lax.broadcasted_iota(jnp.int32, (span, count), 0)
    limit = jnp.minimum(start + lax.broadcasted_iota(jnp.int32, (1, count), 1), length - 1)
    return jnp.where(kpos <= limit, scores, -1e30)


def attn_forward(first_call, block, lengths, x_own, x_oth, w, b, ow, *rest):
    if first_call:
        qkv, lse, att, br_own, br_oth, k_s = rest
    else:
        pr_own, pr_oth, qkv, lse, att, br_own, br_oth, k_s = rest
    c, seq = place()
    length = lengths[seq]
    rows = x_own.shape[0]
    local = w.shape[0] // 3
    heads = local // HD
    span = 2 * rows
    parts = ((x_own, c), (x_oth, 1 - c))
    for x, p in parts:
        at = pl.ds(pl.multiple_of(p * rows, rows), rows)
        y = dg(w[...], x[...], NT) + b[...]
        for h in range(heads):
            lo = h * HD
            qkv[0, h, :, at] = (y[lo : lo + HD] * 0.125).astype(BF16)
            kt = y[local + lo : local + lo + HD]
            qkv[1, h, :, at] = kt.astype(BF16)
            k_s[h, at, :] = kt.T.astype(BF16)
            qkv[2, h, :, at] = y[2 * local + lo : 2 * local + lo + HD].astype(BF16)

    def head(h, carry):
        for i in range(span // block):
            stop = (i + 1) * block
            cols = slice(i * block, stop)
            scores = mm(k_s[h, :stop, :], qkv[0, h, :, cols])
            scores = mask_scores(scores, i * block, length)
            top = jnp.max(scores, axis=0, keepdims=True)
            e = jnp.exp(scores - top)
            total = jnp.sum(e, axis=0, keepdims=True)
            probs = (e * (1.0 / total)).astype(BF16)
            att[h, :, cols] = mm(qkv[2, h, :, :stop], probs).astype(BF16)
            lse[h, :, cols] = top + jnp.log(total)
        return carry

    lax.fori_loop(0, heads, head, 0)
    for (x, p), prev, out in zip(parts, (None, None) if first_call else (pr_own, pr_oth), (br_own, br_oth)):
        at = pl.ds(pl.multiple_of(p * rows, rows), rows)
        a = att[:, :, at].reshape(local, rows)
        r = dg(a, ow[...], TN)
        if prev is not None:
            r = r + prev[...]
        out[...] = r.astype(out.dtype)


def attn_backward(first_call, block, lengths, qkv, lse, att, d_own, d_oth, x_own, x_oth, w, ow, *rest):
    if first_call:
        gq, gb, f_own, f_oth, do_n, do_t, q_n, k_n, v_n, dqkv, dk, dv = rest
    else:
        pf_own, pf_oth, gq, gb, f_own, f_oth, do_n, do_t, q_n, k_n, v_n, dqkv, dk, dv = rest
    c, seq = place()
    length = lengths[seq]
    rows = x_own.shape[0]
    local = w.shape[0] // 3
    heads = local // HD
    span = 2 * rows
    spots = [pl.ds(pl.multiple_of(p * rows, rows), rows) for p in (c, 1 - c)]
    gout = None
    for d, at in zip((d_own, d_oth), spots):
        y = dg(ow[...], d[...], NT)
        for h in range(heads):
            part = y[h * HD : h * HD + HD]
            do_t[h, :, at] = part.astype(BF16)
            do_n[h, at, :] = part.T.astype(BF16)
        a = att[:, :, at].reshape(local, rows)
        term = mm(a, d[...])
        gout = term if gout is None else gout + term
    gq[3 * local :, :] = gout.astype(gq.dtype)

    def head(h, carry):
        q_n[...] = qkv[0, h].astype(F32).T.astype(BF16)
        k_n[...] = qkv[1, h].astype(F32).T.astype(BF16)
        v_n[...] = qkv[2, h].astype(F32).T.astype(BF16)
        for i in range(span // block):
            stop = (i + 1) * block
            cols = slice(i * block, stop)
            scores = mm(k_n[:stop, :], qkv[0, h, :, cols])
            scores = mask_scores(scores, i * block, length)
            probs = jnp.exp(scores - lse[h, :, cols])
            dp = mm(v_n[:stop, :], do_t[h, :, cols])
            total = jnp.sum(probs * dp, axis=0, keepdims=True)
            ds = (probs * (dp - total)).astype(BF16)
            dqkv[0, h, :, cols] = (mm(qkv[1, h, :, :stop], ds) * 0.125).astype(BF16)
            pv = mm(probs.astype(BF16), do_n[h, cols, :])
            pk = mm(ds, q_n[cols, :])
            last = i * block
            if i:
                dv[:last, :] += pv[:last]
                dk[:last, :] += pk[:last]
            dv[last:stop, :] = pv[last:]
            dk[last:stop, :] = pk[last:]
        dqkv[1, h] = dk[...].T.astype(BF16)
        dqkv[2, h] = dv[...].T.astype(BF16)
        return carry

    lax.fori_loop(0, heads, head, 0)
    gqkv = None
    gbias = None
    for x, at, prev, out in zip((x_own, x_oth), spots, (None, None) if first_call else (pf_own, pf_oth), (f_own, f_oth)):
        d = dqkv[:, :, :, at].reshape(3 * local, rows)
        term = mm(d, x[...])
        gqkv = term if gqkv is None else gqkv + term
        s = dg(jnp.ones((8, rows), BF16), d, NT)
        gbias = s if gbias is None else gbias + s
        r = dg(d, w[...], TN)
        if prev is not None:
            r = r + prev[...]
        out[...] = r.astype(out.dtype)
    gq[: 3 * local, :] = gqkv.astype(gq.dtype)
    gb[...] = jnp.zeros_like(gb)
    gb[:, : 3 * local] = gbias


def mlp_kernel(first_call, s_own, s_oth, c_own, c_oth, fc, fb, pw, *rest):
    if first_call:
        gf, gp, gb, fe_own, fe_oth, ds_own, ds_oth, st = rest
        prev = (None, None, None, None)
    else:
        prev = rest[:4]
        gf, gp, gb, fe_own, fe_oth, ds_own, ds_oth, st = rest[4:12]
        accs = rest[12:]
    j = pl.program_id(0)
    rows = s_own.shape[0]

    @pl.when(j == 0)
    def _():
        st[:, :rows] = s_own[...].T
        st[:, rows:] = s_oth[...].T

    gfc = gproj = gbias = None
    for n, (s, ct, fe, ds) in enumerate(((s_own, c_own, fe_own, ds_own), (s_oth, c_oth, fe_oth, ds_oth))):
        pre = mm(s[...], fc[...]) + fb[...]
        sq = pre * pre
        t = jnp.tanh(GELU_K * (pre + GELU_C * sq * pre))
        half = 0.5 * (1.0 + t)
        act = (pre * half).astype(BF16)
        slope = half + (0.5 * GELU_K) * pre * (1.0 - t * t) * (1.0 + (3.0 * GELU_C) * sq)
        dpre = dg(ct[...], pw[...], NT) * slope
        low = dpre.astype(BF16)
        bs = jnp.sum(low.astype(F32), axis=0, keepdims=True)
        tf = mm(st[:, n * rows : (n + 1) * rows], low)
        tp = dg(act, ct[...], TN)
        gfc = tf if gfc is None else gfc + tf
        gproj = tp if gproj is None else gproj + tp
        gbias = bs if gbias is None else gbias + bs
        add_f = mm(act, pw[...])
        add_s = dg(low, fc[...], NT)
        if first_call:
            fa, sa, pf, ps = fe, ds, None, None
        else:
            fa, sa = accs[2 * n], accs[2 * n + 1]
            pf, ps = prev[n], prev[2 + n]

        @pl.when(j == 0)
        def _():
            fa[...] = add_f if pf is None else add_f + pf[...]
            sa[...] = add_s if ps is None else add_s + ps[...]

        @pl.when(j > 0)
        def _():
            fa[...] += add_f
            sa[...] += add_s

        if not first_call:
            @pl.when(j == pl.num_programs(0) - 1)
            def _():
                fe[...] = fa[...].astype(fe.dtype)
                ds[...] = sa[...].astype(ds.dtype)

    gf[...] = gfc.astype(gf.dtype)
    gp[...] = gproj.astype(gp.dtype)
    gb[...] = gbias


def mlp(first_call, s_own, s_oth, c_own, c_oth, fc, fb, pw, prev=()):
    rows, width = s_own.shape
    hidden = fc.shape[1]
    hb = 256
    fixed = pl.BlockSpec((rows, width), lambda j: (0, 0))
    oth = F32 if first_call else BF16
    sums = [(rows, width)] * 4
    scratch = [pltpu.VMEM((width, 2 * rows), BF16)]
    if not first_call:
        scratch += [pltpu.VMEM(s, F32) for s in sums]
    return pl.pallas_call(
        lambda *r: mlp_kernel(first_call, *r),
        grid=(hidden // hb,),
        in_specs=[fixed] * 4
        + [
            pl.BlockSpec((width, hb), lambda j: (0, j)),
            pl.BlockSpec((1, hb), lambda j: (0, j)),
            pl.BlockSpec((hb, width), lambda j: (j, 0)),
        ]
        + [fixed] * len(prev),
        out_specs=[
            pl.BlockSpec((width, hb), lambda j: (0, j)),
            pl.BlockSpec((hb, width), lambda j: (j, 0)),
            pl.BlockSpec((1, hb), lambda j: (0, j)),
        ]
        + [fixed] * 4,
        out_shape=[
            jax.ShapeDtypeStruct((width, hidden), BF16),
            jax.ShapeDtypeStruct((hidden, width), BF16),
            jax.ShapeDtypeStruct((1, hidden), F32),
            jax.ShapeDtypeStruct((rows, width), F32),
            jax.ShapeDtypeStruct((rows, width), oth),
            jax.ShapeDtypeStruct((rows, width), F32),
            jax.ShapeDtypeStruct((rows, width), oth),
        ],
        scratch_shapes=scratch,
        cost_estimate=pl.CostEstimate(flops=24 * rows * width * hidden, bytes_accessed=20 * rows * width, transcendentals=0),
        compiler_params=pltpu.CompilerParams(vmem_limit_bytes=56 << 20),
    )(s_own, s_oth, c_own, c_oth, fc, fb, pw, *prev)


def partners():
    t, d = lax.axis_index("tensor"), lax.axis_index("dp")
    bits = {"x": d % 2, "1": (d // 2) % 2, "2": d // 4}
    to = {
        "c": {"tensor": t + 1 - 2 * (t % 2)},
        "y": {"tensor": (t + 2) % 4},
        "x": {"dp": d + 1 - 2 * bits["x"]},
        "1": {"dp": d + 2 - 4 * bits["1"]},
        "2": {"dp": (d + 4) % 8},
        "3": {"dp": (d + 4) % 8 + 2 - 4 * bits["1"]},
    }
    return to, bits


def remote(src, dst, send, recv, where):
    return pltpu.make_async_remote_copy(
        src_ref=src, dst_ref=dst, send_sem=send, recv_sem=recv, device_id=where, device_id_type=pl.DeviceIdType.MESH
    )


def aligned(start, n, by=16):
    return pl.ds(pl.multiple_of(start, by), n)


class Flow:
    def __init__(self, own, oth, res, buf, outs, order, to, bits, sems):
        self.acts, self.outs = [], [pltpu.make_async_copy(res.at[src], out, sems(None)) for src, out in outs]
        base, n, at, both = 0, own.shape[0], 0, True
        back, waits, adds, slot = [], [], [], 0
        for k, o in enumerate(order):
            copies, sums = [], []
            last = k == len(order) - 1
            if o == "y":
                here = aligned(base, n)
                got = buf.at[aligned(at, n)]
                at += n
                copies.append(remote(oth.at[here], got, *sems(slot), to[o]))
                sums.append(((res if last else own).at[here], own.at[here], [got]))
                slot += 1
                both = False
            elif o == "e":
                here = aligned(base, n)
                got = buf.at[aligned(at, n)]
                copies.append(remote(own.at[here], got, *sems(slot), to["2"]))
                sums.append((res.at[here], own.at[here], [got]))
                slot += 1
            else:
                size = n // 4 if o == "Z" else n // 2
                back.append((o, base, size))
                mine = bits["1"] + 2 * bits["2"] if o == "Z" else bits[o]
                keep = aligned(base + mine * size, size)
                for ref in (own, oth) if both else (own,):
                    gots = []
                    for peer in "123" if o == "Z" else o:
                        other = zs(bits, peer) if o == "Z" else 1 - mine
                        got = buf.at[aligned(at, size)]
                        at += size
                        copies.append(remote(ref.at[aligned(base + other * size, size)], got, *sems(slot), to[peer]))
                        gots.append(got)
                        slot += 1
                    sums.append(((res if last else ref).at[keep], ref.at[keep], gots))
                base, n = base + mine * size, size
            if k == 0 and both:
                self.acts += [([], [], copies[:1]), ([], [], copies[1:])]
            else:
                self.acts.append((waits, adds, copies))
            waits, adds = copies, sums
        for o, start, size in reversed(back):
            here = res.at[aligned(base, n)]
            copies = []
            for peer in "123" if o == "Z" else o:
                copies.append(remote(here, here, *sems(slot), to[peer]))
                slot += 1
            self.acts.append((waits, adds, copies))
            waits, adds = copies, []
            base, n = start, size * (4 if o == "Z" else 2)
        self.acts.append((waits, adds, self.outs))

    def step(self, k):
        waits, adds, starts = self.acts[k]
        for copy in waits:
            copy.wait()
        for dst, mine, gots in adds:
            total = mine[...].astype(F32)
            for got in gots:
                total = total + got[...].astype(F32)
            dst[...] = total.astype(BF16)
        for copy in starts:
            copy.start()


def zs(bits, peer):
    one = 1 - bits["1"] if peer in "13" else bits["1"]
    two = 1 - bits["2"] if peer in "23" else bits["2"]
    return one + 2 * two


def pick(gains, chosen):
    row = gains[0:1, :]
    for i in range(1, gains.shape[0]):
        row = jnp.where(chosen == i, gains[i : i + 1, :], row)
    return row


def block_kernel(*refs):
    (lengths, sets, tok_h, ct_h, w_h, ow_h, fc_h, pw_h, qkv_b, fc_b, ob, pb, gains, biases) = refs[:14]
    block_out, grad_in, o_p, o_f, o_q, o_o, pack = refs[14:21]
    (tok, ct, ct_oth, first, first_oth, w, ow, fc, pw, bias, qkv, lse, att, nat, trn) = refs[21:36]
    (give, fe_send, br_in, middle, second, second_oth, st, acc, ds_in, fe_in) = refs[36:46]
    (dlow_oth, q_n, k_n, v_n, dqkv, dk, dv, df_in, q_t) = refs[46:55]
    (grad, res, buf, fbg, r_pack, load, sends, recvs, wsend, wrecv, done) = refs[55:]
    dlow = second
    block = 256
    to, bits = partners()
    c, seq = place()
    length, chosen = lengths[seq], sets[seq]
    rows, width = tok.shape
    local = ow.shape[1]
    heads = local // HD
    span = 2 * rows
    hidden = fc.shape[2]
    blocks = hidden // block
    spots = [pl.ds(pl.multiple_of(p * rows, rows), rows) for p in (c, 1 - c)]

    loads = {}
    for name, src, dst in (
        ("tok", tok_h, tok),
        ("w", w_h, w.at[0]),
        ("ow", ow_h, ow.at[0]),
        ("ct", ct_h, ct),
        ("fc", fc_h, fc.at[0]),
        ("pw", pw_h, pw.at[0]),
    ):
        loads[name] = pltpu.make_async_copy(src, dst, load.at[len(loads)])
        loads[name].start()

    barrier = pltpu.get_barrier_semaphore()
    for where in to.values():
        pl.semaphore_signal(barrier, inc=1, device_id=where, device_id_type=pl.DeviceIdType.MESH)
    pl.semaphore_wait(barrier, len(to))

    bias[0] = jnp.zeros(bias.shape[1:], BF16)
    edge = hidden + 256
    bias[0, 0:1, :hidden] = fc_b[...].reshape(1, hidden)
    bias[0, 0:1, hidden : hidden + local] = qkv_b[0:1, :]
    bias[0, 0:1, edge : edge + local] = qkv_b[1:2, :]
    bias_copy = remote(bias.at[0], bias.at[1], wsend.at[0], wrecv.at[0], to["y"])
    pieces = []
    for src, dst, start, n in (
        (w_h, w, 0, local),
        (w_h, w, local, local),
        (w_h, w, 2 * local, local),
        (ow_h, ow, 0, local),
        (fc_h, fc, 0, width // 2),
        (fc_h, fc, width // 2, width // 2),
        (pw_h, pw, 0, hidden // 2),
        (pw_h, pw, hidden // 2, hidden // 2),
    ):
        k = 1 + 4 * len(pieces)
        first_way, last_way = ("1", "x") if len(pieces) % 2 else ("x", "1")

        def quarter(x, z, start=start, n=n):
            return aligned(start + (2 * z + x) * (n // 4), n // 4, 8)

        mine = quarter(bits["x"], bits["1"])
        there = dst.at[1, mine]
        got = quarter(1 - bits["x"], bits["1"]) if first_way == "x" else quarter(bits["x"], 1 - bits["1"])
        pieces.append(
            (
                remote(src.at[mine], there, wsend.at[k], wrecv.at[k], to["y"]),
                remote(there, there, wsend.at[k + 1], wrecv.at[k + 1], to[first_way]),
                remote(there, there, wsend.at[k + 2], wrecv.at[k + 2], to[last_way]),
                remote(dst.at[1, got], dst.at[1, got], wsend.at[k + 3], wrecv.at[k + 3], to[last_way]),
            )
        )
    bias_copy.start()
    for over, *_ in pieces:
        over.start()

    def forward(acts):
        for i, act in acts:
            over, one, two, rest = pieces[i]
            if act == 0:
                over.wait()
                one.start()
                two.start()
            elif act == 1:
                one.wait()
                rest.start()
            else:
                two.wait()
                rest.wait()

    flows = []
    n_flow = 9
    for f in range(n_flow):
        unit, j = f // 3, f % 3
        part = (slice(None), slice(j * block, (j + 1) * block)) if unit == 1 else (slice(j * block, (j + 1) * block),)
        if unit < 2:
            outs = [((slice(None),), (o_p, o_f)[unit].at[part])]
        else:
            outs = [((slice(n * HD, (n + 1) * HD),), o_q.at[pl.ds(n * local + j * HD, HD)]) for n in range(3)]
            outs.append(((slice(3 * HD, 4 * HD),), o_o.at[pl.ds(j * HD, HD)]))
        room = (slice(None), part[1]) if unit == 1 else (slice(j * 2 * block, (j + 1) * 2 * block),)

        def sems(k, f=f):
            return done.at[f] if k is None else (sends.at[f, k], recvs.at[f, k])

        flows.append(
            Flow(
                grad.at[(0, unit, *part)],
                grad.at[(1, unit, *part)],
                res.at[(unit, *part)],
                buf.at[(unit, *room)],
                outs,
                ORDERS[f],
                to,
                bits,
                sems,
            )
        )

    def swap(n, src, dst):
        return remote(src, dst, sends.at[n_flow, n], recvs.at[n_flow, n], to["c"])

    small_order = "cyx12"
    small_copies = [
        remote(pack, r_pack.at[n], sends.at[n_flow + 1, n], recvs.at[n_flow + 1, n], to[o]) for n, o in enumerate(small_order)
    ]

    def small(n):
        if n:
            small_copies[n - 1].wait()
            got = r_pack[n - 1]
            mid = pack[16:24, :]
            if n == 2:
                mid = mid + got[24:]
            elif n > 2:
                mid = mid + got[16:24]
            pack[:16, :] = pack[:16, :] + got[:16]
            pack[16:24, :] = mid
        if n < len(small_order):
            small_copies[n].start()

    def run(events):
        for f, k in events:
            if f < 0:
                small(k)
            else:
                flows[f].step(k)

    def at_step(i, table, what):
        for n, some in enumerate(table):
            if some:

                @pl.when(i == n)
                def _():
                    what(some)

    tile = 128

    def by_rows(step, carry=0):
        return lax.fori_loop(0, rows // tile, lambda i, held: step(pl.multiple_of(i * tile, tile), held), carry)

    def norm(n, v):
        return (stats(v)[0] * pick(gains[n], chosen) + pick(biases[n], chosen)).astype(BF16)

    zero = jnp.zeros((1, width), F32)

    loads["tok"].wait()

    def norm_tokens(r, carry):
        r = pl.ds(r, tile)
        first[r] = norm(0, tok[r].astype(F32))
        return carry

    by_rows(norm_tokens)
    first_swap = swap(0, first, first_oth)
    first_swap.start()
    loads["ct"].wait()
    ct_swap = swap(1, ct, ct_oth)
    ct_swap.start()
    loads["w"].wait()

    q_t[HD:, :] = (lax.broadcasted_iota(jnp.int32, (HD, span), 0) == 0).astype(BF16)
    true_key = lax.broadcasted_iota(jnp.int32, (span, HD), 0) < length
    key_lane = lax.broadcasted_iota(jnp.int32, (span, HD), 1) == 0
    key_mask = jnp.where(true_key, 0.0, jnp.where(key_lane, -1e30, 0.0)).astype(BF16)
    for h in range(heads):
        nat[0, h, :, HD:] = key_mask
    k_n[:, HD:] = key_mask
    later = lax.broadcasted_iota(jnp.int32, (block, block), 0) > lax.broadcasted_iota(jnp.int32, (block, block), 1)

    def scores(keys, last, stop):
        cols = slice(last, stop)
        same = jnp.where(later, -1e30, mm(keys(cols), q_t[:, cols]))
        return [mm(keys(slice(0, last)), q_t[:, cols]), same] if last else [same]

    pick_row = (lax.broadcasted_iota(jnp.int32, (16, rows), 0) == 0).astype(BF16)

    def attend(s, carry):
        @pl.when(s == 1)
        def _():
            forward(FORWARD_SECOND)
            bias_copy.wait()

        q_col = dg(bias[s, :, hidden : hidden + local], pick_row, TN)
        v_col = dg(bias[s, :, edge : edge + local], pick_row, TN)
        for n, (x, at) in enumerate(zip((first, first_oth), spots)):
            if n:

                @pl.when(s == 0)
                def _():
                    first_swap.wait()

            y = dg(w[s], x[...], NT)
            for h in range(heads):
                lo = h * HD
                qkv[s, 0, h, :, at] = ((y[lo : lo + HD] + q_col[lo : lo + HD]) * 0.125).astype(BF16)
                kt = y[local + lo : local + lo + HD]
                qkv[s, 1, h, :, at] = kt.astype(BF16)
                nat[0, h, at, :HD] = kt.T.astype(BF16)
                vt = y[2 * local + lo : 2 * local + lo + HD]
                qkv[s, 2, h, :, at] = (vt + v_col[lo : lo + HD]).astype(BF16)
            at_step(s, FORWARD_ROWS[n], forward)

        def head(h, carry):
            q_t[:HD, :] = qkv[s, 0, h]
            for i in range(span // block):
                last, stop = i * block, (i + 1) * block
                cols = slice(last, stop)
                parts = scores(lambda rows: nat[0, h, rows, :], last, stop)
                top = parts[-1].max(axis=0, keepdims=True)
                if i:
                    top = jnp.maximum(top, parts[0].max(axis=0, keepdims=True))
                total = out = None
                for v, keys in zip(parts, (slice(0, last), cols) if i else (cols,)):
                    e = jnp.exp(v - top)
                    add = jnp.sum(e, axis=0, keepdims=True)
                    term = mm(qkv[s, 2, h, :, keys], e.astype(BF16))
                    total = add if total is None else total + add
                    out = term if out is None else out + term
                att[s, h, :, cols] = (out * (1.0 / total)).astype(BF16)
                lse[s, h, :, cols] = top + jnp.log(total)
            at_step(s * heads + h, FORWARD_HEADS, forward)
            return carry

        lax.fori_loop(0, heads, head, 0)
        return carry

    lax.fori_loop(0, 2, attend, 0)
    loads["ow"].wait()
    forward(FORWARD_PROJECT)

    def project(p, r):
        at = pl.ds(pl.multiple_of(p * rows + r, tile), tile)
        return dg(att[0, :, :, at].reshape(local, tile), ow[0], TN) + dg(att[1, :, :, at].reshape(local, tile), ow[1], TN)

    def project_other(r, carry):
        give[pl.ds(r, tile)] = project(1 - c, r).astype(BF16)
        return carry

    by_rows(project_other)
    br_swap = swap(2, give, br_in)
    br_swap.start()

    def project_own(r, carry):
        middle[pl.ds(r, tile)] = tok[pl.ds(r, tile)].astype(F32) + ob[...].astype(F32).reshape(1, width) + project(c, r)
        return carry

    by_rows(project_own)
    forward(FORWARD_MIDDLE)
    br_swap.wait()

    def norm_middle(r, carry):
        r = pl.ds(r, tile)
        mid = middle[r] + br_in[r].astype(F32)
        middle[r] = mid
        second[r] = norm(1, mid)
        return carry

    by_rows(norm_middle)
    forward(FORWARD_NORM)
    second_swap = swap(3, second, second_oth)
    second_swap.start()
    st[:, :rows] = second[...].T
    loads["fc"].wait()
    loads["pw"].wait()

    ds_swap, fe_swap = swap(4, give, ds_in), swap(5, fe_send, fe_in)
    halves = ((second, ct), (second_oth, ct_oth))

    def units(jj, carry, turn=(1, 0)):
        s, j = jj // blocks, jj % blocks
        here = pl.ds(pl.multiple_of(j * block, block), block)

        @pl.when(jj == blocks)
        def _():
            forward(FORWARD_OTHER)

        gfc = gproj = gbias = None
        for n in turn:
            x, g = halves[n]
            if turn == (0, 1) and n:
                ct_swap.wait()
                second_swap.wait()
                st[:, rows:] = second_oth[...].T
            pre = mm(x[...], fc[s, :, here]) + bias[s, 0:1, here].astype(F32)
            sq = pre * pre
            t = jnp.tanh(GELU_K * (pre + GELU_C * sq * pre))
            half = 0.5 * (1.0 + t)
            act = (pre * half).astype(BF16)
            slope = half + (0.5 * GELU_K) * pre * (1.0 - t * t) * (1.0 + (3.0 * GELU_C) * sq)
            low = (dg(g[...], pw[s, here, :], NT) * slope).astype(BF16)
            bs = jnp.sum(low.astype(F32), axis=0, keepdims=True)
            tf = mm(st[:, n * rows : (n + 1) * rows], low)
            tp = dg(act, g[...], TN)
            gfc = tf if gfc is None else gfc + tf
            gproj = tp if gproj is None else gproj + tp
            gbias = bs if gbias is None else gbias + bs
            add_f = mm(act, pw[s, here, :])
            add_s = dg(low, fc[s, :, here], NT)

            if turn == (0, 1):
                acc[n] = add_f
                acc[2 + n] = add_s
            else:
                acc[n] += add_f
                acc[2 + n] += add_s
            if n == 1:

                @pl.when(jj == 2 * blocks - 1)
                def _():
                    give[...] = acc[3].astype(BF16)
                    ds_swap.start()
                    fe_send[...] = acc[1].astype(BF16)
                    fe_swap.start()

            if n == turn[0]:
                at_step(jj, FORWARD_UNITS_MID, forward)
                at_step(jj, UNITS_MID, run)

        grad[s, 1, :, here] = gfc.astype(BF16)
        grad[s, 0, here, :] = gproj.astype(BF16)
        fbg[s, 0:1, here] = gbias
        at_step(jj, FORWARD_UNITS, forward)
        at_step(jj, UNITS, run)
        return carry

    units(0, 0, (0, 1))
    lax.fori_loop(1, 2 * blocks, units, 0)
    run(AFTER_UNITS)
    ds_swap.wait()
    fe_swap.wait()

    def back_middle(r, held):
        r = pl.ds(r, tile)
        mid, cot = middle[r], ct[r].astype(F32)
        block_out[r] = (mid + (acc[0, r] + fe_in[r].astype(F32)) + pb[...].astype(F32).reshape(1, width)).astype(BF16)
        d, gg, gb = norm_pull(mid, acc[2, r] + ds_in[r].astype(F32), pick(gains[1], chosen))
        d = d + cot
        middle[r] = d
        dlow[r] = d.astype(BF16)
        new = (jnp.sum(d, axis=0, keepdims=True), jnp.sum(cot, axis=0, keepdims=True), gg, gb)
        return tuple(a + b for a, b in zip(held, new))

    sums = by_rows(back_middle, (zero,) * 4)
    low_swap = swap(6, dlow, dlow_oth)
    low_swap.start()
    pack[0:1, :] = sums[0]
    pack[1:2, :] = sums[1]
    split_sets(pack.at[0:8], 2, chosen, gains.shape[1], sums[2], sums[3])
    run(AFTER_SECOND)

    for n, (g, at) in enumerate(zip((dlow, dlow_oth), spots)):
        if n:
            low_swap.wait()
        for s in range(2):
            y = dg(ow[s], g[...], NT)
            for h in range(heads):
                piece = y[h * HD : h * HD + HD]
                trn[s, h, :, at] = piece.astype(BF16)
                nat[s, h, at, :HD] = piece.T.astype(BF16)

    def pull(i, carry):
        s = h = 0
        for n, (shard, which) in enumerate(HEAD_ORDER):
            s, h = jnp.where(i == n, shard, s), jnp.where(i == n, which, h)
        q_t[:HD, :] = qkv[s, 0, h]
        q_n[...] = qkv[s, 0, h].astype(F32).T.astype(BF16)
        k_n[:, :HD] = qkv[s, 1, h].astype(F32).T.astype(BF16)
        v_n[...] = qkv[s, 2, h].astype(F32).T.astype(BF16)
        for b in range(span // block):
            last, stop = b * block, (b + 1) * block
            cols = slice(last, stop)
            parts = scores(lambda rows: k_n[rows, :], last, stop)
            total = jnp.sum(att[s, h, :, cols].astype(F32) * trn[s, h, :, cols].astype(F32), axis=0, keepdims=True)
            dq = None
            for v, keys in zip(parts, (slice(0, last), cols) if b else (cols,)):
                probs = jnp.exp(v - lse[s, h, :, cols])
                ds = (probs * (mm(v_n[keys, :], trn[s, h, :, cols]) - total)).astype(BF16)
                term = mm(qkv[s, 1, h, :, keys], ds)
                dq = term if dq is None else dq + term
                pv = mm(probs.astype(BF16), nat[s, h, cols, :HD])
                pk = mm(ds, q_n[cols, :])
                if keys.stop == stop:
                    dv[keys, :] = pv
                    dk[keys, :] = pk
                else:
                    dv[keys, :] += pv
                    dk[keys, :] += pk
            dqkv[s, 0, h, :, cols] = (dq * 0.125).astype(BF16)
            if stop < span:
                at_step(i, HEADS[b], run)
        dqkv[s, 1, h] = dk[...].T.astype(BF16)
        dqkv[s, 2, h] = dv[...].T.astype(BF16)
        gq = go = None
        for x, g, at in zip((first, first_oth), (dlow, dlow_oth), spots):
            tq = mm(dqkv[s, :, h, :, at].reshape(3 * HD, rows), x[...])
            to_ = mm(att[s, h, :, at], g[...])
            gq = tq if gq is None else gq + tq
            go = to_ if go is None else go + to_
        top = pl.multiple_of(h * 4 * HD, 4 * HD)
        grad[s, 2, pl.ds(top, 3 * HD), :] = gq.astype(BF16)
        grad[s, 2, pl.ds(top + 3 * HD, HD), :] = go.astype(BF16)
        at_step(i, HEADS[-1], run)
        return carry

    lax.fori_loop(0, 2 * heads, pull, 0)

    def pull_first(p, r):
        at = pl.ds(pl.multiple_of(p * rows + r, tile), tile)
        return dg(dqkv[0, :, :, :, at].reshape(3 * local, tile), w[0], TN) + dg(
            dqkv[1, :, :, :, at].reshape(3 * local, tile), w[1], TN
        )

    def pull_other(r, carry):
        give[pl.ds(r, tile)] = pull_first(1 - c, r).astype(BF16)
        return carry

    by_rows(pull_other)
    df_swap = swap(7, give, df_in)
    df_swap.start()
    run(AFTER_HEADS)

    def pull_own(r, carry):
        acc[0, pl.ds(r, tile)] = pull_first(c, r)
        return carry

    by_rows(pull_own)
    df_swap.wait()

    def back_tokens(r, held):
        r = pl.ds(r, tile)
        d, gg, gb = norm_pull(tok[r].astype(F32), acc[0, r] + df_in[r].astype(F32), pick(gains[0], chosen))
        grad_in[r] = (d + middle[r]).astype(BF16)
        return (held[0] + gg, held[1] + gb)

    sums = by_rows(back_tokens, (zero,) * 2)
    split_sets(pack.at[8:16], 0, chosen, gains.shape[1], sums[0], sums[1])
    for s in range(2):
        at = 16 + 8 * s
        pack[at : at + 8, :] = jnp.zeros((8, width), F32)
        pack[at : at + 1, : 3 * local] = dg(jnp.ones((8, span), BF16), dqkv[s].reshape(3 * local, span), NT)[0:1]
        pack[at + 1 : at + 2, :] = fbg[s, 0:1]
    run(TAIL)
    for flow in flows:
        for out in flow.outs:
            out.wait()


FORWARD_ROWS = ([[(0, 0), (1, 0)], []], [[(2, 0)], [(3, 1), (5, 0)]])
FORWARD_HEADS = ([(0, 1)], [(1, 1), (2, 1), (3, 0)], [(4, 0)], [], [], [(3, 2)])
FORWARD_SECOND = [(1, 2), (0, 2), (2, 2)]
FORWARD_PROJECT = []
FORWARD_MIDDLE = [(6, 0), (5, 1), (7, 0), (4, 1)]
FORWARD_NORM = []
FORWARD_OTHER = [(4, 2), (5, 2)]
FORWARD_UNITS_MID = ([], [(7, 1)], [])
FORWARD_UNITS = ([(6, 1)], [], [(6, 2), (7, 2)])
HEAD_ORDER = ((1, 0), (1, 1), (0, 0), (1, 2), (0, 1), (0, 2))
ORDERS = ("xy1e", "1xye", "x1ye", "yx1e", "xy12", "1yxe", "yx1e", "yx1e", "yx1e")
UNITS_MID = (
    [],
    [],
    [(4, 0)],
    [],
    [],
    [(4, 1)],
)
UNITS = (
    [],
    [(0, 0), (1, 0)],
    [],
    [(3, 0), (0, 1), (5, 0)],
    [],
    [(5, 1), (0, 2)],
)
AFTER_UNITS = [
    (3, 1), (1, 1),
]
AFTER_SECOND = [
    (4, 2), (2, 0), (2, 1), (5, 2), (0, 3),
]
HEADS = (
    (
        [],
        [],
        [(3, 3), (5, 3)],
        [(5, 4)],
        [(1, 3), (8, 0)],
        [],
    ),
    (
        [(3, 2)],
        [(4, 3)],
        [(1, 2), (0, 5), (4, 4)],
        [(3, 4), (6, 1)],
        [(5, 5), (3, 5)],
        [(0, 6), (2, 3)],
    ),
    (
        [],
        [],
        [],
        [(4, 5)],
        [(6, 2)],
        [(6, 3), (5, 6)],
    ),
    (
        [(0, 4), (6, 0)],
        [],
        [(7, 0)],
        [(2, 2)],
        [(4, 6), (7, 1)],
        [(3, 6), (1, 4)],
    ),
)
AFTER_HEADS = [
    (8, 1), (6, 4), (7, 2),
]
TAIL = [
    (-1, 0), (4, 7), (5, 7), (2, 4), (1, 5), (-1, 1), (8, 2), (7, 3), (4, 8), (-1, 2), (2, 5), (6, 5), (8, 3),
    (0, 7), (7, 4), (-1, 3), (2, 6), (6, 6), (8, 4), (7, 5), (2, 7), (-1, 4), (1, 6), (8, 5), (7, 6), (8, 6),
    (-1, 5), (1, 7),
]


def block_call(lengths, sets, tok, ct, w, ow, fc, pw, qkv_b, fc_b, ob, pb, gains, biases):
    rows, width = tok.shape
    local, hidden = ow.shape[0], fc.shape[1]
    heads, span = local // HD, 2 * rows
    total = 4 * local
    assert total == width == hidden
    any_spec = pl.BlockSpec(memory_space=pl.ANY)

    def v(*shape, dtype=BF16):
        return pltpu.VMEM(shape, dtype)

    act, wide = v(rows, width), v(rows, width, dtype=F32)
    one, one_acc = v(span, HD), v(span, HD, dtype=F32)
    dma = pltpu.SemaphoreType.DMA
    scratch = [act, act, act, act, act]
    scratch += [v(2, 3 * local, width), v(2, local, width), v(2, width, hidden), v(2, hidden, width), v(2, 16, hidden + 512)]
    scratch += [v(2, 3, heads, HD, span), v(2, heads, 1, span, dtype=F32), v(2, heads, HD, span), v(2, heads, span, 2 * HD), v(2, heads, HD, span)]
    scratch += [act, act, act, wide, act, act, v(width, span), v(4, rows, width, dtype=F32), act, act]
    scratch += [act, one, v(span, 2 * HD), one, v(2, 3, heads, HD, span), one_acc, one_acc, act, v(2 * HD, span)]
    scratch += [v(2, 3, total, width), v(3, total, width), v(3, 2 * total, width), v(2, 8, hidden, dtype=F32), v(5, 32, width, dtype=F32)]
    scratch += [dma((7,)), dma((11, 16)), dma((11, 16)), dma((33,)), dma((33,)), dma((9,))]
    shapes = [(rows, width)] * 2 + [(total, width)] * 2 + [(3 * local, width), (local, width)]
    return pl.pallas_call(
        block_kernel,
        out_shape=[jax.ShapeDtypeStruct(s, BF16) for s in shapes] + [jax.ShapeDtypeStruct((32, width), F32)],
        in_specs=[SMEM] * 2 + [any_spec] * 6 + [VMEM] * 6,
        out_specs=[VMEM] * 2 + [any_spec] * 4 + [VMEM],
        scratch_shapes=scratch,
        compiler_params=pltpu.CompilerParams(vmem_limit_bytes=63 << 20, collective_id=1, has_side_effects=True),
    )(lengths, sets, tok, ct, w, ow, fc, pw, qkv_b, fc_b, ob, pb, gains, biases)


def finish_kernel(b, g, p, f, q, o, pack, block_out, grad_in, gq, gqb, go, gob, gf, gfb, gp, gpb, gains, biases):
    block_out[...] = b[...]
    grad_in[...] = g[...]
    for src, dst in ((p, gp), (f, gf), (q, gq), (o, go)):
        dst[...] = src[...].astype(F32)

    @pl.when(pl.program_id(0) == 0)
    def _():
        local = gqb.shape[1]
        count = gains.shape[1]
        gqb[0:1, :] = pack[16:17, :local]
        gqb[1:2, :] = pack[16:17, 2 * local : 3 * local]
        for row, dst in ((0, gob), (1, gpb), (17, gfb)):
            dst[...] = pack[row : row + 1, :].reshape(dst.shape)
        for n, at in ((0, 8), (1, 2)):
            gains[n] = pack[at : at + count, :]
            biases[n] = pack[at + count : at + 2 * count, :]


def finish(parts, local, count):
    rows, width = parts[0].shape
    steps = 4

    def spec(array):
        return pl.BlockSpec((array.shape[0] // steps, width), lambda i: (i, 0))

    def whole(*shape):
        return pl.BlockSpec(shape, lambda i: (0,) * len(shape))

    b, g, p, f, q, o, pack = parts
    sets = (2, count, width)
    small = [(2, local), (width,), (p.shape[0],), (width,), sets, sets]
    order = [(b, BF16), (g, BF16), (q, F32), small[0], (o, F32), small[1], (f, F32), small[2], (p, F32)] + small[3:]
    big = [isinstance(v[0], jax.Array) for v in order]
    return pl.pallas_call(
        finish_kernel,
        grid=(steps,),
        in_specs=[spec(v) for v in parts[:6]] + [whole(*pack.shape)],
        out_specs=[spec(v[0]) if k else whole(*v) for v, k in zip(order, big)],
        out_shape=[jax.ShapeDtypeStruct(*((v[0].shape, v[1]) if k else (v, F32))) for v, k in zip(order, big)],
    )(*parts)


def generic(tokens, cotangent, lengths, tie_sets, qkv_weight, qkv_bias, out_weight, out_bias, fc_weight, fc_bias, proj_weight, proj_bias, norm_gain, norm_bias):
    rows, width = tokens.shape
    local = qkv_weight.shape[2]
    heads = local // HD
    hidden = fc_weight.shape[1]
    span = 2 * rows

    def swap_core(v):
        return lax.ppermute(v, "tensor", [(i, i ^ 1) for i in range(4)])

    def swap_chip(v):
        return lax.ppermute(v, "tensor", [(i, i ^ 2) for i in range(4)])

    def after(v, *first):
        return lax.optimization_barrier((v, *first))[0]

    w_own = qkv_weight.transpose(1, 2, 0).reshape(3 * local, width)
    b_own = jnp.concatenate([qkv_bias[:1], jnp.zeros_like(qkv_bias[:1]), qkv_bias[1:]], axis=0)
    bias_pack = jnp.concatenate([b_own.reshape(1, 3 * local), fc_bias.reshape(1, hidden)], axis=1)
    w_oth = swap_chip(w_own)
    bias_oth = swap_chip(bias_pack)
    ow_oth = swap_chip(out_weight)
    fc_oth = swap_chip(fc_weight)
    pw_oth = swap_chip(proj_weight)
    c_oth = swap_core(cotangent)

    def col(pack):
        return pack[:, : 3 * local].astype(F32).reshape(3 * local, 1)

    def fcb(pack):
        return pack[:, 3 * local :].astype(F32)

    act_bytes = rows * width * 4
    first = call(norm_first, [((rows, width), BF16)], 4, smem=1, nbytes=act_bytes)(
        tie_sets, tokens, norm_gain[0], norm_bias[0]
    )[0]
    first_oth = swap_core(first)

    block = min(256, span)
    att_flops = 2 * 2 * rows * width * 4 * local + heads * 4 * span * span * HD * 4
    saved = [((3, heads, HD, span), BF16), ((heads, 1, span), F32), ((heads, HD, span), BF16)]
    k_scr = [pltpu.VMEM((heads, span, HD), BF16)]

    def forward(first_call, w, b, ow, prev=()):
        outs = saved + [((rows, width), F32), ((rows, width), F32 if first_call else BF16)]
        return call(
            lambda *r: attn_forward(first_call, block, *r),
            outs,
            6 + len(prev),
            smem=1,
            scratch=k_scr,
            flops=att_flops,
            nbytes=8 * act_bytes,
        )(lengths, first, first_oth, w, b, ow, *prev)

    qkv_a, lse_a, att_a, br_own, br_oth = forward(True, w_own, col(bias_pack), out_weight)
    w_oth, bias_oth, ow_oth = (after(v, br_own) for v in (w_oth, bias_oth, ow_oth))
    qkv_b, lse_b, att_b, br_own, br_oth = forward(False, w_oth, col(bias_oth), ow_oth, (br_own, br_oth))
    br_in = swap_core(br_oth)
    middle, second = call(norm_second, [((rows, width), F32), ((rows, width), BF16)], 7, smem=1, nbytes=3 * act_bytes)(
        tie_sets, tokens, br_own, br_in, out_bias.astype(F32).reshape(1, width), norm_gain[1], norm_bias[1]
    )
    second_oth = swap_core(second)
    gf_a, gp_a, gfb_a, fe_own, fe_oth, ds_own, ds_oth = mlp(
        True, second, second_oth, cotangent, c_oth, fc_weight, fcb(bias_pack), proj_weight
    )
    fc_oth, pw_oth = (after(v, fe_own) for v in (fc_oth, pw_oth))
    gf_b, gp_b, gfb_b, fe_own, fe_oth, ds_own, ds_oth = mlp(
        False, second, second_oth, cotangent, c_oth, fc_oth, fcb(bias_oth), pw_oth, (fe_own, fe_oth, ds_own, ds_oth)
    )
    ds_in = swap_core(ds_oth)
    fe_in = swap_core(fe_oth)
    block_out, dmid, dlow, small_two = call(
        back_second,
        [((rows, width), BF16), ((rows, width), F32), ((rows, width), BF16), ((8, width), F32)],
        9,
        smem=1,
        nbytes=6 * act_bytes,
    )(tie_sets, middle, fe_own, fe_in, proj_bias.astype(F32).reshape(1, width), ds_own, ds_in, cotangent, norm_gain[1])
    dlow_oth = swap_core(dlow)

    def backward(first_call, qkv, lse, att, w, ow, prev=()):
        outs = [
            ((4 * local, width), BF16),
            ((8, width), F32),
            ((rows, width), F32),
            ((rows, width), F32 if first_call else BF16),
        ]
        n = pltpu.VMEM((heads, span, HD), BF16)
        tr = pltpu.VMEM((heads, HD, span), BF16)
        one = pltpu.VMEM((span, HD), BF16)
        acc = pltpu.VMEM((span, HD), F32)
        return call(
            lambda *r: attn_backward(first_call, block, *r),
            outs,
            10 + len(prev),
            smem=1,
            scratch=[n, tr, one, one, one, pltpu.VMEM((3, heads, HD, span), BF16), acc, acc],
            flops=3 * att_flops,
            nbytes=12 * act_bytes,
        )(lengths, qkv, lse, att, dlow, dlow_oth, first, first_oth, w, ow, *prev)

    gq_b, gqb_b, df_own, df_oth = backward(True, qkv_b, lse_b, att_b, w_oth, ow_oth)
    gq_a, gqb_a, df_own, df_oth = backward(False, qkv_a, lse_a, att_a, w_own, out_weight, (df_own, df_oth))
    df_in = swap_core(df_oth)
    grad_input, small_one = call(back_first, [((rows, width), BF16), ((8, width), F32)], 6, smem=1, nbytes=4 * act_bytes)(
        tie_sets, tokens, df_own, df_in, dmid, norm_gain[0]
    )
    def total(own, other):
        return lax.psum((own.astype(F32) + swap_chip(other).astype(F32)).astype(BF16), "dp")

    g_p, g_f, g_q = total(gp_a, gp_b), total(gf_a, gf_b), total(gq_a, gq_b)
    bias_a = jnp.concatenate([gqb_a[:1], gfb_a], axis=0)
    bias_b = jnp.concatenate([gqb_b[:1], gfb_b], axis=0)
    pack = jnp.concatenate(
        [
            lax.psum(jnp.concatenate([small_two, small_one], axis=0), ("dp", "tensor")),
            lax.psum(bias_a + swap_chip(bias_b), "dp"),
        ],
        axis=0,
    )
    return block_out, grad_input, g_p, g_f, g_q, pack


def body(
    tokens,
    cotangent,
    lengths,
    tie_sets,
    qkv_weight,
    qkv_bias,
    out_weight,
    out_bias,
    fc_weight,
    fc_bias,
    proj_weight,
    proj_bias,
    norm_gain,
    norm_bias,
):
    rows, width = tokens.shape
    groups = lax.axis_size("tensor")
    local = qkv_weight.shape[2]
    heads = local // HD
    hidden = fc_weight.shape[1]
    span = rows * groups // lengths.shape[0]
    assert groups == 4 and span == 2 * rows
    set_count = norm_gain.shape[1]
    dps = lax.axis_size("dp")

    if dps == 8:
        w = qkv_weight.transpose(1, 2, 0).reshape(3 * local, width)
        parts = block_call(
            lengths,
            tie_sets,
            tokens,
            cotangent,
            w,
            out_weight,
            fc_weight,
            proj_weight,
            qkv_bias,
            fc_bias,
            out_bias,
            proj_bias,
            norm_gain,
            norm_bias,
        )
        outs = finish(parts, local, set_count)
        return (*outs[:2], outs[2].reshape(3, local, width).transpose(2, 0, 1), *outs[3:])
    block_out, grad_input, g_p, g_f, g_q, pack = generic(
        tokens,
        cotangent,
        lengths,
        tie_sets,
        qkv_weight,
        qkv_bias,
        out_weight,
        out_bias,
        fc_weight,
        fc_bias,
        proj_weight,
        proj_bias,
        norm_gain,
        norm_bias,
    )
    gains = jnp.stack([pack[8 : 8 + set_count], pack[2 : 2 + set_count]])
    biases = jnp.stack([pack[8 + set_count : 8 + 2 * set_count], pack[2 + set_count : 2 + 2 * set_count]])
    gqb = pack[16, : 3 * local].reshape(3, local)
    return (
        block_out,
        grad_input,
        g_q[: 3 * local].astype(F32).reshape(3, local, width).transpose(2, 0, 1),
        jnp.stack([gqb[0], gqb[2]]),
        g_q[3 * local :].astype(F32),
        pack[0],
        g_f.astype(F32),
        pack[17],
        g_p.astype(F32),
        pack[1],
        gains,
        biases,
    )


def solution(mesh):
    in_specs = (
        P(("dp", "tensor"), None),
        P(("dp", "tensor"), None),
        P("dp"),
        P("dp"),
        P(None, None, "tensor"),
        P(None, "tensor"),
        P("tensor", None),
        P(),
        P(None, "tensor"),
        P("tensor"),
        P("tensor", None),
        P(),
        P(),
        P(),
    )
    out_specs = (
        P(("dp", "tensor"), None),
        P(("dp", "tensor"), None),
        P(None, None, "tensor"),
        P(None, "tensor"),
        P("tensor", None),
        P(),
        P(None, "tensor"),
        P("tensor"),
        P("tensor", None),
        P(),
        P(),
        P(),
    )
    return jax.shard_map(body, mesh=mesh, in_specs=in_specs, out_specs=out_specs, check_vma=False)
```

```python
import jax
import jax.numpy as jnp
from jax import lax
from jax.experimental import pallas as pl
from jax.experimental.pallas import tpu as pltpu
from jax.sharding import PartitionSpec as P

HD = 64
EPS = 1e-05
F32 = jnp.float32
BF16 = jnp.bfloat16
GELU_K = 0.7978845608028654
GELU_C = 0.044715
VMEM = pl.BlockSpec(memory_space=pltpu.VMEM)
SMEM = pl.BlockSpec(memory_space=pltpu.SMEM)
NT = (((1,), (1,)), ((), ()))
TN = (((0,), (0,)), ((), ()))


def dg(a, b, dims):
    return lax.dot_general(a, b, dims, preferred_element_type=F32)


def mm(a, b):
    return jnp.dot(a, b, preferred_element_type=F32)


def call(kernel, outs, n_in, smem=0, scratch=(), limit=48, flops=0, nbytes=0):
    return pl.pallas_call(
        kernel,
        out_shape=[jax.ShapeDtypeStruct(s, d) for s, d in outs],
        in_specs=[SMEM] * smem + [VMEM] * (n_in - smem),
        out_specs=[VMEM] * len(outs),
        scratch_shapes=list(scratch),
        cost_estimate=pl.CostEstimate(flops=flops, bytes_accessed=nbytes, transcendentals=0),
        compiler_params=pltpu.CompilerParams(vmem_limit_bytes=limit << 20),
    )


def place():
    t = lax.axis_index("tensor")
    return t % 2, t // 2


def stats(v):
    mean = jnp.mean(v, axis=-1, keepdims=True)
    cent = v - mean
    var = jnp.mean(cent * cent, axis=-1, keepdims=True)
    r = lax.rsqrt(var + EPS)
    return cent * r, r


def norm_first(sets, x, gain, bias, out):
    k = sets[place()[1]]
    xhat, _ = stats(x[...].astype(F32))
    out[...] = (xhat * gain[pl.ds(k, 1), :] + bias[pl.ds(k, 1), :]).astype(BF16)


def norm_second(sets, x, br, br_in, ob, gain, bias, middle, out):
    k = sets[place()[1]]
    mid = x[...].astype(F32) + (br[...] + br_in[...].astype(F32)) + ob[...]
    middle[...] = mid
    xhat, _ = stats(mid)
    out[...] = (xhat * gain[pl.ds(k, 1), :] + bias[pl.ds(k, 1), :]).astype(BF16)


def norm_pull(v, d, gain):
    xhat, r = stats(v)
    e = d * gain
    m1 = jnp.mean(e, axis=-1, keepdims=True)
    m2 = jnp.mean(e * xhat, axis=-1, keepdims=True)
    return r * (e - m1 - xhat * m2), jnp.sum(d * xhat, axis=0, keepdims=True), jnp.sum(d, axis=0, keepdims=True)


def split_sets(small, at, k, count, gg, gb):
    for i in range(count):
        mine = (k == i).astype(F32)
        small[at + i : at + i + 1, :] = gg * mine
        small[at + count + i : at + count + i + 1, :] = gb * mine
    end = at + 2 * count
    small[end:, :] = jnp.zeros((small.shape[0] - end, small.shape[1]), F32)


def back_second(sets, middle, feed, feed_in, pb, ds, ds_in, ct, gain, block_out, dmid, dlow, small):
    k = sets[place()[1]]
    mid = middle[...]
    block_out[...] = (mid + (feed[...] + feed_in[...].astype(F32)) + pb[...]).astype(BF16)
    d, gg, gb = norm_pull(mid, ds[...] + ds_in[...].astype(F32), gain[pl.ds(k, 1), :])
    c = ct[...].astype(F32)
    d = d + c
    dmid[...] = d
    dlow[...] = d.astype(BF16)
    small[0:1, :] = jnp.sum(d, axis=0, keepdims=True)
    small[1:2, :] = jnp.sum(c, axis=0, keepdims=True)
    split_sets(small, 2, k, gain.shape[0], gg, gb)


def back_first(sets, x, df, df_in, dmid, gain, grad_in, small):
    k = sets[place()[1]]
    d, gg, gb = norm_pull(x[...].astype(F32), df[...] + df_in[...].astype(F32), gain[pl.ds(k, 1), :])
    grad_in[...] = (d + dmid[...]).astype(BF16)
    split_sets(small, 0, k, gain.shape[0], gg, gb)


def mask_scores(scores, start, length):
    span, count = scores.shape
    kpos = lax.broadcasted_iota(jnp.int32, (span, count), 0)
    limit = jnp.minimum(start + lax.broadcasted_iota(jnp.int32, (1, count), 1), length - 1)
    return jnp.where(kpos <= limit, scores, -1e30)


def attn_forward(first_call, block, lengths, x_own, x_oth, w, b, ow, *rest):
    if first_call:
        qkv, lse, att, br_own, br_oth, k_s = rest
    else:
        pr_own, pr_oth, qkv, lse, att, br_own, br_oth, k_s = rest
    c, seq = place()
    length = lengths[seq]
    rows = x_own.shape[0]
    local = w.shape[0] // 3
    heads = local // HD
    span = 2 * rows
    parts = ((x_own, c), (x_oth, 1 - c))
    for x, p in parts:
        at = pl.ds(pl.multiple_of(p * rows, rows), rows)
        y = dg(w[...], x[...], NT) + b[...]
        for h in range(heads):
            lo = h * HD
            qkv[0, h, :, at] = (y[lo : lo + HD] * 0.125).astype(BF16)
            kt = y[local + lo : local + lo + HD]
            qkv[1, h, :, at] = kt.astype(BF16)
            k_s[h, at, :] = kt.T.astype(BF16)
            qkv[2, h, :, at] = y[2 * local + lo : 2 * local + lo + HD].astype(BF16)

    def head(h, carry):
        for i in range(span // block):
            stop = (i + 1) * block
            cols = slice(i * block, stop)
            scores = mm(k_s[h, :stop, :], qkv[0, h, :, cols])
            scores = mask_scores(scores, i * block, length)
            top = jnp.max(scores, axis=0, keepdims=True)
            e = jnp.exp(scores - top)
            total = jnp.sum(e, axis=0, keepdims=True)
            probs = (e * (1.0 / total)).astype(BF16)
            att[h, :, cols] = mm(qkv[2, h, :, :stop], probs).astype(BF16)
            lse[h, :, cols] = top + jnp.log(total)
        return carry

    lax.fori_loop(0, heads, head, 0)
    for (x, p), prev, out in zip(parts, (None, None) if first_call else (pr_own, pr_oth), (br_own, br_oth)):
        at = pl.ds(pl.multiple_of(p * rows, rows), rows)
        a = att[:, :, at].reshape(local, rows)
        r = dg(a, ow[...], TN)
        if prev is not None:
            r = r + prev[...]
        out[...] = r.astype(out.dtype)


def attn_backward(first_call, block, lengths, qkv, lse, att, d_own, d_oth, x_own, x_oth, w, ow, *rest):
    if first_call:
        gq, gb, f_own, f_oth, do_n, do_t, q_n, k_n, v_n, dqkv, dk, dv = rest
    else:
        pf_own, pf_oth, gq, gb, f_own, f_oth, do_n, do_t, q_n, k_n, v_n, dqkv, dk, dv = rest
    c, seq = place()
    length = lengths[seq]
    rows = x_own.shape[0]
    local = w.shape[0] // 3
    heads = local // HD
    span = 2 * rows
    spots = [pl.ds(pl.multiple_of(p * rows, rows), rows) for p in (c, 1 - c)]
    gout = None
    for d, at in zip((d_own, d_oth), spots):
        y = dg(ow[...], d[...], NT)
        for h in range(heads):
            part = y[h * HD : h * HD + HD]
            do_t[h, :, at] = part.astype(BF16)
            do_n[h, at, :] = part.T.astype(BF16)
        a = att[:, :, at].reshape(local, rows)
        term = mm(a, d[...])
        gout = term if gout is None else gout + term
    gq[3 * local :, :] = gout.astype(gq.dtype)

    def head(h, carry):
        q_n[...] = qkv[0, h].astype(F32).T.astype(BF16)
        k_n[...] = qkv[1, h].astype(F32).T.astype(BF16)
        v_n[...] = qkv[2, h].astype(F32).T.astype(BF16)
        for i in range(span // block):
            stop = (i + 1) * block
            cols = slice(i * block, stop)
            scores = mm(k_n[:stop, :], qkv[0, h, :, cols])
            scores = mask_scores(scores, i * block, length)
            probs = jnp.exp(scores - lse[h, :, cols])
            dp = mm(v_n[:stop, :], do_t[h, :, cols])
            total = jnp.sum(probs * dp, axis=0, keepdims=True)
            ds = (probs * (dp - total)).astype(BF16)
            dqkv[0, h, :, cols] = (mm(qkv[1, h, :, :stop], ds) * 0.125).astype(BF16)
            pv = mm(probs.astype(BF16), do_n[h, cols, :])
            pk = mm(ds, q_n[cols, :])
            last = i * block
            if i:
                dv[:last, :] += pv[:last]
                dk[:last, :] += pk[:last]
            dv[last:stop, :] = pv[last:]
            dk[last:stop, :] = pk[last:]
        dqkv[1, h] = dk[...].T.astype(BF16)
        dqkv[2, h] = dv[...].T.astype(BF16)
        return carry

    lax.fori_loop(0, heads, head, 0)
    gqkv = None
    gbias = None
    for x, at, prev, out in zip((x_own, x_oth), spots, (None, None) if first_call else (pf_own, pf_oth), (f_own, f_oth)):
        d = dqkv[:, :, :, at].reshape(3 * local, rows)
        term = mm(d, x[...])
        gqkv = term if gqkv is None else gqkv + term
        s = dg(jnp.ones((8, rows), BF16), d, NT)
        gbias = s if gbias is None else gbias + s
        r = dg(d, w[...], TN)
        if prev is not None:
            r = r + prev[...]
        out[...] = r.astype(out.dtype)
    gq[: 3 * local, :] = gqkv.astype(gq.dtype)
    gb[...] = jnp.zeros_like(gb)
    gb[:, : 3 * local] = gbias


def mlp_kernel(first_call, s_own, s_oth, c_own, c_oth, fc, fb, pw, *rest):
    if first_call:
        gf, gp, gb, fe_own, fe_oth, ds_own, ds_oth, st = rest
        prev = (None, None, None, None)
    else:
        prev = rest[:4]
        gf, gp, gb, fe_own, fe_oth, ds_own, ds_oth, st = rest[4:12]
        accs = rest[12:]
    j = pl.program_id(0)
    rows = s_own.shape[0]

    @pl.when(j == 0)
    def _():
        st[:, :rows] = s_own[...].T
        st[:, rows:] = s_oth[...].T

    gfc = gproj = gbias = None
    for n, (s, ct, fe, ds) in enumerate(((s_own, c_own, fe_own, ds_own), (s_oth, c_oth, fe_oth, ds_oth))):
        pre = mm(s[...], fc[...]) + fb[...]
        sq = pre * pre
        t = jnp.tanh(GELU_K * (pre + GELU_C * sq * pre))
        half = 0.5 * (1.0 + t)
        act = (pre * half).astype(BF16)
        slope = half + (0.5 * GELU_K) * pre * (1.0 - t * t) * (1.0 + (3.0 * GELU_C) * sq)
        dpre = dg(ct[...], pw[...], NT) * slope
        low = dpre.astype(BF16)
        bs = jnp.sum(low.astype(F32), axis=0, keepdims=True)
        tf = mm(st[:, n * rows : (n + 1) * rows], low)
        tp = dg(act, ct[...], TN)
        gfc = tf if gfc is None else gfc + tf
        gproj = tp if gproj is None else gproj + tp
        gbias = bs if gbias is None else gbias + bs
        add_f = mm(act, pw[...])
        add_s = dg(low, fc[...], NT)
        if first_call:
            fa, sa, pf, ps = fe, ds, None, None
        else:
            fa, sa = accs[2 * n], accs[2 * n + 1]
            pf, ps = prev[n], prev[2 + n]

        @pl.when(j == 0)
        def _():
            fa[...] = add_f if pf is None else add_f + pf[...]
            sa[...] = add_s if ps is None else add_s + ps[...]

        @pl.when(j > 0)
        def _():
            fa[...] += add_f
            sa[...] += add_s

        if not first_call:
            @pl.when(j == pl.num_programs(0) - 1)
            def _():
                fe[...] = fa[...].astype(fe.dtype)
                ds[...] = sa[...].astype(ds.dtype)

    gf[...] = gfc.astype(gf.dtype)
    gp[...] = gproj.astype(gp.dtype)
    gb[...] = gbias


def mlp(first_call, s_own, s_oth, c_own, c_oth, fc, fb, pw, prev=()):
    rows, width = s_own.shape
    hidden = fc.shape[1]
    hb = 256
    fixed = pl.BlockSpec((rows, width), lambda j: (0, 0))
    oth = F32 if first_call else BF16
    sums = [(rows, width)] * 4
    scratch = [pltpu.VMEM((width, 2 * rows), BF16)]
    if not first_call:
        scratch += [pltpu.VMEM(s, F32) for s in sums]
    return pl.pallas_call(
        lambda *r: mlp_kernel(first_call, *r),
        grid=(hidden // hb,),
        in_specs=[fixed] * 4
        + [
            pl.BlockSpec((width, hb), lambda j: (0, j)),
            pl.BlockSpec((1, hb), lambda j: (0, j)),
            pl.BlockSpec((hb, width), lambda j: (j, 0)),
        ]
        + [fixed] * len(prev),
        out_specs=[
            pl.BlockSpec((width, hb), lambda j: (0, j)),
            pl.BlockSpec((hb, width), lambda j: (j, 0)),
            pl.BlockSpec((1, hb), lambda j: (0, j)),
        ]
        + [fixed] * 4,
        out_shape=[
            jax.ShapeDtypeStruct((width, hidden), BF16),
            jax.ShapeDtypeStruct((hidden, width), BF16),
            jax.ShapeDtypeStruct((1, hidden), F32),
            jax.ShapeDtypeStruct((rows, width), F32),
            jax.ShapeDtypeStruct((rows, width), oth),
            jax.ShapeDtypeStruct((rows, width), F32),
            jax.ShapeDtypeStruct((rows, width), oth),
        ],
        scratch_shapes=scratch,
        cost_estimate=pl.CostEstimate(flops=24 * rows * width * hidden, bytes_accessed=20 * rows * width, transcendentals=0),
        compiler_params=pltpu.CompilerParams(vmem_limit_bytes=56 << 20),
    )(s_own, s_oth, c_own, c_oth, fc, fb, pw, *prev)


def partners():
    t, d = lax.axis_index("tensor"), lax.axis_index("dp")
    bits = {"x": d % 2, "1": (d // 2) % 2, "2": d // 4}
    to = {
        "c": {"tensor": t + 1 - 2 * (t % 2)},
        "y": {"tensor": (t + 2) % 4},
        "x": {"dp": d + 1 - 2 * bits["x"]},
        "1": {"dp": d + 2 - 4 * bits["1"]},
        "2": {"dp": (d + 4) % 8},
        "3": {"dp": (d + 4) % 8 + 2 - 4 * bits["1"]},
    }
    return to, bits


def remote(src, dst, send, recv, where):
    return pltpu.make_async_remote_copy(
        src_ref=src, dst_ref=dst, send_sem=send, recv_sem=recv, device_id=where, device_id_type=pl.DeviceIdType.MESH
    )


def aligned(start, n, by=16):
    return pl.ds(pl.multiple_of(start, by), n)


class Flow:
    def __init__(self, own, oth, res, buf, outs, order, to, bits, sems):
        self.acts, self.outs = [], [pltpu.make_async_copy(res.at[src], out, sems(None)) for src, out in outs]
        base, n, at, both = 0, own.shape[0], 0, True
        back, waits, adds, slot = [], [], [], 0
        for k, o in enumerate(order):
            copies, sums = [], []
            last = k == len(order) - 1
            if o == "y":
                here = aligned(base, n)
                got = buf.at[aligned(at, n)]
                at += n
                copies.append(remote(oth.at[here], got, *sems(slot), to[o]))
                sums.append(((res if last else own).at[here], own.at[here], [got]))
                slot += 1
                both = False
            elif o == "e":
                here = aligned(base, n)
                got = buf.at[aligned(at, n)]
                copies.append(remote(own.at[here], got, *sems(slot), to["2"]))
                sums.append((res.at[here], own.at[here], [got]))
                slot += 1
            else:
                size = n // 4 if o == "Z" else n // 2
                back.append((o, base, size))
                mine = bits["1"] + 2 * bits["2"] if o == "Z" else bits[o]
                keep = aligned(base + mine * size, size)
                for ref in (own, oth) if both else (own,):
                    gots = []
                    for peer in "123" if o == "Z" else o:
                        other = zs(bits, peer) if o == "Z" else 1 - mine
                        got = buf.at[aligned(at, size)]
                        at += size
                        copies.append(remote(ref.at[aligned(base + other * size, size)], got, *sems(slot), to[peer]))
                        gots.append(got)
                        slot += 1
                    sums.append(((res if last else ref).at[keep], ref.at[keep], gots))
                base, n = base + mine * size, size
            if k == 0 and both:
                self.acts += [([], [], copies[:1]), ([], [], copies[1:])]
            else:
                self.acts.append((waits, adds, copies))
            waits, adds = copies, sums
        for o, start, size in reversed(back):
            here = res.at[aligned(base, n)]
            copies = []
            for peer in "123" if o == "Z" else o:
                copies.append(remote(here, here, *sems(slot), to[peer]))
                slot += 1
            self.acts.append((waits, adds, copies))
            waits, adds = copies, []
            base, n = start, size * (4 if o == "Z" else 2)
        self.acts.append((waits, adds, self.outs))

    def step(self, k):
        waits, adds, starts = self.acts[k]
        for copy in waits:
            copy.wait()
        for dst, mine, gots in adds:
            total = mine[...].astype(F32)
            for got in gots:
                total = total + got[...].astype(F32)
            dst[...] = total.astype(BF16)
        for copy in starts:
            copy.start()


def zs(bits, peer):
    one = 1 - bits["1"] if peer in "13" else bits["1"]
    two = 1 - bits["2"] if peer in "23" else bits["2"]
    return one + 2 * two


def pick(gains, chosen):
    row = gains[0:1, :]
    for i in range(1, gains.shape[0]):
        row = jnp.where(chosen == i, gains[i : i + 1, :], row)
    return row


def block_kernel(*refs):
    (lengths, sets, tok_h, ct_h, w_h, ow_h, fc_h, pw_h, qkv_b, fc_b, ob, pb, gains, biases) = refs[:14]
    block_out, grad_in, o_p, o_f, o_q, o_o, pack = refs[14:21]
    (tok, ct, ct_oth, first, first_oth, w, ow, fc, pw, bias, qkv, lse, att, nat, trn) = refs[21:36]
    (give, fe_send, br_in, middle, second, second_oth, st, acc, ds_in, fe_in) = refs[36:46]
    (dlow_oth, q_n, k_n, v_n, dqkv, dk, dv, df_in, q_t) = refs[46:55]
    (grad, res, buf, fbg, r_pack, load, sends, recvs, wsend, wrecv, done) = refs[55:]
    dlow = second
    block, wide = 256, 512
    to, bits = partners()
    c, seq = place()
    length, chosen = lengths[seq], sets[seq]
    rows, width = tok.shape
    local = ow.shape[1]
    heads = local // HD
    span = 2 * rows
    hidden = fc.shape[2]
    blocks = hidden // block
    spots = [pl.ds(pl.multiple_of(p * rows, rows), rows) for p in (c, 1 - c)]

    loads = {}
    for name, src, dst in (
        ("tok", tok_h, tok),
        ("w", w_h, w.at[0]),
        ("ow", ow_h, ow.at[0]),
        ("ct", ct_h, ct),
        ("fc", fc_h, fc.at[0]),
        ("pw", pw_h, pw.at[0]),
    ):
        loads[name] = pltpu.make_async_copy(src, dst, load.at[len(loads)])
        loads[name].start()

    barrier = pltpu.get_barrier_semaphore()
    for where in to.values():
        pl.semaphore_signal(barrier, inc=1, device_id=where, device_id_type=pl.DeviceIdType.MESH)
    pl.semaphore_wait(barrier, len(to))

    bias[0] = jnp.zeros(bias.shape[1:], BF16)
    edge = hidden + 256
    bias[0, 0:1, :hidden] = fc_b[...].reshape(1, hidden)
    bias[0, 0:1, hidden : hidden + local] = qkv_b[0:1, :]
    bias[0, 0:1, edge : edge + local] = qkv_b[1:2, :]
    bias_copy = remote(bias.at[0], bias.at[1], wsend.at[0], wrecv.at[0], to["y"])
    pieces = []
    for src, dst, start, n in (
        (w_h, w, 0, local),
        (w_h, w, local, local),
        (w_h, w, 2 * local, local),
        (ow_h, ow, 0, local),
        (fc_h, fc, 0, width // 2),
        (fc_h, fc, width // 2, width // 2),
        (pw_h, pw, 0, hidden // 2),
        (pw_h, pw, hidden // 2, hidden // 2),
    ):
        k = 1 + 4 * len(pieces)
        first_way, last_way = ("1", "x") if len(pieces) % 2 else ("x", "1")

        def quarter(x, z, start=start, n=n):
            return aligned(start + (2 * z + x) * (n // 4), n // 4, 8)

        mine = quarter(bits["x"], bits["1"])
        there = dst.at[1, mine]
        got = quarter(1 - bits["x"], bits["1"]) if first_way == "x" else quarter(bits["x"], 1 - bits["1"])
        over = remote(src.at[mine], there, wsend.at[k], wrecv.at[k], to["y"])
        one = remote(there, there, wsend.at[k + 1], wrecv.at[k + 1], to[first_way])
        two = remote(there, there, wsend.at[k + 2], wrecv.at[k + 2], to[last_way])
        rest = remote(dst.at[1, got], dst.at[1, got], wsend.at[k + 3], wrecv.at[k + 3], to[last_way])
        pieces.append((over, [one, two], [one], [rest], [two, rest]))
    bias_copy.start()
    for over, *_ in pieces:
        over.start()

    def forward(acts):
        for i, act in acts:
            over, on, waits, starts, ends = pieces[i]
            if act == 0:
                waits, starts = [over], on
            elif act == 2:
                waits, starts = ends, []
            for copy in waits:
                copy.wait()
            for copy in starts:
                copy.start()

    flows = []
    n_flow = 9
    for f in range(n_flow):
        unit, j = f // 3, f % 3
        part = (slice(None), slice(j * block, (j + 1) * block)) if unit == 1 else (slice(j * block, (j + 1) * block),)
        if unit < 2:
            outs = [((slice(None),), (o_p, o_f)[unit].at[part])]
        else:
            outs = [((slice(n * HD, (n + 1) * HD),), o_q.at[pl.ds(n * local + j * HD, HD)]) for n in range(3)]
            outs.append(((slice(3 * HD, 4 * HD),), o_o.at[pl.ds(j * HD, HD)]))
        room = (slice(None), part[1]) if unit == 1 else (slice(j * 2 * block, (j + 1) * 2 * block),)

        def sems(k, f=f):
            return done.at[f] if k is None else (sends.at[f, k], recvs.at[f, k])

        flows.append(
            Flow(
                grad.at[(0, unit, *part)],
                grad.at[(1, unit, *part)],
                res.at[(unit, *part)],
                buf.at[(unit, *room)],
                outs,
                ORDERS[f],
                to,
                bits,
                sems,
            )
        )

    def swap(n, src, dst):
        return remote(src, dst, sends.at[n_flow, n], recvs.at[n_flow, n], to["c"])

    small_order = "cyx12"
    small_copies = [
        remote(pack, r_pack.at[n], sends.at[n_flow + 1, n], recvs.at[n_flow + 1, n], to[o]) for n, o in enumerate(small_order)
    ]

    def small(n):
        if n:
            small_copies[n - 1].wait()
            got = r_pack[n - 1]
            mid = pack[16:24, :]
            if n == 2:
                mid = mid + got[24:]
            elif n > 2:
                mid = mid + got[16:24]
            pack[:16, :] = pack[:16, :] + got[:16]
            pack[16:24, :] = mid
        if n < len(small_order):
            small_copies[n].start()

    def run(events):
        for f, k in events:
            if f < 0:
                small(k)
            else:
                flows[f].step(k)

    def at_step(i, table, what):
        for n, some in enumerate(table):
            if some:

                @pl.when(i == n)
                def _():
                    what(some)

    tile = 256

    def by_rows(step, carry=0, copies=()):
        def one(i, held):
            held = step(pl.multiple_of(i * tile, tile), held)
            for n, copy in enumerate(copies):
                pl.when(i == n)(copy.start)
            return held

        return lax.fori_loop(0, rows // tile, one, carry)

    def swap_tiles(n, src, dst):
        parts = [pl.ds(t * tile, tile) for t in range(rows // tile)]
        pairs = [(sends.at[n_flow, n + 8 * t], recvs.at[n_flow, n + 8 * t]) for t in range(len(parts))]
        return [remote(src.at[r], dst.at[r], *pair, to["c"]) for r, pair in zip(parts, pairs)]

    def wait_all(copies):
        for copy in copies:
            copy.wait()

    def norm(n, v):
        return (stats(v)[0] * pick(gains[n], chosen) + pick(biases[n], chosen)).astype(BF16)

    zero = jnp.zeros((1, width), F32)

    loads["tok"].wait()

    def norm_tokens(r, carry):
        r = pl.ds(r, tile)
        first[r] = norm(0, tok[r].astype(F32))
        return carry

    first_swap = swap_tiles(0, first, first_oth)
    by_rows(norm_tokens, copies=first_swap)
    loads["ct"].wait()
    ct_swap = swap(1, ct, ct_oth)
    ct_swap.start()
    loads["w"].wait()

    q_t[HD:, :] = (lax.broadcasted_iota(jnp.int32, (HD, span), 0) == 0).astype(BF16)
    true_key = lax.broadcasted_iota(jnp.int32, (span, HD), 0) < length
    key_lane = lax.broadcasted_iota(jnp.int32, (span, HD), 1) == 0
    key_mask = jnp.where(true_key, 0.0, jnp.where(key_lane, -1e30, 0.0)).astype(BF16)
    for h in range(heads):
        nat[0, h, :, HD:] = key_mask
    k_n[:, HD:] = key_mask
    later = lax.broadcasted_iota(jnp.int32, (wide, wide), 0) > lax.broadcasted_iota(jnp.int32, (wide, wide), 1)

    def scores(keys, last, stop):
        cols = slice(last, stop)
        same = jnp.where(later, -1e30, mm(keys(cols), q_t[:, cols]))
        return [mm(keys(slice(0, last)), q_t[:, cols]), same] if last else [same]

    pick_row = (lax.broadcasted_iota(jnp.int32, (16, rows), 0) == 0).astype(BF16)

    def attend(s, carry):
        @pl.when(s == 1)
        def _():
            forward(FORWARD_SECOND)
            bias_copy.wait()

        q_col = dg(bias[s, :, hidden : hidden + local], pick_row, TN)
        v_col = dg(bias[s, :, edge : edge + local], pick_row, TN)
        for n, (x, at) in enumerate(zip((first, first_oth), spots)):
            if n:

                @pl.when(s == 0)
                def _():
                    wait_all(first_swap)

            y = dg(w[s], x[...], NT)
            for h in range(heads):
                lo = h * HD
                qkv[s, 0, h, :, at] = ((y[lo : lo + HD] + q_col[lo : lo + HD]) * 0.125).astype(BF16)
                kt = y[local + lo : local + lo + HD]
                qkv[s, 1, h, :, at] = kt.astype(BF16)
                nat[0, h, at, :HD] = kt.T.astype(BF16)
                vt = y[2 * local + lo : 2 * local + lo + HD]
                qkv[s, 2, h, :, at] = (vt + v_col[lo : lo + HD]).astype(BF16)
            at_step(s, FORWARD_ROWS[n], forward)

        def head(h, carry):
            q_t[:HD, :] = qkv[s, 0, h]
            for i in range(span // wide):
                last, stop = i * wide, (i + 1) * wide
                cols = slice(last, stop)
                parts = scores(lambda rows: nat[0, h, rows, :], last, stop)
                top = parts[-1].max(axis=0, keepdims=True)
                if i:
                    top = jnp.maximum(top, parts[0].max(axis=0, keepdims=True))
                total = out = None
                for v, keys in zip(parts, (slice(0, last), cols) if i else (cols,)):
                    e = jnp.exp(v - top)
                    add = jnp.sum(e, axis=0, keepdims=True)
                    term = mm(qkv[s, 2, h, :, keys], e.astype(BF16))
                    total = add if total is None else total + add
                    out = term if out is None else out + term
                att[s, h, :, cols] = (out * (1.0 / total)).astype(BF16)
                lse[s, h, :, cols] = top + jnp.log(total)
            at_step(s * heads + h, FORWARD_HEADS, forward)
            return carry

        lax.fori_loop(0, heads, head, 0)
        return carry

    lax.fori_loop(0, 2, attend, 0)
    loads["ow"].wait()
    forward(FORWARD_PROJECT)

    def project(p, r):
        at = pl.ds(pl.multiple_of(p * rows + r, tile), tile)
        return dg(att[0, :, :, at].reshape(local, tile), ow[0], TN) + dg(att[1, :, :, at].reshape(local, tile), ow[1], TN)

    def project_other(r, carry):
        give[pl.ds(r, tile)] = project(1 - c, r).astype(BF16)
        return carry

    br_swap = swap_tiles(2, give, br_in)
    by_rows(project_other, copies=br_swap)

    def project_own(r, carry):
        middle[pl.ds(r, tile)] = tok[pl.ds(r, tile)].astype(F32) + ob[...].astype(F32).reshape(1, width) + project(c, r)
        return carry

    by_rows(project_own)
    forward(FORWARD_MIDDLE)
    wait_all(br_swap)

    def norm_middle(r, carry):
        r = pl.ds(r, tile)
        mid = middle[r] + br_in[r].astype(F32)
        middle[r] = mid
        second[r] = norm(1, mid)
        return carry

    second_swap = swap_tiles(3, second, second_oth)
    by_rows(norm_middle, copies=second_swap)
    forward(FORWARD_NORM)
    st[:, :rows] = second[...].T
    loads["fc"].wait()
    loads["pw"].wait()

    ds_swap, fe_swap = swap(4, give, ds_in), swap(5, fe_send, fe_in)
    halves = ((second, ct), (second_oth, ct_oth))

    def units(jj, carry, turn=(1, 0)):
        s, j = jj // blocks, jj % blocks
        here = pl.ds(pl.multiple_of(j * block, block), block)

        @pl.when(jj == blocks)
        def _():
            forward(FORWARD_OTHER)

        gfc = gproj = gbias = None
        for n in turn:
            x, g = halves[n]
            if turn == (0, 1) and n:
                ct_swap.wait()
                wait_all(second_swap)
                st[:, rows:] = second_oth[...].T
            pre = mm(x[...], fc[s, :, here]) + bias[s, 0:1, here].astype(F32)
            sq = pre * pre
            t = jnp.tanh(pre * (GELU_K + (GELU_K * GELU_C) * sq))
            half = 0.5 + 0.5 * t
            full = pre * half
            act = full.astype(BF16)
            slope = half + full * (1.0 - t) * (GELU_K + (3.0 * GELU_K * GELU_C) * sq)
            low = (dg(g[...], pw[s, here, :], NT) * slope).astype(BF16)
            bs = jnp.sum(low.astype(F32), axis=0, keepdims=True)
            tf = mm(st[:, n * rows : (n + 1) * rows], low)
            tp = dg(act, g[...], TN)
            gfc = tf if gfc is None else gfc + tf
            gproj = tp if gproj is None else gproj + tp
            gbias = bs if gbias is None else gbias + bs
            add_f = mm(act, pw[s, here, :])
            add_s = dg(low, fc[s, :, here], NT)

            if turn == (0, 1):
                acc[n] = add_f
                acc[2 + n] = add_s
            else:
                acc[n] += add_f
                acc[2 + n] += add_s
            if n == 1:

                @pl.when(jj == 2 * blocks - 1)
                def _():
                    give[...] = acc[3].astype(BF16)
                    ds_swap.start()
                    fe_send[...] = acc[1].astype(BF16)
                    fe_swap.start()

            if n == turn[0]:
                at_step(jj, FORWARD_UNITS_MID, forward)
                at_step(jj, UNITS_MID, run)

        grad[s, 1, :, here] = gfc.astype(BF16)
        grad[s, 0, here, :] = gproj.astype(BF16)
        fbg[s, 0:1, here] = gbias
        at_step(jj, FORWARD_UNITS, forward)
        at_step(jj, UNITS, run)
        return carry

    units(0, 0, (0, 1))
    lax.fori_loop(1, 2 * blocks, units, 0)
    run(AFTER_UNITS)
    ds_swap.wait()
    fe_swap.wait()

    def back_middle(r, held):
        r = pl.ds(r, tile)
        mid, cot = middle[r], ct[r].astype(F32)
        block_out[r] = (mid + (acc[0, r] + fe_in[r].astype(F32)) + pb[...].astype(F32).reshape(1, width)).astype(BF16)
        d, gg, gb = norm_pull(mid, acc[2, r] + ds_in[r].astype(F32), pick(gains[1], chosen))
        d = d + cot
        middle[r] = d
        dlow[r] = d.astype(BF16)
        new = (jnp.sum(d, axis=0, keepdims=True), jnp.sum(cot, axis=0, keepdims=True), gg, gb)
        return tuple(a + b for a, b in zip(held, new))

    low_swap = swap_tiles(6, dlow, dlow_oth)
    sums = by_rows(back_middle, (zero,) * 4, low_swap)
    pack[0:1, :] = sums[0]
    pack[1:2, :] = sums[1]
    split_sets(pack.at[0:8], 2, chosen, gains.shape[1], sums[2], sums[3])
    run(AFTER_SECOND)

    for n, (g, at) in enumerate(zip((dlow, dlow_oth), spots)):
        if n:
            wait_all(low_swap)
        for s in range(2):
            y = dg(ow[s], g[...], NT)
            for h in range(heads):
                piece = y[h * HD : h * HD + HD]
                trn[s, h, :, at] = piece.astype(BF16)
                nat[s, h, at, :HD] = piece.T.astype(BF16)

    def pull(i, carry):
        s = h = 0
        for n, (shard, which) in enumerate(HEAD_ORDER):
            s, h = jnp.where(i == n, shard, s), jnp.where(i == n, which, h)
        q_t[:HD, :] = qkv[s, 0, h]
        q_n[...] = qkv[s, 0, h].astype(F32).T.astype(BF16)
        k_n[:, :HD] = qkv[s, 1, h].astype(F32).T.astype(BF16)
        v_n[...] = qkv[s, 2, h].astype(F32).T.astype(BF16)
        for b in range(span // wide):
            last, stop = b * wide, (b + 1) * wide
            cols = slice(last, stop)
            parts = scores(lambda rows: k_n[rows, :], last, stop)
            total = jnp.sum(att[s, h, :, cols].astype(F32) * trn[s, h, :, cols].astype(F32), axis=0, keepdims=True)
            dq = None
            for v, keys in zip(parts, (slice(0, last), cols) if b else (cols,)):
                probs = jnp.exp(v - lse[s, h, :, cols])
                ds = (probs * (mm(v_n[keys, :], trn[s, h, :, cols]) - total)).astype(BF16)
                term = mm(qkv[s, 1, h, :, keys], ds)
                dq = term if dq is None else dq + term
                pv = mm(probs.astype(BF16), nat[s, h, cols, :HD])
                pk = mm(ds, q_n[cols, :])
                if keys.stop == stop:
                    dv[keys, :] = pv
                    dk[keys, :] = pk
                else:
                    dv[keys, :] += pv
                    dk[keys, :] += pk
            dqkv[s, 0, h, :, cols] = (dq * 0.125).astype(BF16)
            if stop < span:
                at_step(i, HEADS[b], run)
        dqkv[s, 1, h] = dk[...].T.astype(BF16)
        dqkv[s, 2, h] = dv[...].T.astype(BF16)
        gq = go = None
        for x, g, at in zip((first, first_oth), (dlow, dlow_oth), spots):
            tq = mm(dqkv[s, :, h, :, at].reshape(3 * HD, rows), x[...])
            to_ = mm(att[s, h, :, at], g[...])
            gq = tq if gq is None else gq + tq
            go = to_ if go is None else go + to_
        top = pl.multiple_of(h * 4 * HD, 4 * HD)
        grad[s, 2, pl.ds(top, 3 * HD), :] = gq.astype(BF16)
        grad[s, 2, pl.ds(top + 3 * HD, HD), :] = go.astype(BF16)
        at_step(i, HEADS[-1], run)
        return carry

    lax.fori_loop(0, 2 * heads, pull, 0)

    def pull_first(p, r):
        at = pl.ds(pl.multiple_of(p * rows + r, tile), tile)
        return dg(dqkv[0, :, :, :, at].reshape(3 * local, tile), w[0], TN) + dg(
            dqkv[1, :, :, :, at].reshape(3 * local, tile), w[1], TN
        )

    def pull_other(r, carry):
        give[pl.ds(r, tile)] = pull_first(1 - c, r).astype(BF16)
        return carry

    df_swap = swap_tiles(7, give, df_in)
    by_rows(pull_other, copies=df_swap)
    run(AFTER_HEADS)

    def pull_own(r, carry):
        acc[0, pl.ds(r, tile)] = pull_first(c, r)
        return carry

    by_rows(pull_own)
    wait_all(df_swap)

    def back_tokens(r, held):
        r = pl.ds(r, tile)
        d, gg, gb = norm_pull(tok[r].astype(F32), acc[0, r] + df_in[r].astype(F32), pick(gains[0], chosen))
        grad_in[r] = (d + middle[r]).astype(BF16)
        return (held[0] + gg, held[1] + gb)

    sums = by_rows(back_tokens, (zero,) * 2)
    split_sets(pack.at[8:16], 0, chosen, gains.shape[1], sums[0], sums[1])
    for s in range(2):
        at = 16 + 8 * s
        pack[at : at + 8, :] = jnp.zeros((8, width), F32)
        pack[at : at + 1, : 3 * local] = dg(jnp.ones((8, span), BF16), dqkv[s].reshape(3 * local, span), NT)[0:1]
        pack[at + 1 : at + 2, :] = fbg[s, 0:1]
    run(TAIL)
    for flow in flows:
        for out in flow.outs:
            out.wait()


FORWARD_ROWS = ([[(0, 0)], []], [[(1, 0), (2, 0), (0, 1)], [(3, 1), (5, 0)]])
FORWARD_HEADS = ([(1, 1)], [(2, 1), (3, 0), (4, 0)], [(1, 2)], [], [(6, 0)], [(3, 2)])
FORWARD_SECOND = [(0, 2), (2, 2)]
FORWARD_PROJECT = []
FORWARD_MIDDLE = [(7, 0), (4, 1), (5, 1)]
FORWARD_NORM = []
FORWARD_OTHER = [(7, 2)]
FORWARD_UNITS_MID = ([(6, 1)], [], [(5, 2), (4, 2), (6, 2)])
FORWARD_UNITS = ([(7, 1)], [], [])
HEAD_ORDER = ((1, 0), (1, 1), (0, 0), (1, 2), (0, 1), (0, 2))
ORDERS = ("x1ye", "xy1e", "1xye", "yx1e", "1xye", "x1ye", "yx1e", "yx1e", "yx1e")
UNITS_MID = (
    [],
    [],
    [(1, 0)],
    [],
    [],
    [(5, 0)],
)
UNITS = (
    [(0, 0)],
    [(4, 0)],
    [(2, 0)],
    [(0, 1), (3, 0)],
    [(1, 1), (4, 1)],
    [],
)
AFTER_UNITS = [
    (0, 2), (2, 1),
]
AFTER_SECOND = [
    (1, 2), (5, 1), (3, 1),
]
HEADS = (
    (
        [(0, 3)],
        [(1, 3), (4, 2), (5, 2)],
        [],
        [],
        [(3, 3)],
        [(6, 2), (7, 1)],
    ),
    (
        [(6, 0)],
        [(7, 0), (0, 4), (2, 2)],
        [(3, 2), (1, 4)],
        [(6, 1), (5, 3), (0, 5), (8, 0)],
        [(0, 6), (1, 5)],
        [(5, 4)],
    ),
)
AFTER_HEADS = [
    (2, 3), (1, 6), (3, 4), (6, 3),
]
TAIL = [
    (-1, 0), (7, 2), (4, 3), (0, 7), (8, 1), (-1, 1), (2, 4), (3, 5), (1, 7), (6, 4), (4, 4), (8, 2), (-1, 2),
    (6, 5), (7, 3), (5, 5), (3, 6), (8, 3), (4, 5), (2, 5), (-1, 3), (5, 6), (7, 4), (6, 6), (8, 4), (-1, 4), (4, 6),
    (2, 6), (7, 5), (8, 5), (5, 7), (7, 6), (-1, 5), (4, 7), (8, 6), (2, 7),
]


def block_call(lengths, sets, tok, ct, w, ow, fc, pw, qkv_b, fc_b, ob, pb, gains, biases):
    rows, width = tok.shape
    local, hidden = ow.shape[0], fc.shape[1]
    heads, span = local // HD, 2 * rows
    total = 4 * local
    assert total == width == hidden
    any_spec = pl.BlockSpec(memory_space=pl.ANY)

    def v(*shape, dtype=BF16):
        return pltpu.VMEM(shape, dtype)

    act, wide = v(rows, width), v(rows, width, dtype=F32)
    one, one_acc = v(span, HD), v(span, HD, dtype=F32)
    dma = pltpu.SemaphoreType.DMA
    scratch = [act, act, act, act, act]
    scratch += [v(2, 3 * local, width), v(2, local, width), v(2, width, hidden), v(2, hidden, width), v(2, 16, hidden + 512)]
    scratch += [v(2, 3, heads, HD, span), v(2, heads, 1, span, dtype=F32), v(2, heads, HD, span), v(2, heads, span, 2 * HD), v(2, heads, HD, span)]
    scratch += [act, act, act, wide, act, act, v(width, span), v(4, rows, width, dtype=F32), act, act]
    scratch += [act, one, v(span, 2 * HD), one, v(2, 3, heads, HD, span), one_acc, one_acc, act, v(2 * HD, span)]
    scratch += [v(2, 3, total, width), v(3, total, width), v(3, 2 * total, width), v(2, 8, hidden, dtype=F32), v(5, 32, width, dtype=F32)]
    scratch += [dma((7,)), dma((11, 16)), dma((11, 16)), dma((33,)), dma((33,)), dma((9,))]
    shapes = [(rows, width)] * 2 + [(total, width)] * 2 + [(3 * local, width), (local, width)]
    return pl.pallas_call(
        block_kernel,
        out_shape=[jax.ShapeDtypeStruct(s, BF16) for s in shapes] + [jax.ShapeDtypeStruct((32, width), F32)],
        in_specs=[SMEM] * 2 + [any_spec] * 6 + [VMEM] * 6,
        out_specs=[VMEM] * 2 + [any_spec] * 4 + [VMEM],
        scratch_shapes=scratch,
        compiler_params=pltpu.CompilerParams(vmem_limit_bytes=63 << 20, collective_id=1, has_side_effects=True),
    )(lengths, sets, tok, ct, w, ow, fc, pw, qkv_b, fc_b, ob, pb, gains, biases)


def finish_kernel(b, g, p, f, q, o, pack, block_out, grad_in, gq, gqb, go, gob, gf, gfb, gp, gpb, gains, biases):
    block_out[...] = b[...]
    grad_in[...] = g[...]
    for src, dst in ((p, gp), (f, gf), (q, gq), (o, go)):
        dst[...] = src[...].astype(F32)

    @pl.when(pl.program_id(0) == 0)
    def _():
        local = gqb.shape[1]
        count = gains.shape[1]
        gqb[0:1, :] = pack[16:17, :local]
        gqb[1:2, :] = pack[16:17, 2 * local : 3 * local]
        for row, dst in ((0, gob), (1, gpb), (17, gfb)):
            dst[...] = pack[row : row + 1, :].reshape(dst.shape)
        for n, at in ((0, 8), (1, 2)):
            gains[n] = pack[at : at + count, :]
            biases[n] = pack[at + count : at + 2 * count, :]


def finish(parts, local, count):
    rows, width = parts[0].shape
    steps = 2

    def spec(array):
        return pl.BlockSpec((array.shape[0] // steps, width), lambda i: (i, 0))

    def whole(*shape):
        return pl.BlockSpec(shape, lambda i: (0,) * len(shape))

    b, g, p, f, q, o, pack = parts
    sets = (2, count, width)
    small = [(2, local), (width,), (p.shape[0],), (width,), sets, sets]
    order = [(b, BF16), (g, BF16), (q, F32), small[0], (o, F32), small[1], (f, F32), small[2], (p, F32)] + small[3:]
    big = [isinstance(v[0], jax.Array) for v in order]
    return pl.pallas_call(
        finish_kernel,
        grid=(steps,),
        in_specs=[spec(v) for v in parts[:6]] + [whole(*pack.shape)],
        out_specs=[spec(v[0]) if k else whole(*v) for v, k in zip(order, big)],
        out_shape=[jax.ShapeDtypeStruct(*((v[0].shape, v[1]) if k else (v, F32))) for v, k in zip(order, big)],
    )(*parts)


def generic(tokens, cotangent, lengths, tie_sets, qkv_weight, qkv_bias, out_weight, out_bias, fc_weight, fc_bias, proj_weight, proj_bias, norm_gain, norm_bias):
    rows, width = tokens.shape
    local = qkv_weight.shape[2]
    heads = local // HD
    hidden = fc_weight.shape[1]
    span = 2 * rows

    def swap_core(v):
        return lax.ppermute(v, "tensor", [(i, i ^ 1) for i in range(4)])

    def swap_chip(v):
        return lax.ppermute(v, "tensor", [(i, i ^ 2) for i in range(4)])

    def after(v, *first):
        return lax.optimization_barrier((v, *first))[0]

    w_own = qkv_weight.transpose(1, 2, 0).reshape(3 * local, width)
    b_own = jnp.concatenate([qkv_bias[:1], jnp.zeros_like(qkv_bias[:1]), qkv_bias[1:]], axis=0)
    bias_pack = jnp.concatenate([b_own.reshape(1, 3 * local), fc_bias.reshape(1, hidden)], axis=1)
    w_oth = swap_chip(w_own)
    bias_oth = swap_chip(bias_pack)
    ow_oth = swap_chip(out_weight)
    fc_oth = swap_chip(fc_weight)
    pw_oth = swap_chip(proj_weight)
    c_oth = swap_core(cotangent)

    def col(pack):
        return pack[:, : 3 * local].astype(F32).reshape(3 * local, 1)

    def fcb(pack):
        return pack[:, 3 * local :].astype(F32)

    act_bytes = rows * width * 4
    first = call(norm_first, [((rows, width), BF16)], 4, smem=1, nbytes=act_bytes)(
        tie_sets, tokens, norm_gain[0], norm_bias[0]
    )[0]
    first_oth = swap_core(first)

    block = min(256, span)
    att_flops = 2 * 2 * rows * width * 4 * local + heads * 4 * span * span * HD * 4
    saved = [((3, heads, HD, span), BF16), ((heads, 1, span), F32), ((heads, HD, span), BF16)]
    k_scr = [pltpu.VMEM((heads, span, HD), BF16)]

    def forward(first_call, w, b, ow, prev=()):
        outs = saved + [((rows, width), F32), ((rows, width), F32 if first_call else BF16)]
        return call(
            lambda *r: attn_forward(first_call, block, *r),
            outs,
            6 + len(prev),
            smem=1,
            scratch=k_scr,
            flops=att_flops,
            nbytes=8 * act_bytes,
        )(lengths, first, first_oth, w, b, ow, *prev)

    qkv_a, lse_a, att_a, br_own, br_oth = forward(True, w_own, col(bias_pack), out_weight)
    w_oth, bias_oth, ow_oth = (after(v, br_own) for v in (w_oth, bias_oth, ow_oth))
    qkv_b, lse_b, att_b, br_own, br_oth = forward(False, w_oth, col(bias_oth), ow_oth, (br_own, br_oth))
    br_in = swap_core(br_oth)
    middle, second = call(norm_second, [((rows, width), F32), ((rows, width), BF16)], 7, smem=1, nbytes=3 * act_bytes)(
        tie_sets, tokens, br_own, br_in, out_bias.astype(F32).reshape(1, width), norm_gain[1], norm_bias[1]
    )
    second_oth = swap_core(second)
    gf_a, gp_a, gfb_a, fe_own, fe_oth, ds_own, ds_oth = mlp(
        True, second, second_oth, cotangent, c_oth, fc_weight, fcb(bias_pack), proj_weight
    )
    fc_oth, pw_oth = (after(v, fe_own) for v in (fc_oth, pw_oth))
    gf_b, gp_b, gfb_b, fe_own, fe_oth, ds_own, ds_oth = mlp(
        False, second, second_oth, cotangent, c_oth, fc_oth, fcb(bias_oth), pw_oth, (fe_own, fe_oth, ds_own, ds_oth)
    )
    ds_in = swap_core(ds_oth)
    fe_in = swap_core(fe_oth)
    block_out, dmid, dlow, small_two = call(
        back_second,
        [((rows, width), BF16), ((rows, width), F32), ((rows, width), BF16), ((8, width), F32)],
        9,
        smem=1,
        nbytes=6 * act_bytes,
    )(tie_sets, middle, fe_own, fe_in, proj_bias.astype(F32).reshape(1, width), ds_own, ds_in, cotangent, norm_gain[1])
    dlow_oth = swap_core(dlow)

    def backward(first_call, qkv, lse, att, w, ow, prev=()):
        outs = [
            ((4 * local, width), BF16),
            ((8, width), F32),
            ((rows, width), F32),
            ((rows, width), F32 if first_call else BF16),
        ]
        n = pltpu.VMEM((heads, span, HD), BF16)
        tr = pltpu.VMEM((heads, HD, span), BF16)
        one = pltpu.VMEM((span, HD), BF16)
        acc = pltpu.VMEM((span, HD), F32)
        return call(
            lambda *r: attn_backward(first_call, block, *r),
            outs,
            10 + len(prev),
            smem=1,
            scratch=[n, tr, one, one, one, pltpu.VMEM((3, heads, HD, span), BF16), acc, acc],
            flops=3 * att_flops,
            nbytes=12 * act_bytes,
        )(lengths, qkv, lse, att, dlow, dlow_oth, first, first_oth, w, ow, *prev)

    gq_b, gqb_b, df_own, df_oth = backward(True, qkv_b, lse_b, att_b, w_oth, ow_oth)
    gq_a, gqb_a, df_own, df_oth = backward(False, qkv_a, lse_a, att_a, w_own, out_weight, (df_own, df_oth))
    df_in = swap_core(df_oth)
    grad_input, small_one = call(back_first, [((rows, width), BF16), ((8, width), F32)], 6, smem=1, nbytes=4 * act_bytes)(
        tie_sets, tokens, df_own, df_in, dmid, norm_gain[0]
    )
    def total(own, other):
        return lax.psum((own.astype(F32) + swap_chip(other).astype(F32)).astype(BF16), "dp")

    g_p, g_f, g_q = total(gp_a, gp_b), total(gf_a, gf_b), total(gq_a, gq_b)
    bias_a = jnp.concatenate([gqb_a[:1], gfb_a], axis=0)
    bias_b = jnp.concatenate([gqb_b[:1], gfb_b], axis=0)
    pack = jnp.concatenate(
        [
            lax.psum(jnp.concatenate([small_two, small_one], axis=0), ("dp", "tensor")),
            lax.psum(bias_a + swap_chip(bias_b), "dp"),
        ],
        axis=0,
    )
    return block_out, grad_input, g_p, g_f, g_q, pack


def body(
    tokens,
    cotangent,
    lengths,
    tie_sets,
    qkv_weight,
    qkv_bias,
    out_weight,
    out_bias,
    fc_weight,
    fc_bias,
    proj_weight,
    proj_bias,
    norm_gain,
    norm_bias,
):
    rows, width = tokens.shape
    groups = lax.axis_size("tensor")
    local = qkv_weight.shape[2]
    heads = local // HD
    hidden = fc_weight.shape[1]
    span = rows * groups // lengths.shape[0]
    assert groups == 4 and span == 2 * rows
    set_count = norm_gain.shape[1]
    dps = lax.axis_size("dp")

    if dps == 8:
        w = qkv_weight.transpose(1, 2, 0).reshape(3 * local, width)
        parts = block_call(
            lengths,
            tie_sets,
            tokens,
            cotangent,
            w,
            out_weight,
            fc_weight,
            proj_weight,
            qkv_bias,
            fc_bias,
            out_bias,
            proj_bias,
            norm_gain,
            norm_bias,
        )
        outs = finish(parts, local, set_count)
        return (*outs[:2], outs[2].reshape(3, local, width).transpose(2, 0, 1), *outs[3:])
    block_out, grad_input, g_p, g_f, g_q, pack = generic(
        tokens,
        cotangent,
        lengths,
        tie_sets,
        qkv_weight,
        qkv_bias,
        out_weight,
        out_bias,
        fc_weight,
        fc_bias,
        proj_weight,
        proj_bias,
        norm_gain,
        norm_bias,
    )
    gains = jnp.stack([pack[8 : 8 + set_count], pack[2 : 2 + set_count]])
    biases = jnp.stack([pack[8 + set_count : 8 + 2 * set_count], pack[2 + set_count : 2 + 2 * set_count]])
    gqb = pack[16, : 3 * local].reshape(3, local)
    return (
        block_out,
        grad_input,
        g_q[: 3 * local].astype(F32).reshape(3, local, width).transpose(2, 0, 1),
        jnp.stack([gqb[0], gqb[2]]),
        g_q[3 * local :].astype(F32),
        pack[0],
        g_f.astype(F32),
        pack[17],
        g_p.astype(F32),
        pack[1],
        gains,
        biases,
    )


def solution(mesh):
    in_specs = (
        P(("dp", "tensor"), None),
        P(("dp", "tensor"), None),
        P("dp"),
        P("dp"),
        P(None, None, "tensor"),
        P(None, "tensor"),
        P("tensor", None),
        P(),
        P(None, "tensor"),
        P("tensor"),
        P("tensor", None),
        P(),
        P(),
        P(),
    )
    out_specs = (
        P(("dp", "tensor"), None),
        P(("dp", "tensor"), None),
        P(None, None, "tensor"),
        P(None, "tensor"),
        P("tensor", None),
        P(),
        P(None, "tensor"),
        P("tensor"),
        P("tensor", None),
        P(),
        P(),
        P(),
    )
    return jax.shard_map(body, mesh=mesh, in_specs=in_specs, out_specs=out_specs, check_vma=False)
```

```python
import jax
import jax.numpy as jnp
from jax import lax
from jax.experimental import pallas as pl
from jax.experimental.pallas import tpu as pltpu
from jax.sharding import PartitionSpec as P

HD = 64
EPS = 1e-05
F32 = jnp.float32
BF16 = jnp.bfloat16
GELU_K = 0.7978845608028654
GELU_C = 0.044715
VMEM = pl.BlockSpec(memory_space=pltpu.VMEM)
SMEM = pl.BlockSpec(memory_space=pltpu.SMEM)
NT = (((1,), (1,)), ((), ()))
TN = (((0,), (0,)), ((), ()))


def dg(a, b, dims):
    return lax.dot_general(a, b, dims, preferred_element_type=F32)


def mm(a, b):
    return jnp.dot(a, b, preferred_element_type=F32)


def call(kernel, outs, n_in, smem=0, scratch=(), limit=48, flops=0, nbytes=0):
    return pl.pallas_call(
        kernel,
        out_shape=[jax.ShapeDtypeStruct(s, d) for s, d in outs],
        in_specs=[SMEM] * smem + [VMEM] * (n_in - smem),
        out_specs=[VMEM] * len(outs),
        scratch_shapes=list(scratch),
        cost_estimate=pl.CostEstimate(flops=flops, bytes_accessed=nbytes, transcendentals=0),
        compiler_params=pltpu.CompilerParams(vmem_limit_bytes=limit << 20),
    )


def place():
    t = lax.axis_index("tensor")
    return t % 2, t // 2


def stats(v):
    mean = jnp.mean(v, axis=-1, keepdims=True)
    cent = v - mean
    var = jnp.mean(cent * cent, axis=-1, keepdims=True)
    r = lax.rsqrt(var + EPS)
    return cent * r, r


def norm_first(sets, x, gain, bias, out):
    k = sets[place()[1]]
    xhat, _ = stats(x[...].astype(F32))
    out[...] = (xhat * gain[pl.ds(k, 1), :] + bias[pl.ds(k, 1), :]).astype(BF16)


def norm_second(sets, x, br, br_in, ob, gain, bias, middle, out):
    k = sets[place()[1]]
    mid = x[...].astype(F32) + (br[...] + br_in[...].astype(F32)) + ob[...]
    middle[...] = mid
    xhat, _ = stats(mid)
    out[...] = (xhat * gain[pl.ds(k, 1), :] + bias[pl.ds(k, 1), :]).astype(BF16)


def norm_pull(v, d, gain):
    xhat, r = stats(v)
    e = d * gain
    m1 = jnp.mean(e, axis=-1, keepdims=True)
    m2 = jnp.mean(e * xhat, axis=-1, keepdims=True)
    return r * (e - m1 - xhat * m2), jnp.sum(d * xhat, axis=0, keepdims=True), jnp.sum(d, axis=0, keepdims=True)


def split_sets(small, at, k, count, gg, gb):
    for i in range(count):
        mine = (k == i).astype(F32)
        small[at + i : at + i + 1, :] = gg * mine
        small[at + count + i : at + count + i + 1, :] = gb * mine
    end = at + 2 * count
    small[end:, :] = jnp.zeros((small.shape[0] - end, small.shape[1]), F32)


def back_second(sets, middle, feed, feed_in, pb, ds, ds_in, ct, gain, block_out, dmid, dlow, small):
    k = sets[place()[1]]
    mid = middle[...]
    block_out[...] = (mid + (feed[...] + feed_in[...].astype(F32)) + pb[...]).astype(BF16)
    d, gg, gb = norm_pull(mid, ds[...] + ds_in[...].astype(F32), gain[pl.ds(k, 1), :])
    c = ct[...].astype(F32)
    d = d + c
    dmid[...] = d
    dlow[...] = d.astype(BF16)
    small[0:1, :] = jnp.sum(d, axis=0, keepdims=True)
    small[1:2, :] = jnp.sum(c, axis=0, keepdims=True)
    split_sets(small, 2, k, gain.shape[0], gg, gb)


def back_first(sets, x, df, df_in, dmid, gain, grad_in, small):
    k = sets[place()[1]]
    d, gg, gb = norm_pull(x[...].astype(F32), df[...] + df_in[...].astype(F32), gain[pl.ds(k, 1), :])
    grad_in[...] = (d + dmid[...]).astype(BF16)
    split_sets(small, 0, k, gain.shape[0], gg, gb)


def mask_scores(scores, start, length):
    span, count = scores.shape
    kpos = lax.broadcasted_iota(jnp.int32, (span, count), 0)
    limit = jnp.minimum(start + lax.broadcasted_iota(jnp.int32, (1, count), 1), length - 1)
    return jnp.where(kpos <= limit, scores, -1e30)


def attn_forward(first_call, block, lengths, x_own, x_oth, w, b, ow, *rest):
    if first_call:
        qkv, lse, att, br_own, br_oth, k_s = rest
    else:
        pr_own, pr_oth, qkv, lse, att, br_own, br_oth, k_s = rest
    c, seq = place()
    length = lengths[seq]
    rows = x_own.shape[0]
    local = w.shape[0] // 3
    heads = local // HD
    span = 2 * rows
    parts = ((x_own, c), (x_oth, 1 - c))
    for x, p in parts:
        at = pl.ds(pl.multiple_of(p * rows, rows), rows)
        y = dg(w[...], x[...], NT) + b[...]
        for h in range(heads):
            lo = h * HD
            qkv[0, h, :, at] = (y[lo : lo + HD] * 0.125).astype(BF16)
            kt = y[local + lo : local + lo + HD]
            qkv[1, h, :, at] = kt.astype(BF16)
            k_s[h, at, :] = kt.T.astype(BF16)
            qkv[2, h, :, at] = y[2 * local + lo : 2 * local + lo + HD].astype(BF16)

    def head(h, carry):
        for i in range(span // block):
            stop = (i + 1) * block
            cols = slice(i * block, stop)
            scores = mm(k_s[h, :stop, :], qkv[0, h, :, cols])
            scores = mask_scores(scores, i * block, length)
            top = jnp.max(scores, axis=0, keepdims=True)
            e = jnp.exp(scores - top)
            total = jnp.sum(e, axis=0, keepdims=True)
            probs = (e * (1.0 / total)).astype(BF16)
            att[h, :, cols] = mm(qkv[2, h, :, :stop], probs).astype(BF16)
            lse[h, :, cols] = top + jnp.log(total)
        return carry

    lax.fori_loop(0, heads, head, 0)
    for (x, p), prev, out in zip(parts, (None, None) if first_call else (pr_own, pr_oth), (br_own, br_oth)):
        at = pl.ds(pl.multiple_of(p * rows, rows), rows)
        a = att[:, :, at].reshape(local, rows)
        r = dg(a, ow[...], TN)
        if prev is not None:
            r = r + prev[...]
        out[...] = r.astype(out.dtype)


def attn_backward(first_call, block, lengths, qkv, lse, att, d_own, d_oth, x_own, x_oth, w, ow, *rest):
    if first_call:
        gq, gb, f_own, f_oth, do_n, do_t, q_n, k_n, v_n, dqkv, dk, dv = rest
    else:
        pf_own, pf_oth, gq, gb, f_own, f_oth, do_n, do_t, q_n, k_n, v_n, dqkv, dk, dv = rest
    c, seq = place()
    length = lengths[seq]
    rows = x_own.shape[0]
    local = w.shape[0] // 3
    heads = local // HD
    span = 2 * rows
    spots = [pl.ds(pl.multiple_of(p * rows, rows), rows) for p in (c, 1 - c)]
    gout = None
    for d, at in zip((d_own, d_oth), spots):
        y = dg(ow[...], d[...], NT)
        for h in range(heads):
            part = y[h * HD : h * HD + HD]
            do_t[h, :, at] = part.astype(BF16)
            do_n[h, at, :] = part.T.astype(BF16)
        a = att[:, :, at].reshape(local, rows)
        term = mm(a, d[...])
        gout = term if gout is None else gout + term
    gq[3 * local :, :] = gout.astype(gq.dtype)

    def head(h, carry):
        q_n[...] = qkv[0, h].astype(F32).T.astype(BF16)
        k_n[...] = qkv[1, h].astype(F32).T.astype(BF16)
        v_n[...] = qkv[2, h].astype(F32).T.astype(BF16)
        for i in range(span // block):
            stop = (i + 1) * block
            cols = slice(i * block, stop)
            scores = mm(k_n[:stop, :], qkv[0, h, :, cols])
            scores = mask_scores(scores, i * block, length)
            probs = jnp.exp(scores - lse[h, :, cols])
            dp = mm(v_n[:stop, :], do_t[h, :, cols])
            total = jnp.sum(probs * dp, axis=0, keepdims=True)
            ds = (probs * (dp - total)).astype(BF16)
            dqkv[0, h, :, cols] = (mm(qkv[1, h, :, :stop], ds) * 0.125).astype(BF16)
            pv = mm(probs.astype(BF16), do_n[h, cols, :])
            pk = mm(ds, q_n[cols, :])
            last = i * block
            if i:
                dv[:last, :] += pv[:last]
                dk[:last, :] += pk[:last]
            dv[last:stop, :] = pv[last:]
            dk[last:stop, :] = pk[last:]
        dqkv[1, h] = dk[...].T.astype(BF16)
        dqkv[2, h] = dv[...].T.astype(BF16)
        return carry

    lax.fori_loop(0, heads, head, 0)
    gqkv = None
    gbias = None
    for x, at, prev, out in zip((x_own, x_oth), spots, (None, None) if first_call else (pf_own, pf_oth), (f_own, f_oth)):
        d = dqkv[:, :, :, at].reshape(3 * local, rows)
        term = mm(d, x[...])
        gqkv = term if gqkv is None else gqkv + term
        s = dg(jnp.ones((8, rows), BF16), d, NT)
        gbias = s if gbias is None else gbias + s
        r = dg(d, w[...], TN)
        if prev is not None:
            r = r + prev[...]
        out[...] = r.astype(out.dtype)
    gq[: 3 * local, :] = gqkv.astype(gq.dtype)
    gb[...] = jnp.zeros_like(gb)
    gb[:, : 3 * local] = gbias


def mlp_kernel(first_call, s_own, s_oth, c_own, c_oth, fc, fb, pw, *rest):
    if first_call:
        gf, gp, gb, fe_own, fe_oth, ds_own, ds_oth, st = rest
        prev = (None, None, None, None)
    else:
        prev = rest[:4]
        gf, gp, gb, fe_own, fe_oth, ds_own, ds_oth, st = rest[4:12]
        accs = rest[12:]
    j = pl.program_id(0)
    rows = s_own.shape[0]

    @pl.when(j == 0)
    def _():
        st[:, :rows] = s_own[...].T
        st[:, rows:] = s_oth[...].T

    gfc = gproj = gbias = None
    for n, (s, ct, fe, ds) in enumerate(((s_own, c_own, fe_own, ds_own), (s_oth, c_oth, fe_oth, ds_oth))):
        pre = mm(s[...], fc[...]) + fb[...]
        sq = pre * pre
        t = jnp.tanh(GELU_K * (pre + GELU_C * sq * pre))
        half = 0.5 * (1.0 + t)
        act = (pre * half).astype(BF16)
        slope = half + (0.5 * GELU_K) * pre * (1.0 - t * t) * (1.0 + (3.0 * GELU_C) * sq)
        dpre = dg(ct[...], pw[...], NT) * slope
        low = dpre.astype(BF16)
        bs = jnp.sum(low.astype(F32), axis=0, keepdims=True)
        tf = mm(st[:, n * rows : (n + 1) * rows], low)
        tp = dg(act, ct[...], TN)
        gfc = tf if gfc is None else gfc + tf
        gproj = tp if gproj is None else gproj + tp
        gbias = bs if gbias is None else gbias + bs
        add_f = mm(act, pw[...])
        add_s = dg(low, fc[...], NT)
        if first_call:
            fa, sa, pf, ps = fe, ds, None, None
        else:
            fa, sa = accs[2 * n], accs[2 * n + 1]
            pf, ps = prev[n], prev[2 + n]

        @pl.when(j == 0)
        def _():
            fa[...] = add_f if pf is None else add_f + pf[...]
            sa[...] = add_s if ps is None else add_s + ps[...]

        @pl.when(j > 0)
        def _():
            fa[...] += add_f
            sa[...] += add_s

        if not first_call:
            @pl.when(j == pl.num_programs(0) - 1)
            def _():
                fe[...] = fa[...].astype(fe.dtype)
                ds[...] = sa[...].astype(ds.dtype)

    gf[...] = gfc.astype(gf.dtype)
    gp[...] = gproj.astype(gp.dtype)
    gb[...] = gbias


def mlp(first_call, s_own, s_oth, c_own, c_oth, fc, fb, pw, prev=()):
    rows, width = s_own.shape
    hidden = fc.shape[1]
    hb = 256
    fixed = pl.BlockSpec((rows, width), lambda j: (0, 0))
    oth = F32 if first_call else BF16
    sums = [(rows, width)] * 4
    scratch = [pltpu.VMEM((width, 2 * rows), BF16)]
    if not first_call:
        scratch += [pltpu.VMEM(s, F32) for s in sums]
    return pl.pallas_call(
        lambda *r: mlp_kernel(first_call, *r),
        grid=(hidden // hb,),
        in_specs=[fixed] * 4
        + [
            pl.BlockSpec((width, hb), lambda j: (0, j)),
            pl.BlockSpec((1, hb), lambda j: (0, j)),
            pl.BlockSpec((hb, width), lambda j: (j, 0)),
        ]
        + [fixed] * len(prev),
        out_specs=[
            pl.BlockSpec((width, hb), lambda j: (0, j)),
            pl.BlockSpec((hb, width), lambda j: (j, 0)),
            pl.BlockSpec((1, hb), lambda j: (0, j)),
        ]
        + [fixed] * 4,
        out_shape=[
            jax.ShapeDtypeStruct((width, hidden), BF16),
            jax.ShapeDtypeStruct((hidden, width), BF16),
            jax.ShapeDtypeStruct((1, hidden), F32),
            jax.ShapeDtypeStruct((rows, width), F32),
            jax.ShapeDtypeStruct((rows, width), oth),
            jax.ShapeDtypeStruct((rows, width), F32),
            jax.ShapeDtypeStruct((rows, width), oth),
        ],
        scratch_shapes=scratch,
        cost_estimate=pl.CostEstimate(flops=24 * rows * width * hidden, bytes_accessed=20 * rows * width, transcendentals=0),
        compiler_params=pltpu.CompilerParams(vmem_limit_bytes=56 << 20),
    )(s_own, s_oth, c_own, c_oth, fc, fb, pw, *prev)


def partners():
    t, d = lax.axis_index("tensor"), lax.axis_index("dp")
    bits = {"x": d % 2, "1": (d // 2) % 2, "2": d // 4}
    to = {
        "c": {"tensor": t + 1 - 2 * (t % 2)},
        "y": {"tensor": (t + 2) % 4},
        "x": {"dp": d + 1 - 2 * bits["x"]},
        "1": {"dp": d + 2 - 4 * bits["1"]},
        "2": {"dp": (d + 4) % 8},
        "3": {"dp": (d + 4) % 8 + 2 - 4 * bits["1"]},
    }
    return to, bits


def remote(src, dst, send, recv, where):
    return pltpu.make_async_remote_copy(
        src_ref=src, dst_ref=dst, send_sem=send, recv_sem=recv, device_id=where, device_id_type=pl.DeviceIdType.MESH
    )


def aligned(start, n, by=16):
    return pl.ds(pl.multiple_of(start, by), n)


class Flow:
    def __init__(self, own, oth, res, buf, outs, order, to, bits, sems):
        self.acts, self.outs = [], [pltpu.make_async_copy(res.at[src], out, sems(None)) for src, out in outs]
        base, n, at, both = 0, own.shape[0], 0, True
        back, waits, adds, slot = [], [], [], 0
        for k, o in enumerate(order):
            copies, sums = [], []
            last = k == len(order) - 1
            if o == "y":
                here = aligned(base, n)
                got = buf.at[aligned(at, n)]
                at += n
                copies.append(remote(oth.at[here], got, *sems(slot), to[o]))
                sums.append(((res if last else own).at[here], own.at[here], [got]))
                slot += 1
                both = False
            elif o == "e":
                here = aligned(base, n)
                got = buf.at[aligned(at, n)]
                copies.append(remote(own.at[here], got, *sems(slot), to["2"]))
                sums.append((res.at[here], own.at[here], [got]))
                slot += 1
            else:
                size = n // 4 if o == "Z" else n // 2
                back.append((o, base, size))
                mine = bits["1"] + 2 * bits["2"] if o == "Z" else bits[o]
                keep = aligned(base + mine * size, size)
                for ref in (own, oth) if both else (own,):
                    gots = []
                    for peer in "123" if o == "Z" else o:
                        other = zs(bits, peer) if o == "Z" else 1 - mine
                        got = buf.at[aligned(at, size)]
                        at += size
                        copies.append(remote(ref.at[aligned(base + other * size, size)], got, *sems(slot), to[peer]))
                        gots.append(got)
                        slot += 1
                    sums.append(((res if last else ref).at[keep], ref.at[keep], gots))
                base, n = base + mine * size, size
            if k == 0 and both:
                self.acts += [([], [], copies[:1]), ([], [], copies[1:])]
            else:
                self.acts.append((waits, adds, copies))
            waits, adds = copies, sums
        for o, start, size in reversed(back):
            here = res.at[aligned(base, n)]
            copies = []
            for peer in "123" if o == "Z" else o:
                copies.append(remote(here, here, *sems(slot), to[peer]))
                slot += 1
            self.acts.append((waits, adds, copies))
            waits, adds = copies, []
            base, n = start, size * (4 if o == "Z" else 2)
        self.acts.append((waits, adds, self.outs))

    def step(self, k):
        waits, adds, starts = self.acts[k]
        for copy in waits:
            copy.wait()
        for dst, mine, gots in adds:
            total = mine[...].astype(F32)
            for got in gots:
                total = total + got[...].astype(F32)
            dst[...] = total.astype(BF16)
        for copy in starts:
            copy.start()


def zs(bits, peer):
    one = 1 - bits["1"] if peer in "13" else bits["1"]
    two = 1 - bits["2"] if peer in "23" else bits["2"]
    return one + 2 * two


def pick(gains, chosen):
    row = gains[0:1, :]
    for i in range(1, gains.shape[0]):
        row = jnp.where(chosen == i, gains[i : i + 1, :], row)
    return row


def block_kernel(*refs):
    (lengths, sets, tok_h, ct_h, w_h, ow_h, fc_h, pw_h, qkv_b, fc_b, ob, pb, gains, biases) = refs[:14]
    out_h, in_h, o_p, o_f, o_q, o_o, pack = refs[14:21]
    (tok, ct, ct_oth, first, first_oth, w, ow, fc, pw, bias, qkv, lse, att, nat, trn) = refs[21:36]
    (give, fe_send, br_in, middle, second, second_oth, st, acc, ds_in, fe_in) = refs[36:46]
    (dlow_oth, q_n, k_n, v_n, dqkv, dk, dv, df_in, q_t, block_out, grad_in) = refs[46:57]
    (grad, res, buf, fbg, r_pack, load, sends, recvs, wsend, wrecv, done) = refs[57:]
    dlow = second
    block, wide = 256, 512
    to, bits = partners()
    c, seq = place()
    length, chosen = lengths[seq], sets[seq]
    rows, width = tok.shape
    local = ow.shape[1]
    heads = local // HD
    span = 2 * rows
    hidden = fc.shape[2]
    blocks = hidden // block
    spots = [pl.ds(pl.multiple_of(p * rows, rows), rows) for p in (c, 1 - c)]

    loads = {}
    for name, src, dst in (
        ("tok", tok_h, tok),
        ("w", w_h, w.at[0]),
        ("ow", ow_h, ow.at[0]),
        ("ct", ct_h, ct),
        ("fc", fc_h, fc.at[0]),
        ("pw", pw_h, pw.at[0]),
    ):
        loads[name] = pltpu.make_async_copy(src, dst, load.at[len(loads)])
        loads[name].start()

    bias[0] = jnp.zeros(bias.shape[1:], BF16)
    bias[1, 8:] = jnp.zeros((8, bias.shape[2]), BF16)
    edge = hidden + 256
    bias[0, 0:1, :hidden] = fc_b[...].reshape(1, hidden)
    bias[0, 0:1, hidden : hidden + local] = qkv_b[0:1, :]
    bias[0, 0:1, edge : edge + local] = qkv_b[1:2, :]

    barrier = pltpu.get_barrier_semaphore()
    for where in to.values():
        pl.semaphore_signal(barrier, inc=1, device_id=where, device_id_type=pl.DeviceIdType.MESH)
    pl.semaphore_wait(barrier, len(to))

    bias_copy = remote(bias.at[0, :8], bias.at[1, :8], wsend.at[0], wrecv.at[0], to["y"])
    pieces = []
    for src, dst, start, n in (
        (w_h, w, 0, local),
        (w_h, w, local, local),
        (w_h, w, 2 * local, local),
        (ow_h, ow, 0, local),
        (fc_h, fc, 0, width // 2),
        (fc_h, fc, width // 2, width // 2),
        (pw_h, pw, 0, hidden // 2),
        (pw_h, pw, hidden // 2, hidden // 2),
    ):
        k = 1 + 4 * len(pieces)
        first_way, last_way = ("1", "x") if len(pieces) % 2 else ("x", "1")

        def quarter(x, z, start=start, n=n):
            return aligned(start + (2 * z + x) * (n // 4), n // 4, 8)

        mine = quarter(bits["x"], bits["1"])
        there = dst.at[1, mine]
        got = quarter(1 - bits["x"], bits["1"]) if first_way == "x" else quarter(bits["x"], 1 - bits["1"])
        over = remote(src.at[mine], there, wsend.at[k], wrecv.at[k], to["y"])
        one = remote(there, there, wsend.at[k + 1], wrecv.at[k + 1], to[first_way])
        two = remote(there, there, wsend.at[k + 2], wrecv.at[k + 2], to[last_way])
        rest = remote(dst.at[1, got], dst.at[1, got], wsend.at[k + 3], wrecv.at[k + 3], to[last_way])
        pieces.append((over, [one, two], [one], [rest], [two, rest]))
    for i, (over, *_) in enumerate(pieces):
        over.start()
        if i == 2:
            bias_copy.start()

    def forward(acts):
        for i, act in acts:
            over, on, waits, starts, ends = pieces[i]
            if act == 0:
                waits, starts = [over], on
            elif act == 2:
                waits, starts = ends, []
            for copy in waits:
                copy.wait()
            for copy in starts:
                copy.start()

    flows = []
    n_flow = 9
    for f in range(n_flow):
        unit, j = f // 3, f % 3
        part = (slice(None), slice(j * block, (j + 1) * block)) if unit == 1 else (slice(j * block, (j + 1) * block),)
        if unit < 2:
            outs = [((slice(None),), (o_p, o_f)[unit].at[part])]
        else:
            outs = [((slice(n * HD, (n + 1) * HD),), o_q.at[pl.ds(n * local + j * HD, HD)]) for n in range(3)]
            outs.append(((slice(3 * HD, 4 * HD),), o_o.at[pl.ds(j * HD, HD)]))
        room = (slice(None), part[1]) if unit == 1 else (slice(j * 2 * block, (j + 1) * 2 * block),)

        def sems(k, f=f):
            return done.at[f] if k is None else (sends.at[f, k], recvs.at[f, k])

        flows.append(
            Flow(
                grad.at[(0, unit, *part)],
                grad.at[(1, unit, *part)],
                res.at[(unit, *part)],
                buf.at[(unit, *room)],
                outs,
                ORDERS[f],
                to,
                bits,
                sems,
            )
        )

    def swap(n, src, dst):
        return remote(src, dst, sends.at[n_flow, n], recvs.at[n_flow, n], to["c"])

    small_order = "cyx12"
    small_copies = [
        remote(pack, r_pack.at[n], sends.at[n_flow + 1, n], recvs.at[n_flow + 1, n], to[o]) for n, o in enumerate(small_order)
    ]

    def small(n):
        if n:
            small_copies[n - 1].wait()
            got = r_pack[n - 1]
            mid = pack[16:24, :]
            if n == 2:
                mid = mid + got[24:]
            elif n > 2:
                mid = mid + got[16:24]
            pack[:16, :] = pack[:16, :] + got[:16]
            pack[16:24, :] = mid
        if n < len(small_order):
            small_copies[n].start()

    def run(events):
        for f, k in events:
            if f < 0:
                small(k)
            else:
                flows[f].step(k)

    def at_step(i, table, what):
        for n, some in enumerate(table):
            if some:

                @pl.when(i == n)
                def _():
                    what(some)

    tile = 256

    def by_rows(step, carry=0, copies=()):
        def one(i, held):
            held = step(pl.multiple_of(i * tile, tile), held)
            for n, copy in enumerate(copies):
                pl.when(i == n)(copy.start)
            return held

        return lax.fori_loop(0, rows // tile, one, carry)

    def swap_tiles(n, src, dst):
        parts = [pl.ds(t * tile, tile) for t in range(rows // tile)]
        pairs = [(sends.at[n_flow, n + 8 * t], recvs.at[n_flow, n + 8 * t]) for t in range(len(parts))]
        return [remote(src.at[r], dst.at[r], *pair, to["c"]) for r, pair in zip(parts, pairs)]

    def wait_all(copies):
        for copy in copies:
            copy.wait()

    def norm(n, v):
        return (stats(v)[0] * pick(gains[n], chosen) + pick(biases[n], chosen)).astype(BF16)

    zero = jnp.zeros((1, width), F32)

    loads["tok"].wait()

    def norm_tokens(r, carry):
        r = pl.ds(r, tile)
        first[r] = norm(0, tok[r].astype(F32))
        return carry

    first_swap = swap_tiles(0, first, first_oth)
    by_rows(norm_tokens, copies=first_swap)
    loads["ct"].wait()
    ct_swap = swap(1, ct, ct_oth)
    ct_swap.start()
    loads["w"].wait()

    q_t[HD:, :] = (lax.broadcasted_iota(jnp.int32, (HD, span), 0) == 0).astype(BF16)
    true_key = lax.broadcasted_iota(jnp.int32, (span, HD), 0) < length
    key_lane = lax.broadcasted_iota(jnp.int32, (span, HD), 1) == 0
    key_mask = jnp.where(true_key, 0.0, jnp.where(key_lane, -1e30, 0.0)).astype(BF16)
    for h in range(heads):
        nat[0, h, :, HD:] = key_mask
    k_n[:, HD:] = key_mask
    later = lax.broadcasted_iota(jnp.int32, (wide, wide), 0) > lax.broadcasted_iota(jnp.int32, (wide, wide), 1)

    def scores(keys, last, stop):
        cols = slice(last, stop)
        same = jnp.where(later, -1e30, mm(keys(cols), q_t[:, cols]))
        return [mm(keys(slice(0, last)), q_t[:, cols]), same] if last else [same]

    pick_row = (lax.broadcasted_iota(jnp.int32, (16, rows), 0) == 0).astype(BF16)

    def attend(s, carry):
        @pl.when(s == 1)
        def _():
            forward(FORWARD_SECOND)
            bias_copy.wait()

        q_col = dg(bias[s, :, hidden : hidden + local], pick_row, TN)
        v_col = dg(bias[s, :, edge : edge + local], pick_row, TN)
        for n, (x, at) in enumerate(zip((first, first_oth), spots)):
            if n:

                @pl.when(s == 0)
                def _():
                    wait_all(first_swap)

            y = dg(w[s], x[...], NT)
            for h in range(heads):
                lo = h * HD
                qkv[s, 0, h, :, at] = ((y[lo : lo + HD] + q_col[lo : lo + HD]) * 0.125).astype(BF16)
                kt = y[local + lo : local + lo + HD]
                qkv[s, 1, h, :, at] = kt.astype(BF16)
                nat[0, h, at, :HD] = kt.T.astype(BF16)
                vt = y[2 * local + lo : 2 * local + lo + HD]
                qkv[s, 2, h, :, at] = (vt + v_col[lo : lo + HD]).astype(BF16)
            at_step(s, FORWARD_ROWS[n], forward)

        def head(h, carry):
            q_t[:HD, :] = qkv[s, 0, h]
            for i in range(span // wide):
                last, stop = i * wide, (i + 1) * wide
                cols = slice(last, stop)
                parts = scores(lambda rows: nat[0, h, rows, :], last, stop)
                top = parts[-1].max(axis=0, keepdims=True)
                if i:
                    top = jnp.maximum(top, parts[0].max(axis=0, keepdims=True))
                total = out = None
                for v, keys in zip(parts, (slice(0, last), cols) if i else (cols,)):
                    e = jnp.exp(v - top)
                    add = jnp.sum(e, axis=0, keepdims=True)
                    term = mm(qkv[s, 2, h, :, keys], e.astype(BF16))
                    total = add if total is None else total + add
                    out = term if out is None else out + term
                att[s, h, :, cols] = (out * (1.0 / total)).astype(BF16)
                lse[s, h, :, cols] = top + jnp.log(total)
            at_step(s * heads + h, FORWARD_HEADS, forward)
            return carry

        lax.fori_loop(0, heads, head, 0)
        return carry

    lax.fori_loop(0, 2, attend, 0)
    loads["ow"].wait()
    forward(FORWARD_PROJECT)

    def project(p, r):
        at = pl.ds(pl.multiple_of(p * rows + r, tile), tile)
        return dg(att[0, :, :, at].reshape(local, tile), ow[0], TN) + dg(att[1, :, :, at].reshape(local, tile), ow[1], TN)

    def project_other(r, carry):
        give[pl.ds(r, tile)] = project(1 - c, r).astype(BF16)
        return carry

    br_swap = swap_tiles(2, give, br_in)
    by_rows(project_other, copies=br_swap)

    def project_own(r, carry):
        middle[pl.ds(r, tile)] = tok[pl.ds(r, tile)].astype(F32) + ob[...].astype(F32).reshape(1, width) + project(c, r)
        return carry

    by_rows(project_own)
    forward(FORWARD_MIDDLE)
    wait_all(br_swap)

    def norm_middle(r, carry):
        r = pl.ds(r, tile)
        mid = middle[r] + br_in[r].astype(F32)
        middle[r] = mid
        second[r] = norm(1, mid)
        return carry

    second_swap = swap_tiles(3, second, second_oth)
    by_rows(norm_middle, copies=second_swap)
    forward(FORWARD_NORM)
    st[:, :rows] = second[...].T
    loads["fc"].wait()
    loads["pw"].wait()

    ds_swap, fe_swap = swap(4, give, ds_in), swap(5, fe_send, fe_in)
    halves = ((second, ct), (second_oth, ct_oth))

    def units(jj, carry, turn=(1, 0)):
        s, j = jj // blocks, jj % blocks
        here = pl.ds(pl.multiple_of(j * block, block), block)

        @pl.when(jj == blocks)
        def _():
            forward(FORWARD_OTHER)

        gfc = gproj = gbias = None
        for n in turn:
            x, g = halves[n]
            if turn == (0, 1) and n:
                ct_swap.wait()
                wait_all(second_swap)
                st[:, rows:] = second_oth[...].T
            pre = mm(x[...], fc[s, :, here]) + bias[s, 0:1, here].astype(F32)
            sq = pre * pre
            t = jnp.tanh(pre * (GELU_K + (GELU_K * GELU_C) * sq))
            half = 0.5 + 0.5 * t
            full = pre * half
            act = full.astype(BF16)
            slope = half + full * (1.0 - t) * (GELU_K + (3.0 * GELU_K * GELU_C) * sq)
            low = (dg(g[...], pw[s, here, :], NT) * slope).astype(BF16)
            bs = jnp.sum(low.astype(F32), axis=0, keepdims=True)
            tf = mm(st[:, n * rows : (n + 1) * rows], low)
            tp = dg(act, g[...], TN)
            gfc = tf if gfc is None else gfc + tf
            gproj = tp if gproj is None else gproj + tp
            gbias = bs if gbias is None else gbias + bs
            add_f = mm(act, pw[s, here, :])
            add_s = dg(low, fc[s, :, here], NT)

            if turn == (0, 1):
                acc[n] = add_f
                acc[2 + n] = add_s
            else:
                acc[n] += add_f
                acc[2 + n] += add_s
            if n == 1:

                @pl.when(jj == 2 * blocks - 1)
                def _():
                    give[...] = acc[3].astype(BF16)
                    ds_swap.start()
                    fe_send[...] = acc[1].astype(BF16)
                    fe_swap.start()

            if n == turn[0]:
                at_step(jj, FORWARD_UNITS_MID, forward)
                at_step(jj, UNITS_MID, run)

        grad[s, 1, :, here] = gfc.astype(BF16)
        grad[s, 0, here, :] = gproj.astype(BF16)
        fbg[s, 0:1, here] = gbias
        at_step(jj, FORWARD_UNITS, forward)
        at_step(jj, UNITS, run)
        return carry

    units(0, 0, (0, 1))
    lax.fori_loop(1, 2 * blocks, units, 0)
    run(AFTER_UNITS)
    ds_swap.wait()
    fe_swap.wait()

    def back_middle(r, held):
        r = pl.ds(r, tile)
        mid, cot = middle[r], ct[r].astype(F32)
        block_out[r] = (mid + (acc[0, r] + fe_in[r].astype(F32)) + pb[...].astype(F32).reshape(1, width)).astype(BF16)
        d, gg, gb = norm_pull(mid, acc[2, r] + ds_in[r].astype(F32), pick(gains[1], chosen))
        d = d + cot
        middle[r] = d
        dlow[r] = d.astype(BF16)
        new = (jnp.sum(d, axis=0, keepdims=True), jnp.sum(cot, axis=0, keepdims=True), gg, gb)
        return tuple(a + b for a, b in zip(held, new))

    low_swap = swap_tiles(6, dlow, dlow_oth)
    sums = by_rows(back_middle, (zero,) * 4, low_swap)
    out_copy = pltpu.make_async_copy(block_out, out_h, load.at[0])
    out_copy.start()
    pack[0:1, :] = sums[0]
    pack[1:2, :] = sums[1]
    split_sets(pack.at[0:8], 2, chosen, gains.shape[1], sums[2], sums[3])
    run(AFTER_SECOND)

    for n, (g, at) in enumerate(zip((dlow, dlow_oth), spots)):
        if n:
            wait_all(low_swap)
        for s in range(2):
            y = dg(ow[s], g[...], NT)
            for h in range(heads):
                piece = y[h * HD : h * HD + HD]
                trn[s, h, :, at] = piece.astype(BF16)
                nat[s, h, at, :HD] = piece.T.astype(BF16)

    def pull(i, carry):
        s = h = 0
        for n, (shard, which) in enumerate(HEAD_ORDER):
            s, h = jnp.where(i == n, shard, s), jnp.where(i == n, which, h)
        q_t[:HD, :] = qkv[s, 0, h]
        q_n[...] = qkv[s, 0, h].astype(F32).T.astype(BF16)
        k_n[:, :HD] = qkv[s, 1, h].astype(F32).T.astype(BF16)
        v_n[...] = qkv[s, 2, h].astype(F32).T.astype(BF16)
        for b in range(span // wide):
            last, stop = b * wide, (b + 1) * wide
            cols = slice(last, stop)
            parts = scores(lambda rows: k_n[rows, :], last, stop)
            total = jnp.sum(att[s, h, :, cols].astype(F32) * trn[s, h, :, cols].astype(F32), axis=0, keepdims=True)
            dq = None
            for v, keys in zip(parts, (slice(0, last), cols) if b else (cols,)):
                probs = jnp.exp(v - lse[s, h, :, cols])
                ds = (probs * (mm(v_n[keys, :], trn[s, h, :, cols]) - total)).astype(BF16)
                term = mm(qkv[s, 1, h, :, keys], ds)
                dq = term if dq is None else dq + term
                pv = mm(probs.astype(BF16), nat[s, h, cols, :HD])
                pk = mm(ds, q_n[cols, :])
                if keys.stop == stop:
                    dv[keys, :] = pv
                    dk[keys, :] = pk
                else:
                    dv[keys, :] += pv
                    dk[keys, :] += pk
            dqkv[s, 0, h, :, cols] = (dq * 0.125).astype(BF16)
            if stop < span:
                at_step(i, HEADS[b], run)
        dqkv[s, 1, h] = dk[...].T.astype(BF16)
        dqkv[s, 2, h] = dv[...].T.astype(BF16)
        gq = go = None
        for x, g, at in zip((first, first_oth), (dlow, dlow_oth), spots):
            tq = mm(dqkv[s, :, h, :, at].reshape(3 * HD, rows), x[...])
            to_ = mm(att[s, h, :, at], g[...])
            gq = tq if gq is None else gq + tq
            go = to_ if go is None else go + to_
        top = pl.multiple_of(h * 4 * HD, 4 * HD)
        grad[s, 2, pl.ds(top, 3 * HD), :] = gq.astype(BF16)
        grad[s, 2, pl.ds(top + 3 * HD, HD), :] = go.astype(BF16)
        at_step(i, HEADS[-1], run)
        return carry

    lax.fori_loop(0, 2 * heads, pull, 0)

    def pull_first(p, r):
        at = pl.ds(pl.multiple_of(p * rows + r, tile), tile)
        return dg(dqkv[0, :, :, :, at].reshape(3 * local, tile), w[0], TN) + dg(
            dqkv[1, :, :, :, at].reshape(3 * local, tile), w[1], TN
        )

    def pull_other(r, carry):
        give[pl.ds(r, tile)] = pull_first(1 - c, r).astype(BF16)
        return carry

    df_swap = swap_tiles(7, give, df_in)
    by_rows(pull_other, copies=df_swap)
    run(AFTER_HEADS)

    def pull_own(r, carry):
        acc[0, pl.ds(r, tile)] = pull_first(c, r)
        return carry

    by_rows(pull_own)
    wait_all(df_swap)

    def back_tokens(r, held):
        r = pl.ds(r, tile)
        d, gg, gb = norm_pull(tok[r].astype(F32), acc[0, r] + df_in[r].astype(F32), pick(gains[0], chosen))
        grad_in[r] = (d + middle[r]).astype(BF16)
        return (held[0] + gg, held[1] + gb)

    sums = by_rows(back_tokens, (zero,) * 2)
    in_copy = pltpu.make_async_copy(grad_in, in_h, load.at[1])
    in_copy.start()
    split_sets(pack.at[8:16], 0, chosen, gains.shape[1], sums[0], sums[1])
    for s in range(2):
        at = 16 + 8 * s
        pack[at : at + 8, :] = jnp.zeros((8, width), F32)
        pack[at : at + 1, : 3 * local] = dg(jnp.ones((8, span), BF16), dqkv[s].reshape(3 * local, span), NT)[0:1]
        pack[at + 1 : at + 2, :] = fbg[s, 0:1]
    run(TAIL)
    for flow in flows:
        for out in flow.outs:
            out.wait()
    out_copy.wait()
    in_copy.wait()


FORWARD_ROWS = ([[(0, 0)], []], [[(1, 0), (2, 0), (0, 1)], [(3, 1), (5, 0)]])
FORWARD_HEADS = ([(1, 1)], [(2, 1), (3, 0), (4, 0)], [(1, 2)], [], [(6, 0)], [(3, 2)])
FORWARD_SECOND = [(0, 2), (2, 2)]
FORWARD_PROJECT = []
FORWARD_MIDDLE = [(7, 0), (4, 1), (5, 1)]
FORWARD_NORM = []
FORWARD_OTHER = [(7, 2)]
FORWARD_UNITS_MID = ([(6, 1)], [], [(5, 2), (4, 2), (6, 2)])
FORWARD_UNITS = ([(7, 1)], [], [])
HEAD_ORDER = ((1, 0), (1, 1), (0, 0), (1, 2), (0, 1), (0, 2))
ORDERS = ("x1ye", "yx12", "1xye", "yx1e", "1xye", "x1ye", "yx1e", "yx1e", "yx1e")
UNITS_MID = (
    [],
    [],
    [],
    [],
    [],
    [(1, 0)],
)
UNITS = (
    [(0, 0)],
    [],
    [(2, 0)],
    [(3, 0), (0, 1), (4, 0), (5, 0)],
    [(4, 1)],
    [(5, 1)],
)
AFTER_UNITS = [
    (0, 2), (2, 1),
]
AFTER_SECOND = [
    (3, 1),
]
HEADS = (
    (
        [(5, 2), (0, 3)],
        [(3, 2), (2, 2), (0, 4), (4, 2)],
        [(7, 0), (1, 2), (3, 3)],
        [(1, 3), (5, 4)],
        [(4, 3), (3, 4), (0, 6)],
        [(5, 5), (3, 5)],
    ),
    (
        [(6, 0), (1, 1)],
        [(5, 3)],
        [(6, 1), (0, 5)],
        [(8, 0)],
        [(6, 2), (1, 4), (2, 3), (7, 1)],
        [(0, 7), (6, 3)],
    ),
)
AFTER_HEADS = [
    (1, 5), (7, 2), (8, 1), (5, 6), (4, 4), (6, 4), (3, 6),
]
TAIL = [
    (-1, 0), (2, 4), (8, 2), (7, 3), (4, 5), (-1, 1), (1, 6), (4, 6), (-1, 2), (5, 7), (2, 5), (6, 5), (8, 3),
    (7, 4), (1, 7), (4, 7), (-1, 3), (8, 4), (7, 5), (6, 6), (-1, 4), (2, 6), (8, 5), (7, 6), (2, 7), (-1, 5),
    (8, 6),
]


def block_call(lengths, sets, tok, ct, w, ow, fc, pw, qkv_b, fc_b, ob, pb, gains, biases):
    rows, width = tok.shape
    local, hidden = ow.shape[0], fc.shape[1]
    heads, span = local // HD, 2 * rows
    total = 4 * local
    assert total == width == hidden
    any_spec = pl.BlockSpec(memory_space=pl.ANY)

    def v(*shape, dtype=BF16):
        return pltpu.VMEM(shape, dtype)

    act, wide = v(rows, width), v(rows, width, dtype=F32)
    one, one_acc = v(span, HD), v(span, HD, dtype=F32)
    dma = pltpu.SemaphoreType.DMA
    scratch = [act, act, act, act, act]
    scratch += [v(2, 3 * local, width), v(2, local, width), v(2, width, hidden), v(2, hidden, width), v(2, 16, hidden + 512)]
    scratch += [v(2, 3, heads, HD, span), v(2, heads, 1, span, dtype=F32), v(2, heads, HD, span), v(2, heads, span, 2 * HD), v(2, heads, HD, span)]
    scratch += [act, act, act, wide, act, act, v(width, span), v(4, rows, width, dtype=F32), act, act]
    scratch += [act, one, v(span, 2 * HD), one, v(2, 3, heads, HD, span), one_acc, one_acc, act, v(2 * HD, span), act, act]
    scratch += [v(2, 3, total, width), v(3, total, width), v(3, 2 * total, width), v(2, 8, hidden, dtype=F32), v(5, 32, width, dtype=F32)]
    scratch += [dma((7,)), dma((11, 16)), dma((11, 16)), dma((33,)), dma((33,)), dma((9,))]
    shapes = [(rows, width)] * 2 + [(total, width)] * 2 + [(3 * local, width), (local, width)]
    return pl.pallas_call(
        block_kernel,
        out_shape=[jax.ShapeDtypeStruct(s, BF16) for s in shapes] + [jax.ShapeDtypeStruct((32, width), F32)],
        in_specs=[SMEM] * 2 + [any_spec] * 6 + [VMEM] * 6,
        out_specs=[any_spec] * 6 + [VMEM],
        scratch_shapes=scratch,
        compiler_params=pltpu.CompilerParams(vmem_limit_bytes=63 << 20, collective_id=1, has_side_effects=True),
    )(lengths, sets, tok, ct, w, ow, fc, pw, qkv_b, fc_b, ob, pb, gains, biases)


def finish_kernel(b, g, p, f, q, o, pack, block_out, grad_in, gq, gqb, go, gob, gf, gfb, gp, gpb, gains, biases):
    block_out[...] = b[...]
    grad_in[...] = g[...]
    for src, dst in ((p, gp), (f, gf), (q, gq), (o, go)):
        dst[...] = src[...].astype(F32)

    @pl.when(pl.program_id(0) == 0)
    def _():
        local = gqb.shape[1]
        count = gains.shape[1]
        gqb[0:1, :] = pack[16:17, :local]
        gqb[1:2, :] = pack[16:17, 2 * local : 3 * local]
        for row, dst in ((0, gob), (1, gpb), (17, gfb)):
            dst[...] = pack[row : row + 1, :].reshape(dst.shape)
        for n, at in ((0, 8), (1, 2)):
            gains[n] = pack[at : at + count, :]
            biases[n] = pack[at + count : at + 2 * count, :]


def finish(parts, local, count):
    rows, width = parts[0].shape
    steps = 2

    def spec(array):
        return pl.BlockSpec((array.shape[0] // steps, width), lambda i: (i, 0))

    def whole(*shape):
        return pl.BlockSpec(shape, lambda i: (0,) * len(shape))

    b, g, p, f, q, o, pack = parts
    sets = (2, count, width)
    small = [(2, local), (width,), (p.shape[0],), (width,), sets, sets]
    order = [(b, BF16), (g, BF16), (q, F32), small[0], (o, F32), small[1], (f, F32), small[2], (p, F32)] + small[3:]
    big = [isinstance(v[0], jax.Array) for v in order]
    return pl.pallas_call(
        finish_kernel,
        grid=(steps,),
        in_specs=[spec(v) for v in parts[:6]] + [whole(*pack.shape)],
        out_specs=[spec(v[0]) if k else whole(*v) for v, k in zip(order, big)],
        out_shape=[jax.ShapeDtypeStruct(*((v[0].shape, v[1]) if k else (v, F32))) for v, k in zip(order, big)],
    )(*parts)


def generic(tokens, cotangent, lengths, tie_sets, qkv_weight, qkv_bias, out_weight, out_bias, fc_weight, fc_bias, proj_weight, proj_bias, norm_gain, norm_bias):
    rows, width = tokens.shape
    local = qkv_weight.shape[2]
    heads = local // HD
    hidden = fc_weight.shape[1]
    span = 2 * rows

    def swap_core(v):
        return lax.ppermute(v, "tensor", [(i, i ^ 1) for i in range(4)])

    def swap_chip(v):
        return lax.ppermute(v, "tensor", [(i, i ^ 2) for i in range(4)])

    def after(v, *first):
        return lax.optimization_barrier((v, *first))[0]

    w_own = qkv_weight.transpose(1, 2, 0).reshape(3 * local, width)
    b_own = jnp.concatenate([qkv_bias[:1], jnp.zeros_like(qkv_bias[:1]), qkv_bias[1:]], axis=0)
    bias_pack = jnp.concatenate([b_own.reshape(1, 3 * local), fc_bias.reshape(1, hidden)], axis=1)
    w_oth = swap_chip(w_own)
    bias_oth = swap_chip(bias_pack)
    ow_oth = swap_chip(out_weight)
    fc_oth = swap_chip(fc_weight)
    pw_oth = swap_chip(proj_weight)
    c_oth = swap_core(cotangent)

    def col(pack):
        return pack[:, : 3 * local].astype(F32).reshape(3 * local, 1)

    def fcb(pack):
        return pack[:, 3 * local :].astype(F32)

    act_bytes = rows * width * 4
    first = call(norm_first, [((rows, width), BF16)], 4, smem=1, nbytes=act_bytes)(
        tie_sets, tokens, norm_gain[0], norm_bias[0]
    )[0]
    first_oth = swap_core(first)

    block = min(256, span)
    att_flops = 2 * 2 * rows * width * 4 * local + heads * 4 * span * span * HD * 4
    saved = [((3, heads, HD, span), BF16), ((heads, 1, span), F32), ((heads, HD, span), BF16)]
    k_scr = [pltpu.VMEM((heads, span, HD), BF16)]

    def forward(first_call, w, b, ow, prev=()):
        outs = saved + [((rows, width), F32), ((rows, width), F32 if first_call else BF16)]
        return call(
            lambda *r: attn_forward(first_call, block, *r),
            outs,
            6 + len(prev),
            smem=1,
            scratch=k_scr,
            flops=att_flops,
            nbytes=8 * act_bytes,
        )(lengths, first, first_oth, w, b, ow, *prev)

    qkv_a, lse_a, att_a, br_own, br_oth = forward(True, w_own, col(bias_pack), out_weight)
    w_oth, bias_oth, ow_oth = (after(v, br_own) for v in (w_oth, bias_oth, ow_oth))
    qkv_b, lse_b, att_b, br_own, br_oth = forward(False, w_oth, col(bias_oth), ow_oth, (br_own, br_oth))
    br_in = swap_core(br_oth)
    middle, second = call(norm_second, [((rows, width), F32), ((rows, width), BF16)], 7, smem=1, nbytes=3 * act_bytes)(
        tie_sets, tokens, br_own, br_in, out_bias.astype(F32).reshape(1, width), norm_gain[1], norm_bias[1]
    )
    second_oth = swap_core(second)
    gf_a, gp_a, gfb_a, fe_own, fe_oth, ds_own, ds_oth = mlp(
        True, second, second_oth, cotangent, c_oth, fc_weight, fcb(bias_pack), proj_weight
    )
    fc_oth, pw_oth = (after(v, fe_own) for v in (fc_oth, pw_oth))
    gf_b, gp_b, gfb_b, fe_own, fe_oth, ds_own, ds_oth = mlp(
        False, second, second_oth, cotangent, c_oth, fc_oth, fcb(bias_oth), pw_oth, (fe_own, fe_oth, ds_own, ds_oth)
    )
    ds_in = swap_core(ds_oth)
    fe_in = swap_core(fe_oth)
    block_out, dmid, dlow, small_two = call(
        back_second,
        [((rows, width), BF16), ((rows, width), F32), ((rows, width), BF16), ((8, width), F32)],
        9,
        smem=1,
        nbytes=6 * act_bytes,
    )(tie_sets, middle, fe_own, fe_in, proj_bias.astype(F32).reshape(1, width), ds_own, ds_in, cotangent, norm_gain[1])
    dlow_oth = swap_core(dlow)

    def backward(first_call, qkv, lse, att, w, ow, prev=()):
        outs = [
            ((4 * local, width), BF16),
            ((8, width), F32),
            ((rows, width), F32),
            ((rows, width), F32 if first_call else BF16),
        ]
        n = pltpu.VMEM((heads, span, HD), BF16)
        tr = pltpu.VMEM((heads, HD, span), BF16)
        one = pltpu.VMEM((span, HD), BF16)
        acc = pltpu.VMEM((span, HD), F32)
        return call(
            lambda *r: attn_backward(first_call, block, *r),
            outs,
            10 + len(prev),
            smem=1,
            scratch=[n, tr, one, one, one, pltpu.VMEM((3, heads, HD, span), BF16), acc, acc],
            flops=3 * att_flops,
            nbytes=12 * act_bytes,
        )(lengths, qkv, lse, att, dlow, dlow_oth, first, first_oth, w, ow, *prev)

    gq_b, gqb_b, df_own, df_oth = backward(True, qkv_b, lse_b, att_b, w_oth, ow_oth)
    gq_a, gqb_a, df_own, df_oth = backward(False, qkv_a, lse_a, att_a, w_own, out_weight, (df_own, df_oth))
    df_in = swap_core(df_oth)
    grad_input, small_one = call(back_first, [((rows, width), BF16), ((8, width), F32)], 6, smem=1, nbytes=4 * act_bytes)(
        tie_sets, tokens, df_own, df_in, dmid, norm_gain[0]
    )
    def total(own, other):
        return lax.psum((own.astype(F32) + swap_chip(other).astype(F32)).astype(BF16), "dp")

    g_p, g_f, g_q = total(gp_a, gp_b), total(gf_a, gf_b), total(gq_a, gq_b)
    bias_a = jnp.concatenate([gqb_a[:1], gfb_a], axis=0)
    bias_b = jnp.concatenate([gqb_b[:1], gfb_b], axis=0)
    pack = jnp.concatenate(
        [
            lax.psum(jnp.concatenate([small_two, small_one], axis=0), ("dp", "tensor")),
            lax.psum(bias_a + swap_chip(bias_b), "dp"),
        ],
        axis=0,
    )
    return block_out, grad_input, g_p, g_f, g_q, pack


def body(
    tokens,
    cotangent,
    lengths,
    tie_sets,
    qkv_weight,
    qkv_bias,
    out_weight,
    out_bias,
    fc_weight,
    fc_bias,
    proj_weight,
    proj_bias,
    norm_gain,
    norm_bias,
):
    rows, width = tokens.shape
    groups = lax.axis_size("tensor")
    local = qkv_weight.shape[2]
    heads = local // HD
    hidden = fc_weight.shape[1]
    span = rows * groups // lengths.shape[0]
    assert groups == 4 and span == 2 * rows
    set_count = norm_gain.shape[1]
    dps = lax.axis_size("dp")

    if dps == 8:
        w = qkv_weight.transpose(1, 2, 0).reshape(3 * local, width)
        parts = block_call(
            lengths,
            tie_sets,
            tokens,
            cotangent,
            w,
            out_weight,
            fc_weight,
            proj_weight,
            qkv_bias,
            fc_bias,
            out_bias,
            proj_bias,
            norm_gain,
            norm_bias,
        )
        outs = finish(parts, local, set_count)
        return (*outs[:2], outs[2].reshape(3, local, width).transpose(2, 0, 1), *outs[3:])
    block_out, grad_input, g_p, g_f, g_q, pack = generic(
        tokens,
        cotangent,
        lengths,
        tie_sets,
        qkv_weight,
        qkv_bias,
        out_weight,
        out_bias,
        fc_weight,
        fc_bias,
        proj_weight,
        proj_bias,
        norm_gain,
        norm_bias,
    )
    gains = jnp.stack([pack[8 : 8 + set_count], pack[2 : 2 + set_count]])
    biases = jnp.stack([pack[8 + set_count : 8 + 2 * set_count], pack[2 + set_count : 2 + 2 * set_count]])
    gqb = pack[16, : 3 * local].reshape(3, local)
    return (
        block_out,
        grad_input,
        g_q[: 3 * local].astype(F32).reshape(3, local, width).transpose(2, 0, 1),
        jnp.stack([gqb[0], gqb[2]]),
        g_q[3 * local :].astype(F32),
        pack[0],
        g_f.astype(F32),
        pack[17],
        g_p.astype(F32),
        pack[1],
        gains,
        biases,
    )


def solution(mesh):
    in_specs = (
        P(("dp", "tensor"), None),
        P(("dp", "tensor"), None),
        P("dp"),
        P("dp"),
        P(None, None, "tensor"),
        P(None, "tensor"),
        P("tensor", None),
        P(),
        P(None, "tensor"),
        P("tensor"),
        P("tensor", None),
        P(),
        P(),
        P(),
    )
    out_specs = (
        P(("dp", "tensor"), None),
        P(("dp", "tensor"), None),
        P(None, None, "tensor"),
        P(None, "tensor"),
        P("tensor", None),
        P(),
        P(None, "tensor"),
        P("tensor"),
        P("tensor", None),
        P(),
        P(),
        P(),
    )
    return jax.shard_map(body, mesh=mesh, in_specs=in_specs, out_specs=out_specs, check_vma=False)
```

```python
import jax
import jax.numpy as jnp
from jax import lax
from jax.experimental import pallas as pl
from jax.experimental.pallas import tpu as pltpu
from jax.sharding import PartitionSpec as P

HD = 64
EPS = 1e-05
F32 = jnp.float32
BF16 = jnp.bfloat16
GELU_K = 0.7978845608028654
GELU_C = 0.044715
VMEM = pl.BlockSpec(memory_space=pltpu.VMEM)
SMEM = pl.BlockSpec(memory_space=pltpu.SMEM)
NT = (((1,), (1,)), ((), ()))
TN = (((0,), (0,)), ((), ()))


def dg(a, b, dims):
    return lax.dot_general(a, b, dims, preferred_element_type=F32)


def mm(a, b):
    return jnp.dot(a, b, preferred_element_type=F32)


def call(kernel, outs, n_in, smem=0, scratch=(), limit=48, flops=0, nbytes=0):
    return pl.pallas_call(
        kernel,
        out_shape=[jax.ShapeDtypeStruct(s, d) for s, d in outs],
        in_specs=[SMEM] * smem + [VMEM] * (n_in - smem),
        out_specs=[VMEM] * len(outs),
        scratch_shapes=list(scratch),
        cost_estimate=pl.CostEstimate(flops=flops, bytes_accessed=nbytes, transcendentals=0),
        compiler_params=pltpu.CompilerParams(vmem_limit_bytes=limit << 20),
    )


def place():
    t = lax.axis_index("tensor")
    return t % 2, t // 2


def stats(v):
    mean = jnp.mean(v, axis=-1, keepdims=True)
    cent = v - mean
    var = jnp.mean(cent * cent, axis=-1, keepdims=True)
    r = lax.rsqrt(var + EPS)
    return cent * r, r


def norm_first(sets, x, gain, bias, out):
    k = sets[place()[1]]
    xhat, _ = stats(x[...].astype(F32))
    out[...] = (xhat * gain[pl.ds(k, 1), :] + bias[pl.ds(k, 1), :]).astype(BF16)


def norm_second(sets, x, br, br_in, ob, gain, bias, middle, out):
    k = sets[place()[1]]
    mid = x[...].astype(F32) + (br[...] + br_in[...].astype(F32)) + ob[...]
    middle[...] = mid
    xhat, _ = stats(mid)
    out[...] = (xhat * gain[pl.ds(k, 1), :] + bias[pl.ds(k, 1), :]).astype(BF16)


def norm_pull(v, d, gain):
    xhat, r = stats(v)
    e = d * gain
    m1 = jnp.mean(e, axis=-1, keepdims=True)
    m2 = jnp.mean(e * xhat, axis=-1, keepdims=True)
    return r * (e - m1 - xhat * m2), jnp.sum(d * xhat, axis=0, keepdims=True), jnp.sum(d, axis=0, keepdims=True)


def split_sets(small, at, k, count, gg, gb):
    for i in range(count):
        mine = (k == i).astype(F32)
        small[at + i : at + i + 1, :] = gg * mine
        small[at + count + i : at + count + i + 1, :] = gb * mine
    end = at + 2 * count
    small[end:, :] = jnp.zeros((small.shape[0] - end, small.shape[1]), F32)


def back_second(sets, middle, feed, feed_in, pb, ds, ds_in, ct, gain, block_out, dmid, dlow, small):
    k = sets[place()[1]]
    mid = middle[...]
    block_out[...] = (mid + (feed[...] + feed_in[...].astype(F32)) + pb[...]).astype(BF16)
    d, gg, gb = norm_pull(mid, ds[...] + ds_in[...].astype(F32), gain[pl.ds(k, 1), :])
    c = ct[...].astype(F32)
    d = d + c
    dmid[...] = d
    dlow[...] = d.astype(BF16)
    small[0:1, :] = jnp.sum(d, axis=0, keepdims=True)
    small[1:2, :] = jnp.sum(c, axis=0, keepdims=True)
    split_sets(small, 2, k, gain.shape[0], gg, gb)


def back_first(sets, x, df, df_in, dmid, gain, grad_in, small):
    k = sets[place()[1]]
    d, gg, gb = norm_pull(x[...].astype(F32), df[...] + df_in[...].astype(F32), gain[pl.ds(k, 1), :])
    grad_in[...] = (d + dmid[...]).astype(BF16)
    split_sets(small, 0, k, gain.shape[0], gg, gb)


def mask_scores(scores, start, length):
    span, count = scores.shape
    kpos = lax.broadcasted_iota(jnp.int32, (span, count), 0)
    limit = jnp.minimum(start + lax.broadcasted_iota(jnp.int32, (1, count), 1), length - 1)
    return jnp.where(kpos <= limit, scores, -1e30)


def attn_forward(first_call, block, lengths, x_own, x_oth, w, b, ow, *rest):
    if first_call:
        qkv, lse, att, br_own, br_oth, k_s = rest
    else:
        pr_own, pr_oth, qkv, lse, att, br_own, br_oth, k_s = rest
    c, seq = place()
    length = lengths[seq]
    rows = x_own.shape[0]
    local = w.shape[0] // 3
    heads = local // HD
    span = 2 * rows
    parts = ((x_own, c), (x_oth, 1 - c))
    for x, p in parts:
        at = pl.ds(pl.multiple_of(p * rows, rows), rows)
        y = dg(w[...], x[...], NT) + b[...]
        for h in range(heads):
            lo = h * HD
            qkv[0, h, :, at] = (y[lo : lo + HD] * 0.125).astype(BF16)
            kt = y[local + lo : local + lo + HD]
            qkv[1, h, :, at] = kt.astype(BF16)
            k_s[h, at, :] = kt.T.astype(BF16)
            qkv[2, h, :, at] = y[2 * local + lo : 2 * local + lo + HD].astype(BF16)

    def head(h, carry):
        for i in range(span // block):
            stop = (i + 1) * block
            cols = slice(i * block, stop)
            scores = mm(k_s[h, :stop, :], qkv[0, h, :, cols])
            scores = mask_scores(scores, i * block, length)
            top = jnp.max(scores, axis=0, keepdims=True)
            e = jnp.exp(scores - top)
            total = jnp.sum(e, axis=0, keepdims=True)
            probs = (e * (1.0 / total)).astype(BF16)
            att[h, :, cols] = mm(qkv[2, h, :, :stop], probs).astype(BF16)
            lse[h, :, cols] = top + jnp.log(total)
        return carry

    lax.fori_loop(0, heads, head, 0)
    for (x, p), prev, out in zip(parts, (None, None) if first_call else (pr_own, pr_oth), (br_own, br_oth)):
        at = pl.ds(pl.multiple_of(p * rows, rows), rows)
        a = att[:, :, at].reshape(local, rows)
        r = dg(a, ow[...], TN)
        if prev is not None:
            r = r + prev[...]
        out[...] = r.astype(out.dtype)


def attn_backward(first_call, block, lengths, qkv, lse, att, d_own, d_oth, x_own, x_oth, w, ow, *rest):
    if first_call:
        gq, gb, f_own, f_oth, do_n, do_t, q_n, k_n, v_n, dqkv, dk, dv = rest
    else:
        pf_own, pf_oth, gq, gb, f_own, f_oth, do_n, do_t, q_n, k_n, v_n, dqkv, dk, dv = rest
    c, seq = place()
    length = lengths[seq]
    rows = x_own.shape[0]
    local = w.shape[0] // 3
    heads = local // HD
    span = 2 * rows
    spots = [pl.ds(pl.multiple_of(p * rows, rows), rows) for p in (c, 1 - c)]
    gout = None
    for d, at in zip((d_own, d_oth), spots):
        y = dg(ow[...], d[...], NT)
        for h in range(heads):
            part = y[h * HD : h * HD + HD]
            do_t[h, :, at] = part.astype(BF16)
            do_n[h, at, :] = part.T.astype(BF16)
        a = att[:, :, at].reshape(local, rows)
        term = mm(a, d[...])
        gout = term if gout is None else gout + term
    gq[3 * local :, :] = gout.astype(gq.dtype)

    def head(h, carry):
        q_n[...] = qkv[0, h].astype(F32).T.astype(BF16)
        k_n[...] = qkv[1, h].astype(F32).T.astype(BF16)
        v_n[...] = qkv[2, h].astype(F32).T.astype(BF16)
        for i in range(span // block):
            stop = (i + 1) * block
            cols = slice(i * block, stop)
            scores = mm(k_n[:stop, :], qkv[0, h, :, cols])
            scores = mask_scores(scores, i * block, length)
            probs = jnp.exp(scores - lse[h, :, cols])
            dp = mm(v_n[:stop, :], do_t[h, :, cols])
            total = jnp.sum(probs * dp, axis=0, keepdims=True)
            ds = (probs * (dp - total)).astype(BF16)
            dqkv[0, h, :, cols] = (mm(qkv[1, h, :, :stop], ds) * 0.125).astype(BF16)
            pv = mm(probs.astype(BF16), do_n[h, cols, :])
            pk = mm(ds, q_n[cols, :])
            last = i * block
            if i:
                dv[:last, :] += pv[:last]
                dk[:last, :] += pk[:last]
            dv[last:stop, :] = pv[last:]
            dk[last:stop, :] = pk[last:]
        dqkv[1, h] = dk[...].T.astype(BF16)
        dqkv[2, h] = dv[...].T.astype(BF16)
        return carry

    lax.fori_loop(0, heads, head, 0)
    gqkv = None
    gbias = None
    for x, at, prev, out in zip((x_own, x_oth), spots, (None, None) if first_call else (pf_own, pf_oth), (f_own, f_oth)):
        d = dqkv[:, :, :, at].reshape(3 * local, rows)
        term = mm(d, x[...])
        gqkv = term if gqkv is None else gqkv + term
        s = dg(jnp.ones((8, rows), BF16), d, NT)
        gbias = s if gbias is None else gbias + s
        r = dg(d, w[...], TN)
        if prev is not None:
            r = r + prev[...]
        out[...] = r.astype(out.dtype)
    gq[: 3 * local, :] = gqkv.astype(gq.dtype)
    gb[...] = jnp.zeros_like(gb)
    gb[:, : 3 * local] = gbias


def mlp_kernel(first_call, s_own, s_oth, c_own, c_oth, fc, fb, pw, *rest):
    if first_call:
        gf, gp, gb, fe_own, fe_oth, ds_own, ds_oth, st = rest
        prev = (None, None, None, None)
    else:
        prev = rest[:4]
        gf, gp, gb, fe_own, fe_oth, ds_own, ds_oth, st = rest[4:12]
        accs = rest[12:]
    j = pl.program_id(0)
    rows = s_own.shape[0]

    @pl.when(j == 0)
    def _():
        st[:, :rows] = s_own[...].T
        st[:, rows:] = s_oth[...].T

    gfc = gproj = gbias = None
    for n, (s, ct, fe, ds) in enumerate(((s_own, c_own, fe_own, ds_own), (s_oth, c_oth, fe_oth, ds_oth))):
        pre = mm(s[...], fc[...]) + fb[...]
        sq = pre * pre
        t = jnp.tanh(GELU_K * (pre + GELU_C * sq * pre))
        half = 0.5 * (1.0 + t)
        act = (pre * half).astype(BF16)
        slope = half + (0.5 * GELU_K) * pre * (1.0 - t * t) * (1.0 + (3.0 * GELU_C) * sq)
        dpre = dg(ct[...], pw[...], NT) * slope
        low = dpre.astype(BF16)
        bs = jnp.sum(low.astype(F32), axis=0, keepdims=True)
        tf = mm(st[:, n * rows : (n + 1) * rows], low)
        tp = dg(act, ct[...], TN)
        gfc = tf if gfc is None else gfc + tf
        gproj = tp if gproj is None else gproj + tp
        gbias = bs if gbias is None else gbias + bs
        add_f = mm(act, pw[...])
        add_s = dg(low, fc[...], NT)
        if first_call:
            fa, sa, pf, ps = fe, ds, None, None
        else:
            fa, sa = accs[2 * n], accs[2 * n + 1]
            pf, ps = prev[n], prev[2 + n]

        @pl.when(j == 0)
        def _():
            fa[...] = add_f if pf is None else add_f + pf[...]
            sa[...] = add_s if ps is None else add_s + ps[...]

        @pl.when(j > 0)
        def _():
            fa[...] += add_f
            sa[...] += add_s

        if not first_call:
            @pl.when(j == pl.num_programs(0) - 1)
            def _():
                fe[...] = fa[...].astype(fe.dtype)
                ds[...] = sa[...].astype(ds.dtype)

    gf[...] = gfc.astype(gf.dtype)
    gp[...] = gproj.astype(gp.dtype)
    gb[...] = gbias


def mlp(first_call, s_own, s_oth, c_own, c_oth, fc, fb, pw, prev=()):
    rows, width = s_own.shape
    hidden = fc.shape[1]
    hb = 256
    fixed = pl.BlockSpec((rows, width), lambda j: (0, 0))
    oth = F32 if first_call else BF16
    sums = [(rows, width)] * 4
    scratch = [pltpu.VMEM((width, 2 * rows), BF16)]
    if not first_call:
        scratch += [pltpu.VMEM(s, F32) for s in sums]
    return pl.pallas_call(
        lambda *r: mlp_kernel(first_call, *r),
        grid=(hidden // hb,),
        in_specs=[fixed] * 4
        + [
            pl.BlockSpec((width, hb), lambda j: (0, j)),
            pl.BlockSpec((1, hb), lambda j: (0, j)),
            pl.BlockSpec((hb, width), lambda j: (j, 0)),
        ]
        + [fixed] * len(prev),
        out_specs=[
            pl.BlockSpec((width, hb), lambda j: (0, j)),
            pl.BlockSpec((hb, width), lambda j: (j, 0)),
            pl.BlockSpec((1, hb), lambda j: (0, j)),
        ]
        + [fixed] * 4,
        out_shape=[
            jax.ShapeDtypeStruct((width, hidden), BF16),
            jax.ShapeDtypeStruct((hidden, width), BF16),
            jax.ShapeDtypeStruct((1, hidden), F32),
            jax.ShapeDtypeStruct((rows, width), F32),
            jax.ShapeDtypeStruct((rows, width), oth),
            jax.ShapeDtypeStruct((rows, width), F32),
            jax.ShapeDtypeStruct((rows, width), oth),
        ],
        scratch_shapes=scratch,
        cost_estimate=pl.CostEstimate(flops=24 * rows * width * hidden, bytes_accessed=20 * rows * width, transcendentals=0),
        compiler_params=pltpu.CompilerParams(vmem_limit_bytes=56 << 20),
    )(s_own, s_oth, c_own, c_oth, fc, fb, pw, *prev)


def partners():
    t, d = lax.axis_index("tensor"), lax.axis_index("dp")
    bits = {"x": d % 2, "1": (d // 2) % 2, "2": d // 4}
    to = {
        "c": {"tensor": t + 1 - 2 * (t % 2)},
        "y": {"tensor": (t + 2) % 4},
        "x": {"dp": d + 1 - 2 * bits["x"]},
        "1": {"dp": d + 2 - 4 * bits["1"]},
        "2": {"dp": (d + 4) % 8},
        "3": {"dp": (d + 4) % 8 + 2 - 4 * bits["1"]},
    }
    return to, bits


def remote(src, dst, send, recv, where):
    return pltpu.make_async_remote_copy(
        src_ref=src, dst_ref=dst, send_sem=send, recv_sem=recv, device_id=where, device_id_type=pl.DeviceIdType.MESH
    )


def aligned(start, n, by=16):
    return pl.ds(pl.multiple_of(start, by), n)


class Flow:
    def __init__(self, own, oth, res, buf, outs, order, to, bits, sems):
        self.acts, self.outs = [], [pltpu.make_async_copy(res.at[src], out, sems(None)) for src, out in outs]
        base, n, at, both = 0, own.shape[0], 0, True
        back, waits, adds, slot = [], [], [], 0
        for k, o in enumerate(order):
            copies, sums = [], []
            last = k == len(order) - 1
            if o == "y":
                here = aligned(base, n)
                got = buf.at[aligned(at, n)]
                at += n
                copies.append(remote(oth.at[here], got, *sems(slot), to[o]))
                sums.append(((res if last else own).at[here], own.at[here], [got]))
                slot += 1
                both = False
            elif o == "e":
                here = aligned(base, n)
                got = buf.at[aligned(at, n)]
                copies.append(remote(own.at[here], got, *sems(slot), to["2"]))
                sums.append((res.at[here], own.at[here], [got]))
                slot += 1
            else:
                size = n // 4 if o == "Z" else n // 2
                back.append((o, base, size))
                mine = bits["1"] + 2 * bits["2"] if o == "Z" else bits[o]
                keep = aligned(base + mine * size, size)
                for ref in (own, oth) if both else (own,):
                    gots = []
                    for peer in "123" if o == "Z" else o:
                        other = zs(bits, peer) if o == "Z" else 1 - mine
                        got = buf.at[aligned(at, size)]
                        at += size
                        copies.append(remote(ref.at[aligned(base + other * size, size)], got, *sems(slot), to[peer]))
                        gots.append(got)
                        slot += 1
                    sums.append(((res if last else ref).at[keep], ref.at[keep], gots))
                base, n = base + mine * size, size
            if k == 0 and both:
                self.acts += [([], [], copies[:1]), ([], [], copies[1:])]
            else:
                self.acts.append((waits, adds, copies))
            waits, adds = copies, sums
        for o, start, size in reversed(back):
            here = res.at[aligned(base, n)]
            copies = []
            for peer in "123" if o == "Z" else o:
                copies.append(remote(here, here, *sems(slot), to[peer]))
                slot += 1
            self.acts.append((waits, adds, copies))
            waits, adds = copies, []
            base, n = start, size * (4 if o == "Z" else 2)
        self.acts.append((waits, adds, self.outs))

    def step(self, k):
        waits, adds, starts = self.acts[k]
        for copy in waits:
            copy.wait()
        for dst, mine, gots in adds:
            total = mine[...].astype(F32)
            for got in gots:
                total = total + got[...].astype(F32)
            dst[...] = total.astype(BF16)
        for copy in starts:
            copy.start()


def zs(bits, peer):
    one = 1 - bits["1"] if peer in "13" else bits["1"]
    two = 1 - bits["2"] if peer in "23" else bits["2"]
    return one + 2 * two


def pick(gains, chosen):
    row = gains[0:1, :]
    for i in range(1, gains.shape[0]):
        row = jnp.where(chosen == i, gains[i : i + 1, :], row)
    return row


def block_kernel(*refs):
    (lengths, sets, tok_h, ct_h, w_h, ow_h, fc_h, pw_h, qkv_b, fc_b, ob, pb, gains, biases) = refs[:14]
    out_h, in_h, o_p, o_f, o_q, o_o, pack = refs[14:21]
    (tok, ct, ct_oth, first, first_oth, w, ow, fc, pw, bias, qkv, lse, att, nat, trn) = refs[21:36]
    (give, fe_send, br_in, middle, second, second_oth, st, acc, ds_in, fe_in) = refs[36:46]
    (dlow_oth, q_n, k_n, v_n, dqkv, dk, dv, df_in, q_t, block_out, grad_in) = refs[46:57]
    (grad, res, buf, fbg, r_pack, load, sends, recvs, wsend, wrecv, done) = refs[57:]
    dlow = second
    block, wide = 256, 512
    to, bits = partners()
    c, seq = place()
    length, chosen = lengths[seq], sets[seq]
    rows, width = tok.shape
    local = ow.shape[1]
    heads = local // HD
    span = 2 * rows
    hidden = fc.shape[2]
    blocks = hidden // block
    spots = [pl.ds(pl.multiple_of(p * rows, rows), rows) for p in (c, 1 - c)]

    loads = {}
    for name, src, dst in (
        ("tok", tok_h, tok),
        ("w", w_h, w.at[0]),
        ("ow", ow_h, ow.at[0]),
        ("ct", ct_h, ct),
        ("fc", fc_h, fc.at[0]),
        ("pw", pw_h, pw.at[0]),
    ):
        loads[name] = pltpu.make_async_copy(src, dst, load.at[len(loads)])
        loads[name].start()

    bias[0] = jnp.zeros(bias.shape[1:], BF16)
    bias[1, 8:] = jnp.zeros((8, bias.shape[2]), BF16)
    edge = hidden + 256
    bias[0, 0:1, :hidden] = fc_b[...].reshape(1, hidden)
    bias[0, 0:1, hidden : hidden + local] = qkv_b[0:1, :]
    bias[0, 0:1, edge : edge + local] = qkv_b[1:2, :]

    barrier = pltpu.get_barrier_semaphore()
    for where in to.values():
        pl.semaphore_signal(barrier, inc=1, device_id=where, device_id_type=pl.DeviceIdType.MESH)
    pl.semaphore_wait(barrier, len(to))

    bias_copy = remote(bias.at[0, :8], bias.at[1, :8], wsend.at[0], wrecv.at[0], to["y"])
    pieces = []
    for src, dst, start, n in (
        (w_h, w, 0, local),
        (w_h, w, local, local),
        (w_h, w, 2 * local, local),
        (ow_h, ow, 0, local),
        (fc_h, fc, 0, width // 2),
        (fc_h, fc, width // 2, width // 2),
        (pw_h, pw, 0, hidden // 2),
        (pw_h, pw, hidden // 2, hidden // 2),
    ):
        k = 1 + 4 * len(pieces)
        first_way, last_way = ("1", "x") if len(pieces) % 2 else ("x", "1")

        def quarter(x, z, start=start, n=n):
            return aligned(start + (2 * z + x) * (n // 4), n // 4, 8)

        mine = quarter(bits["x"], bits["1"])
        there = dst.at[1, mine]
        got = quarter(1 - bits["x"], bits["1"]) if first_way == "x" else quarter(bits["x"], 1 - bits["1"])
        over = remote(src.at[mine], there, wsend.at[k], wrecv.at[k], to["y"])
        one = remote(there, there, wsend.at[k + 1], wrecv.at[k + 1], to[first_way])
        two = remote(there, there, wsend.at[k + 2], wrecv.at[k + 2], to[last_way])
        rest = remote(dst.at[1, got], dst.at[1, got], wsend.at[k + 3], wrecv.at[k + 3], to[last_way])
        pieces.append((over, [one, two], [one], [rest], [two, rest]))
    for i, (over, *_) in enumerate(pieces):
        over.start()
        if i == 2:
            bias_copy.start()

    def forward(acts):
        for i, act in acts:
            over, on, waits, starts, ends = pieces[i]
            if act == 0:
                waits, starts = [over], on
            elif act == 2:
                waits, starts = ends, []
            for copy in waits:
                copy.wait()
            for copy in starts:
                copy.start()

    flows = []
    n_flow = 9
    for f in range(n_flow):
        unit, j = f // 3, f % 3
        part = (slice(None), slice(j * block, (j + 1) * block)) if unit == 1 else (slice(j * block, (j + 1) * block),)
        if unit < 2:
            outs = [((slice(None),), (o_p, o_f)[unit].at[part])]
        else:
            outs = [((slice(n * HD, (n + 1) * HD),), o_q.at[pl.ds(n * local + j * HD, HD)]) for n in range(3)]
            outs.append(((slice(3 * HD, 4 * HD),), o_o.at[pl.ds(j * HD, HD)]))
        room = (slice(None), part[1]) if unit == 1 else (slice(j * 2 * block, (j + 1) * 2 * block),)

        def sems(k, f=f):
            return done.at[f] if k is None else (sends.at[f, k], recvs.at[f, k])

        flows.append(
            Flow(
                grad.at[(0, unit, *part)],
                grad.at[(1, unit, *part)],
                res.at[(unit, *part)],
                buf.at[(unit, *room)],
                outs,
                ORDERS[f],
                to,
                bits,
                sems,
            )
        )

    def swap(n, src, dst):
        return remote(src, dst, sends.at[n_flow, n], recvs.at[n_flow, n], to["c"])

    small_order = "cyx12"
    small_copies = [
        remote(pack, r_pack.at[n], sends.at[n_flow + 1, n], recvs.at[n_flow + 1, n], to[o]) for n, o in enumerate(small_order)
    ]

    def small(n):
        if n:
            small_copies[n - 1].wait()
            got = r_pack[n - 1]
            mid = pack[16:24, :]
            if n == 2:
                mid = mid + got[24:]
            elif n > 2:
                mid = mid + got[16:24]
            pack[:16, :] = pack[:16, :] + got[:16]
            pack[16:24, :] = mid
        if n < len(small_order):
            small_copies[n].start()

    def run(events):
        for f, k in events:
            if f < 0:
                small(k)
            else:
                flows[f].step(k)

    def at_step(i, table, what):
        for n, some in enumerate(table):
            if some:

                @pl.when(i == n)
                def _():
                    what(some)

    tile = 256

    def by_rows(step, carry=0, copies=()):
        def one(i, held):
            held = step(pl.multiple_of(i * tile, tile), held)
            for n, copy in enumerate(copies):
                pl.when(i == n)(copy.start)
            return held

        return lax.fori_loop(0, rows // tile, one, carry)

    def swap_tiles(n, src, dst):
        parts = [pl.ds(t * tile, tile) for t in range(rows // tile)]
        pairs = [(sends.at[n_flow, n + 8 * t], recvs.at[n_flow, n + 8 * t]) for t in range(len(parts))]
        return [remote(src.at[r], dst.at[r], *pair, to["c"]) for r, pair in zip(parts, pairs)]

    def wait_all(copies):
        for copy in copies:
            copy.wait()

    def norm(n, v):
        return (stats(v)[0] * pick(gains[n], chosen) + pick(biases[n], chosen)).astype(BF16)

    zero = jnp.zeros((1, width), F32)

    loads["tok"].wait()

    def norm_tokens(r, carry):
        r = pl.ds(r, tile)
        first[r] = norm(0, tok[r].astype(F32))
        return carry

    first_swap = swap_tiles(0, first, first_oth)
    by_rows(norm_tokens, copies=first_swap)
    loads["ct"].wait()
    ct_swap = swap(1, ct, ct_oth)
    ct_swap.start()
    loads["w"].wait()

    q_t[HD:, :] = (lax.broadcasted_iota(jnp.int32, (HD, span), 0) == 0).astype(BF16)
    true_key = lax.broadcasted_iota(jnp.int32, (span, HD), 0) < length
    key_lane = lax.broadcasted_iota(jnp.int32, (span, HD), 1) == 0
    key_mask = jnp.where(true_key, 0.0, jnp.where(key_lane, -1e30, 0.0)).astype(BF16)
    for h in range(heads):
        nat[0, h, :, HD:] = key_mask
    k_n[:, HD:] = key_mask
    later = lax.broadcasted_iota(jnp.int32, (wide, wide), 0) > lax.broadcasted_iota(jnp.int32, (wide, wide), 1)

    def scores(keys, last, stop):
        cols = slice(last, stop)
        same = jnp.where(later, -1e30, mm(keys(cols), q_t[:, cols]))
        return [mm(keys(slice(0, last)), q_t[:, cols]), same] if last else [same]

    pick_row = (lax.broadcasted_iota(jnp.int32, (16, rows), 0) == 0).astype(BF16)

    def attend(s, carry):
        @pl.when(s == 1)
        def _():
            forward(FORWARD_SECOND)
            bias_copy.wait()

        q_col = dg(bias[s, :, hidden : hidden + local], pick_row, TN)
        v_col = dg(bias[s, :, edge : edge + local], pick_row, TN)
        for n, (x, at) in enumerate(zip((first, first_oth), spots)):
            if n:

                @pl.when(s == 0)
                def _():
                    wait_all(first_swap)

            y = dg(w[s], x[...], NT)
            for h in range(heads):
                lo = h * HD
                qkv[s, 0, h, :, at] = ((y[lo : lo + HD] + q_col[lo : lo + HD]) * 0.125).astype(BF16)
                kt = y[local + lo : local + lo + HD]
                qkv[s, 1, h, :, at] = kt.astype(BF16)
                nat[0, h, at, :HD] = kt.T.astype(BF16)
                vt = y[2 * local + lo : 2 * local + lo + HD]
                qkv[s, 2, h, :, at] = (vt + v_col[lo : lo + HD]).astype(BF16)
            at_step(s, FORWARD_ROWS[n], forward)

        def head(h, carry):
            q_t[:HD, :] = qkv[s, 0, h]
            for i in range(span // wide):
                last, stop = i * wide, (i + 1) * wide
                cols = slice(last, stop)
                parts = scores(lambda rows: nat[0, h, rows, :], last, stop)
                top = parts[-1].max(axis=0, keepdims=True)
                if i:
                    top = jnp.maximum(top, parts[0].max(axis=0, keepdims=True))
                total = out = None
                for v, keys in zip(parts, (slice(0, last), cols) if i else (cols,)):
                    e = jnp.exp(v - top)
                    add = jnp.sum(e, axis=0, keepdims=True)
                    term = mm(qkv[s, 2, h, :, keys], e.astype(BF16))
                    total = add if total is None else total + add
                    out = term if out is None else out + term
                att[s, h, :, cols] = (out * (1.0 / total)).astype(BF16)
                lse[s, h, :, cols] = top + jnp.log(total)
            at_step(s * heads + h, FORWARD_HEADS, forward)
            return carry

        lax.fori_loop(0, heads, head, 0, unroll=True)
        return carry

    lax.fori_loop(0, 2, attend, 0)
    loads["ow"].wait()
    forward(FORWARD_PROJECT)

    def project(p, r):
        at = pl.ds(pl.multiple_of(p * rows + r, tile), tile)
        return dg(att[0, :, :, at].reshape(local, tile), ow[0], TN) + dg(att[1, :, :, at].reshape(local, tile), ow[1], TN)

    def project_other(r, carry):
        give[pl.ds(r, tile)] = project(1 - c, r).astype(BF16)
        return carry

    br_swap = swap_tiles(2, give, br_in)
    by_rows(project_other, copies=br_swap)

    def project_own(r, carry):
        middle[pl.ds(r, tile)] = tok[pl.ds(r, tile)].astype(F32) + ob[...].astype(F32).reshape(1, width) + project(c, r)
        return carry

    by_rows(project_own)
    forward(FORWARD_MIDDLE)
    wait_all(br_swap)

    def norm_middle(r, carry):
        r = pl.ds(r, tile)
        mid = middle[r] + br_in[r].astype(F32)
        middle[r] = mid
        second[r] = norm(1, mid)
        return carry

    second_swap = swap_tiles(3, second, second_oth)
    by_rows(norm_middle, copies=second_swap)
    forward(FORWARD_NORM)
    st[:, :rows] = second[...].T
    loads["fc"].wait()
    loads["pw"].wait()

    ds_swap, fe_swap = swap(4, give, ds_in), swap(5, fe_send, fe_in)
    halves = ((second, ct), (second_oth, ct_oth))

    def units(jj, carry, turn=(1, 0)):
        s, j = jj // blocks, jj % blocks
        here = pl.ds(pl.multiple_of(j * block, block), block)

        @pl.when(jj == blocks)
        def _():
            forward(FORWARD_OTHER)

        gfc = gproj = gbias = None
        for n in turn:
            x, g = halves[n]
            if turn == (0, 1) and n:
                ct_swap.wait()
                wait_all(second_swap)
                st[:, rows:] = second_oth[...].T
            pre = mm(x[...], fc[s, :, here]) + bias[s, 0:1, here].astype(F32)
            sq = pre * pre
            t = jnp.tanh(pre * (GELU_K + (GELU_K * GELU_C) * sq))
            half = 0.5 + 0.5 * t
            full = pre * half
            act = full.astype(BF16)
            slope = half + full * (1.0 - t) * (GELU_K + (3.0 * GELU_K * GELU_C) * sq)
            low = (dg(g[...], pw[s, here, :], NT) * slope).astype(BF16)
            bs = jnp.sum(low.astype(F32), axis=0, keepdims=True)
            tf = mm(st[:, n * rows : (n + 1) * rows], low)
            tp = dg(act, g[...], TN)
            gfc = tf if gfc is None else gfc + tf
            gproj = tp if gproj is None else gproj + tp
            gbias = bs if gbias is None else gbias + bs
            add_f = mm(act, pw[s, here, :])
            add_s = dg(low, fc[s, :, here], NT)

            if turn == (0, 1):
                acc[n] = add_f
                acc[2 + n] = add_s
            else:
                acc[n] += add_f
                acc[2 + n] += add_s
            if n == 1:

                @pl.when(jj == 2 * blocks - 1)
                def _():
                    give[...] = acc[3].astype(BF16)
                    ds_swap.start()
                    fe_send[...] = acc[1].astype(BF16)
                    fe_swap.start()

            if n == turn[0]:
                at_step(jj, FORWARD_UNITS_MID, forward)
                at_step(jj, UNITS_MID, run)

        grad[s, 1, :, here] = gfc.astype(BF16)
        grad[s, 0, here, :] = gproj.astype(BF16)
        fbg[s, 0:1, here] = gbias
        at_step(jj, FORWARD_UNITS, forward)
        at_step(jj, UNITS, run)
        return carry

    units(0, 0, (0, 1))
    lax.fori_loop(1, 2 * blocks, units, 0)
    run(AFTER_UNITS)
    ds_swap.wait()
    fe_swap.wait()

    def back_middle(r, held):
        r = pl.ds(r, tile)
        mid, cot = middle[r], ct[r].astype(F32)
        block_out[r] = (mid + (acc[0, r] + fe_in[r].astype(F32)) + pb[...].astype(F32).reshape(1, width)).astype(BF16)
        d, gg, gb = norm_pull(mid, acc[2, r] + ds_in[r].astype(F32), pick(gains[1], chosen))
        d = d + cot
        middle[r] = d
        dlow[r] = d.astype(BF16)
        new = (jnp.sum(d, axis=0, keepdims=True), jnp.sum(cot, axis=0, keepdims=True), gg, gb)
        return tuple(a + b for a, b in zip(held, new))

    low_swap = swap_tiles(6, dlow, dlow_oth)
    sums = by_rows(back_middle, (zero,) * 4, low_swap)
    out_copy = pltpu.make_async_copy(block_out, out_h, load.at[0])
    out_copy.start()
    pack[0:1, :] = sums[0]
    pack[1:2, :] = sums[1]
    split_sets(pack.at[0:8], 2, chosen, gains.shape[1], sums[2], sums[3])
    run(AFTER_SECOND)

    for n, (g, at) in enumerate(zip((dlow, dlow_oth), spots)):
        if n:
            wait_all(low_swap)
        for s in range(2):
            y = dg(ow[s], g[...], NT)
            for h in range(heads):
                piece = y[h * HD : h * HD + HD]
                trn[s, h, :, at] = piece.astype(BF16)
                nat[s, h, at, :HD] = piece.T.astype(BF16)

    def pull(i, carry):
        s = h = 0
        for n, (shard, which) in enumerate(HEAD_ORDER):
            s, h = jnp.where(i == n, shard, s), jnp.where(i == n, which, h)
        q_t[:HD, :] = qkv[s, 0, h]
        q_n[...] = qkv[s, 0, h].astype(F32).T.astype(BF16)
        k_n[:, :HD] = qkv[s, 1, h].astype(F32).T.astype(BF16)
        v_n[...] = qkv[s, 2, h].astype(F32).T.astype(BF16)
        for b in range(span // wide):
            last, stop = b * wide, (b + 1) * wide
            cols = slice(last, stop)
            parts = scores(lambda rows: k_n[rows, :], last, stop)
            total = jnp.sum(att[s, h, :, cols].astype(F32) * trn[s, h, :, cols].astype(F32), axis=0, keepdims=True)
            dq = None
            for v, keys in zip(parts, (slice(0, last), cols) if b else (cols,)):
                probs = jnp.exp(v - lse[s, h, :, cols])
                ds = (probs * (mm(v_n[keys, :], trn[s, h, :, cols]) - total)).astype(BF16)
                term = mm(qkv[s, 1, h, :, keys], ds)
                dq = term if dq is None else dq + term
                pv = mm(probs.astype(BF16), nat[s, h, cols, :HD])
                pk = mm(ds, q_n[cols, :])
                if keys.stop == stop:
                    dv[keys, :] = pv
                    dk[keys, :] = pk
                else:
                    dv[keys, :] += pv
                    dk[keys, :] += pk
            dqkv[s, 0, h, :, cols] = (dq * 0.125).astype(BF16)
            if stop < span:
                at_step(i, HEADS[b], run)
        dqkv[s, 1, h] = dk[...].T.astype(BF16)
        dqkv[s, 2, h] = dv[...].T.astype(BF16)
        gq = go = None
        for x, g, at in zip((first, first_oth), (dlow, dlow_oth), spots):
            tq = mm(dqkv[s, :, h, :, at].reshape(3 * HD, rows), x[...])
            to_ = mm(att[s, h, :, at], g[...])
            gq = tq if gq is None else gq + tq
            go = to_ if go is None else go + to_
        top = pl.multiple_of(h * 4 * HD, 4 * HD)
        grad[s, 2, pl.ds(top, 3 * HD), :] = gq.astype(BF16)
        grad[s, 2, pl.ds(top + 3 * HD, HD), :] = go.astype(BF16)
        at_step(i, HEADS[-1], run)
        return carry

    lax.fori_loop(0, 2 * heads, pull, 0)

    def pull_first(p, r):
        at = pl.ds(pl.multiple_of(p * rows + r, tile), tile)
        return dg(dqkv[0, :, :, :, at].reshape(3 * local, tile), w[0], TN) + dg(
            dqkv[1, :, :, :, at].reshape(3 * local, tile), w[1], TN
        )

    def pull_other(r, carry):
        give[pl.ds(r, tile)] = pull_first(1 - c, r).astype(BF16)
        return carry

    df_swap = swap_tiles(7, give, df_in)
    by_rows(pull_other, copies=df_swap)
    run(AFTER_HEADS)

    def pull_own(r, carry):
        acc[0, pl.ds(r, tile)] = pull_first(c, r)
        return carry

    by_rows(pull_own)
    wait_all(df_swap)

    def back_tokens(r, held):
        r = pl.ds(r, tile)
        d, gg, gb = norm_pull(tok[r].astype(F32), acc[0, r] + df_in[r].astype(F32), pick(gains[0], chosen))
        grad_in[r] = (d + middle[r]).astype(BF16)
        return (held[0] + gg, held[1] + gb)

    sums = by_rows(back_tokens, (zero,) * 2)
    in_copy = pltpu.make_async_copy(grad_in, in_h, load.at[1])
    in_copy.start()
    split_sets(pack.at[8:16], 0, chosen, gains.shape[1], sums[0], sums[1])
    for s in range(2):
        at = 16 + 8 * s
        pack[at : at + 8, :] = jnp.zeros((8, width), F32)
        pack[at : at + 1, : 3 * local] = dg(jnp.ones((8, span), BF16), dqkv[s].reshape(3 * local, span), NT)[0:1]
        pack[at + 1 : at + 2, :] = fbg[s, 0:1]
    run(TAIL)
    for flow in flows:
        for out in flow.outs:
            out.wait()
    out_copy.wait()
    in_copy.wait()


FORWARD_ROWS = ([[(0, 0)], []], [[(1, 0), (2, 0), (0, 1)], [(3, 1), (5, 0)]])
FORWARD_HEADS = ([(1, 1)], [(2, 1), (3, 0), (4, 0)], [(1, 2)], [], [(6, 0)], [(3, 2)])
FORWARD_SECOND = [(0, 2), (2, 2)]
FORWARD_PROJECT = []
FORWARD_MIDDLE = [(7, 0), (4, 1), (5, 1)]
FORWARD_NORM = []
FORWARD_OTHER = [(7, 2)]
FORWARD_UNITS_MID = ([(6, 1)], [], [(5, 2), (4, 2), (6, 2)])
FORWARD_UNITS = ([(7, 1)], [], [])
HEAD_ORDER = ((1, 0), (1, 1), (0, 0), (1, 2), (0, 1), (0, 2))
ORDERS = ("x1ye", "yx12", "1xye", "yx1e", "1xye", "x1ye", "yx1e", "yx1e", "yx1e")
UNITS_MID = (
    [],
    [],
    [],
    [],
    [],
    [(1, 0)],
)
UNITS = (
    [(0, 0)],
    [],
    [(2, 0)],
    [(3, 0), (0, 1), (4, 0), (5, 0)],
    [(4, 1)],
    [(5, 1)],
)
AFTER_UNITS = [
    (0, 2), (2, 1),
]
AFTER_SECOND = [
    (3, 1),
]
HEADS = (
    (
        [(5, 2), (0, 3)],
        [(3, 2), (2, 2), (0, 4), (4, 2)],
        [(7, 0), (1, 2), (3, 3)],
        [(1, 3), (5, 4)],
        [(4, 3), (3, 4), (0, 6)],
        [(5, 5), (3, 5)],
    ),
    (
        [(6, 0), (1, 1)],
        [(5, 3)],
        [(6, 1), (0, 5)],
        [(8, 0)],
        [(6, 2), (1, 4), (2, 3), (7, 1)],
        [(0, 7), (6, 3)],
    ),
)
AFTER_HEADS = [
    (1, 5), (7, 2), (8, 1), (5, 6), (4, 4), (6, 4), (3, 6),
]
TAIL = [
    (-1, 0), (2, 4), (8, 2), (7, 3), (4, 5), (-1, 1), (1, 6), (4, 6), (-1, 2), (5, 7), (2, 5), (6, 5), (8, 3),
    (7, 4), (1, 7), (4, 7), (-1, 3), (8, 4), (7, 5), (6, 6), (-1, 4), (2, 6), (8, 5), (7, 6), (2, 7), (-1, 5),
    (8, 6),
]


def block_call(lengths, sets, tok, ct, w, ow, fc, pw, qkv_b, fc_b, ob, pb, gains, biases):
    rows, width = tok.shape
    local, hidden = ow.shape[0], fc.shape[1]
    heads, span = local // HD, 2 * rows
    total = 4 * local
    assert total == width == hidden
    any_spec = pl.BlockSpec(memory_space=pl.ANY)

    def v(*shape, dtype=BF16):
        return pltpu.VMEM(shape, dtype)

    act, wide = v(rows, width), v(rows, width, dtype=F32)
    one, one_acc = v(span, HD), v(span, HD, dtype=F32)
    dma = pltpu.SemaphoreType.DMA
    scratch = [act, act, act, act, act]
    scratch += [v(2, 3 * local, width), v(2, local, width), v(2, width, hidden), v(2, hidden, width), v(2, 16, hidden + 512)]
    scratch += [v(2, 3, heads, HD, span), v(2, heads, 1, span, dtype=F32), v(2, heads, HD, span), v(2, heads, span, 2 * HD), v(2, heads, HD, span)]
    scratch += [act, act, act, wide, act, act, v(width, span), v(4, rows, width, dtype=F32), act, act]
    scratch += [act, one, v(span, 2 * HD), one, v(2, 3, heads, HD, span), one_acc, one_acc, act, v(2 * HD, span), act, act]
    scratch += [v(2, 3, total, width), v(3, total, width), v(3, 2 * total, width), v(2, 8, hidden, dtype=F32), v(5, 32, width, dtype=F32)]
    scratch += [dma((7,)), dma((11, 16)), dma((11, 16)), dma((33,)), dma((33,)), dma((9,))]
    shapes = [(rows, width)] * 2 + [(total, width)] * 2 + [(3 * local, width), (local, width)]
    return pl.pallas_call(
        block_kernel,
        out_shape=[jax.ShapeDtypeStruct(s, BF16) for s in shapes] + [jax.ShapeDtypeStruct((32, width), F32)],
        in_specs=[SMEM] * 2 + [any_spec] * 6 + [VMEM] * 6,
        out_specs=[any_spec] * 6 + [VMEM],
        scratch_shapes=scratch,
        compiler_params=pltpu.CompilerParams(vmem_limit_bytes=63 << 20, collective_id=1, has_side_effects=True),
    )(lengths, sets, tok, ct, w, ow, fc, pw, qkv_b, fc_b, ob, pb, gains, biases)


def finish_kernel(b, g, p, f, q, o, pack, block_out, grad_in, gq, gqb, go, gob, gf, gfb, gp, gpb, gains, biases):
    block_out[...] = b[...]
    grad_in[...] = g[...]
    for src, dst in ((p, gp), (f, gf), (q, gq), (o, go)):
        dst[...] = src[...].astype(F32)

    @pl.when(pl.program_id(0) == 0)
    def _():
        local = gqb.shape[1]
        count = gains.shape[1]
        gqb[0:1, :] = pack[16:17, :local]
        gqb[1:2, :] = pack[16:17, 2 * local : 3 * local]
        for row, dst in ((0, gob), (1, gpb), (17, gfb)):
            dst[...] = pack[row : row + 1, :].reshape(dst.shape)
        for n, at in ((0, 8), (1, 2)):
            gains[n] = pack[at : at + count, :]
            biases[n] = pack[at + count : at + 2 * count, :]


def finish(parts, local, count):
    rows, width = parts[0].shape
    steps = 2

    def spec(array):
        return pl.BlockSpec((array.shape[0] // steps, width), lambda i: (i, 0))

    def whole(*shape):
        return pl.BlockSpec(shape, lambda i: (0,) * len(shape))

    b, g, p, f, q, o, pack = parts
    sets = (2, count, width)
    small = [(2, local), (width,), (p.shape[0],), (width,), sets, sets]
    order = [(b, BF16), (g, BF16), (q, F32), small[0], (o, F32), small[1], (f, F32), small[2], (p, F32)] + small[3:]
    big = [isinstance(v[0], jax.Array) for v in order]
    return pl.pallas_call(
        finish_kernel,
        grid=(steps,),
        in_specs=[spec(v) for v in parts[:6]] + [whole(*pack.shape)],
        out_specs=[spec(v[0]) if k else whole(*v) for v, k in zip(order, big)],
        out_shape=[jax.ShapeDtypeStruct(*((v[0].shape, v[1]) if k else (v, F32))) for v, k in zip(order, big)],
    )(*parts)


def generic(tokens, cotangent, lengths, tie_sets, qkv_weight, qkv_bias, out_weight, out_bias, fc_weight, fc_bias, proj_weight, proj_bias, norm_gain, norm_bias):
    rows, width = tokens.shape
    local = qkv_weight.shape[2]
    heads = local // HD
    hidden = fc_weight.shape[1]
    span = 2 * rows

    def swap_core(v):
        return lax.ppermute(v, "tensor", [(i, i ^ 1) for i in range(4)])

    def swap_chip(v):
        return lax.ppermute(v, "tensor", [(i, i ^ 2) for i in range(4)])

    def after(v, *first):
        return lax.optimization_barrier((v, *first))[0]

    w_own = qkv_weight.transpose(1, 2, 0).reshape(3 * local, width)
    b_own = jnp.concatenate([qkv_bias[:1], jnp.zeros_like(qkv_bias[:1]), qkv_bias[1:]], axis=0)
    bias_pack = jnp.concatenate([b_own.reshape(1, 3 * local), fc_bias.reshape(1, hidden)], axis=1)
    w_oth = swap_chip(w_own)
    bias_oth = swap_chip(bias_pack)
    ow_oth = swap_chip(out_weight)
    fc_oth = swap_chip(fc_weight)
    pw_oth = swap_chip(proj_weight)
    c_oth = swap_core(cotangent)

    def col(pack):
        return pack[:, : 3 * local].astype(F32).reshape(3 * local, 1)

    def fcb(pack):
        return pack[:, 3 * local :].astype(F32)

    act_bytes = rows * width * 4
    first = call(norm_first, [((rows, width), BF16)], 4, smem=1, nbytes=act_bytes)(
        tie_sets, tokens, norm_gain[0], norm_bias[0]
    )[0]
    first_oth = swap_core(first)

    block = min(256, span)
    att_flops = 2 * 2 * rows * width * 4 * local + heads * 4 * span * span * HD * 4
    saved = [((3, heads, HD, span), BF16), ((heads, 1, span), F32), ((heads, HD, span), BF16)]
    k_scr = [pltpu.VMEM((heads, span, HD), BF16)]

    def forward(first_call, w, b, ow, prev=()):
        outs = saved + [((rows, width), F32), ((rows, width), F32 if first_call else BF16)]
        return call(
            lambda *r: attn_forward(first_call, block, *r),
            outs,
            6 + len(prev),
            smem=1,
            scratch=k_scr,
            flops=att_flops,
            nbytes=8 * act_bytes,
        )(lengths, first, first_oth, w, b, ow, *prev)

    qkv_a, lse_a, att_a, br_own, br_oth = forward(True, w_own, col(bias_pack), out_weight)
    w_oth, bias_oth, ow_oth = (after(v, br_own) for v in (w_oth, bias_oth, ow_oth))
    qkv_b, lse_b, att_b, br_own, br_oth = forward(False, w_oth, col(bias_oth), ow_oth, (br_own, br_oth))
    br_in = swap_core(br_oth)
    middle, second = call(norm_second, [((rows, width), F32), ((rows, width), BF16)], 7, smem=1, nbytes=3 * act_bytes)(
        tie_sets, tokens, br_own, br_in, out_bias.astype(F32).reshape(1, width), norm_gain[1], norm_bias[1]
    )
    second_oth = swap_core(second)
    gf_a, gp_a, gfb_a, fe_own, fe_oth, ds_own, ds_oth = mlp(
        True, second, second_oth, cotangent, c_oth, fc_weight, fcb(bias_pack), proj_weight
    )
    fc_oth, pw_oth = (after(v, fe_own) for v in (fc_oth, pw_oth))
    gf_b, gp_b, gfb_b, fe_own, fe_oth, ds_own, ds_oth = mlp(
        False, second, second_oth, cotangent, c_oth, fc_oth, fcb(bias_oth), pw_oth, (fe_own, fe_oth, ds_own, ds_oth)
    )
    ds_in = swap_core(ds_oth)
    fe_in = swap_core(fe_oth)
    block_out, dmid, dlow, small_two = call(
        back_second,
        [((rows, width), BF16), ((rows, width), F32), ((rows, width), BF16), ((8, width), F32)],
        9,
        smem=1,
        nbytes=6 * act_bytes,
    )(tie_sets, middle, fe_own, fe_in, proj_bias.astype(F32).reshape(1, width), ds_own, ds_in, cotangent, norm_gain[1])
    dlow_oth = swap_core(dlow)

    def backward(first_call, qkv, lse, att, w, ow, prev=()):
        outs = [
            ((4 * local, width), BF16),
            ((8, width), F32),
            ((rows, width), F32),
            ((rows, width), F32 if first_call else BF16),
        ]
        n = pltpu.VMEM((heads, span, HD), BF16)
        tr = pltpu.VMEM((heads, HD, span), BF16)
        one = pltpu.VMEM((span, HD), BF16)
        acc = pltpu.VMEM((span, HD), F32)
        return call(
            lambda *r: attn_backward(first_call, block, *r),
            outs,
            10 + len(prev),
            smem=1,
            scratch=[n, tr, one, one, one, pltpu.VMEM((3, heads, HD, span), BF16), acc, acc],
            flops=3 * att_flops,
            nbytes=12 * act_bytes,
        )(lengths, qkv, lse, att, dlow, dlow_oth, first, first_oth, w, ow, *prev)

    gq_b, gqb_b, df_own, df_oth = backward(True, qkv_b, lse_b, att_b, w_oth, ow_oth)
    gq_a, gqb_a, df_own, df_oth = backward(False, qkv_a, lse_a, att_a, w_own, out_weight, (df_own, df_oth))
    df_in = swap_core(df_oth)
    grad_input, small_one = call(back_first, [((rows, width), BF16), ((8, width), F32)], 6, smem=1, nbytes=4 * act_bytes)(
        tie_sets, tokens, df_own, df_in, dmid, norm_gain[0]
    )
    def total(own, other):
        return lax.psum((own.astype(F32) + swap_chip(other).astype(F32)).astype(BF16), "dp")

    g_p, g_f, g_q = total(gp_a, gp_b), total(gf_a, gf_b), total(gq_a, gq_b)
    bias_a = jnp.concatenate([gqb_a[:1], gfb_a], axis=0)
    bias_b = jnp.concatenate([gqb_b[:1], gfb_b], axis=0)
    pack = jnp.concatenate(
        [
            lax.psum(jnp.concatenate([small_two, small_one], axis=0), ("dp", "tensor")),
            lax.psum(bias_a + swap_chip(bias_b), "dp"),
        ],
        axis=0,
    )
    return block_out, grad_input, g_p, g_f, g_q, pack


def body(
    tokens,
    cotangent,
    lengths,
    tie_sets,
    qkv_weight,
    qkv_bias,
    out_weight,
    out_bias,
    fc_weight,
    fc_bias,
    proj_weight,
    proj_bias,
    norm_gain,
    norm_bias,
):
    rows, width = tokens.shape
    groups = lax.axis_size("tensor")
    local = qkv_weight.shape[2]
    heads = local // HD
    hidden = fc_weight.shape[1]
    span = rows * groups // lengths.shape[0]
    assert groups == 4 and span == 2 * rows
    set_count = norm_gain.shape[1]
    dps = lax.axis_size("dp")

    if dps == 8:
        w = qkv_weight.transpose(1, 2, 0).reshape(3 * local, width)
        parts = block_call(
            lengths,
            tie_sets,
            tokens,
            cotangent,
            w,
            out_weight,
            fc_weight,
            proj_weight,
            qkv_bias,
            fc_bias,
            out_bias,
            proj_bias,
            norm_gain,
            norm_bias,
        )
        outs = finish(parts, local, set_count)
        return (*outs[:2], outs[2].reshape(3, local, width).transpose(2, 0, 1), *outs[3:])
    block_out, grad_input, g_p, g_f, g_q, pack = generic(
        tokens,
        cotangent,
        lengths,
        tie_sets,
        qkv_weight,
        qkv_bias,
        out_weight,
        out_bias,
        fc_weight,
        fc_bias,
        proj_weight,
        proj_bias,
        norm_gain,
        norm_bias,
    )
    gains = jnp.stack([pack[8 : 8 + set_count], pack[2 : 2 + set_count]])
    biases = jnp.stack([pack[8 + set_count : 8 + 2 * set_count], pack[2 + set_count : 2 + 2 * set_count]])
    gqb = pack[16, : 3 * local].reshape(3, local)
    return (
        block_out,
        grad_input,
        g_q[: 3 * local].astype(F32).reshape(3, local, width).transpose(2, 0, 1),
        jnp.stack([gqb[0], gqb[2]]),
        g_q[3 * local :].astype(F32),
        pack[0],
        g_f.astype(F32),
        pack[17],
        g_p.astype(F32),
        pack[1],
        gains,
        biases,
    )


def solution(mesh):
    in_specs = (
        P(("dp", "tensor"), None),
        P(("dp", "tensor"), None),
        P("dp"),
        P("dp"),
        P(None, None, "tensor"),
        P(None, "tensor"),
        P("tensor", None),
        P(),
        P(None, "tensor"),
        P("tensor"),
        P("tensor", None),
        P(),
        P(),
        P(),
    )
    out_specs = (
        P(("dp", "tensor"), None),
        P(("dp", "tensor"), None),
        P(None, None, "tensor"),
        P(None, "tensor"),
        P("tensor", None),
        P(),
        P(None, "tensor"),
        P("tensor"),
        P("tensor", None),
        P(),
        P(),
        P(),
    )
    return jax.shard_map(body, mesh=mesh, in_specs=in_specs, out_specs=out_specs, check_vma=False)
```
